256 devices in a mesh: row: 16 (over z_lo, y, core), col: 16 (over z_hi, x).
Axes of the slice: x: 4, y: 4, z: 8 (z_hi: 4, z_lo: 2; z = z_hi * 2 + z_lo), core: 2. Of those that a mesh axis runs over, the one named last changes fastest.
Arguments:
- state: float32 [3, 2048, 4096], P(None, 'row', 'col'), may hold values from -0.675 to 1.5, as said below
- row_count: int32 [16, 16], P('row', 'col'), may hold values from 0 to 64, as said below
- col_count: int32 [16, 16], P('row', 'col'), may hold values from 0 to 64, as said below
- patch_pos: int32 [16, 16, 2], P('row', 'col'), may hold values from 0 to 192, as said below
- patch_ext: int32 [16, 16, 2], P('row', 'col'), may hold values from 16 to 64, as said below
Outputs:
- richardson_error: float32 [1024, 2048], P('row', 'col')
- moved_state: float32 [3, 2048, 4096], P(None, 'row', 'col')
- refined_patch: float32 [3, 2048, 2048], P(None, 'row', 'col')
The draws below stay inside these ranges and needn't reach their ends.
Inputs may be any that keep to these rules, and one draw needn't show every extreme that they name: `state`: depth lies in [0.5, 1.5]; the momenta are depth times a velocity of magnitude at most 0.45. `row_count`: some tile takes over exactly 64 rows and some none. `col_count`: some tile takes over exactly 64 columns and some none. `patch_pos`: component 0 is at most 64 and component 1 at most 192; both ends are reached. `patch_ext`: some tile is flagged over its whole patch.
All inputs are finite; a program needn't handle non-finite values.
Results may differ from the reference program's by a relative error of at most 0.0003.
Values sent between devices are 32-bit elements; how exact they have to be, the bound alone decides.
A program may use at most 128 MiB of HBM per device.

```python
import jax
import jax.numpy as jnp
from jax import lax

TILE_R = 128
TILE_C = 256
SLAB = 64
PATCH = 64
GR = 16
GC = 16
NX = 2048
NY = 4096


def draw_state(key, part):
    keys = jax.random.split(jax.random.fold_in(key, 7), 3)
    depth_draw = jax.random.uniform(keys[0], (NX, NY), jnp.float32)
    first_vel = jax.random.uniform(keys[1], (NX, NY), jnp.float32, -1.0, 1.0)
    second_vel = jax.random.uniform(keys[2], (NX, NY), jnp.float32, -1.0, 1.0)
    depth = 0.5 + depth_draw
    first_vel = 0.45 * first_vel
    second_vel = 0.45 * second_vel
    return jnp.stack([depth, depth * first_vel, depth * second_vel]).astype(jnp.float32)


def draw_counts(key, salt):
    counts = jax.random.randint(jax.random.fold_in(key, salt), (GR, GC), 0, SLAB + 1)
    return counts.at[0, 0].set(SLAB).at[GR - 1, GC - 1].set(0).astype(jnp.int32)


def draw_row_count(key, part):
    return draw_counts(key, 11)


def draw_col_count(key, part):
    return draw_counts(key, 12)


def draw_patch_pos(key, part):
    first_key, second_key = jax.random.split(jax.random.fold_in(key, 13))
    limit = jnp.array([TILE_R - PATCH, TILE_C - PATCH], jnp.int32)
    base = jax.random.randint(first_key, (GR, GC, 2), 0, limit + 1)
    pick = jax.random.randint(second_key, (GR, GC, 2), 0, 4)
    placed = jnp.where(pick == 0, 0, jnp.where(pick == 1, limit, base))
    return placed.at[0, 0].set(limit).at[GR - 1, GC - 1].set(0).astype(jnp.int32)


def draw_patch_ext(key, part):
    extent = jax.random.randint(jax.random.fold_in(key, 14), (GR, GC, 2), PATCH // 4, PATCH + 1)
    return extent.at[0, 0].set(PATCH).at[GR - 1, GC - 1].set(PATCH // 4).astype(jnp.int32)


def setup_inputs(seed: int = 0) -> dict:
    key_of = jax.random.split(jax.random.key(seed), 6)
    state = draw_state(jax.random.fold_in(key_of[5], 71), 0)
    row_count = draw_row_count(jax.random.fold_in(key_of[5], 71), 0)
    col_count = draw_col_count(jax.random.fold_in(key_of[5], 71), 0)
    patch_pos = draw_patch_pos(jax.random.fold_in(key_of[5], 71), 0)
    patch_ext = draw_patch_ext(jax.random.fold_in(key_of[5], 71), 0)
    return dict(state=state, row_count=row_count, col_count=col_count, patch_pos=patch_pos, patch_ext=patch_ext)


GRAV = 1.0
RATIO = 0.1
ERR_SCALE = 10.0

def face_flux(left_vals, right_vals, normal):
    tangent = 3 - normal

    def physical(fields):
        depth = fields[0]
        velocity = fields[normal] / depth
        flux = [None, None, None]
        flux[0] = fields[normal]
        flux[normal] = fields[normal] * velocity + 0.5 * GRAV * depth * depth
        flux[tangent] = fields[tangent] * velocity
        return (flux, jnp.abs(velocity) + jnp.sqrt(GRAV * depth))
    flux_left, speed_left = physical(left_vals)
    flux_right, speed_right = physical(right_vals)
    speed = jnp.maximum(speed_left, speed_right)
    return [0.5 * (flux_left[comp] + flux_right[comp]) - 0.5 * speed * (right_vals[comp] - left_vals[comp]) for comp in range(3)]

def rusanov_step(cells):
    fields = [cells[comp] for comp in range(3)]
    flux_row = face_flux([f[:-1, 1:-1] for f in fields], [f[1:, 1:-1] for f in fields], 1)
    flux_col = face_flux([f[1:-1, :-1] for f in fields], [f[1:-1, 1:] for f in fields], 2)
    result = [fields[comp][1:-1, 1:-1] - RATIO * (flux_row[comp][1:] - flux_row[comp][:-1]) - RATIO * (flux_col[comp][:, 1:] - flux_col[comp][:, :-1]) for comp in range(3)]
    return jnp.stack(result)

def coarsen(cells):
    shaped = cells.reshape(cells.shape[0], cells.shape[1] // 2, 2, cells.shape[2] // 2, 2)
    return 0.25 * (shaped[:, :, 0, :, 0] + shaped[:, :, 1, :, 0] + shaped[:, :, 0, :, 1] + shaped[:, :, 1, :, 1])

def richardson(fine_two, coarse_one):
    return ERR_SCALE * lax.optimization_barrier(jnp.sum(jnp.abs(coarsen(fine_two) - coarse_one), axis=0))

def minmod(lower_diff, upper_diff):
    chosen = jnp.where(jnp.abs(lower_diff) < jnp.abs(upper_diff), lower_diff, upper_diff)
    return jnp.where(lower_diff * upper_diff > 0, chosen, 0.0)

def muscl_step(cells):
    fields = [cells[comp] for comp in range(3)]
    inner_rows = cells.shape[1] - 4
    inner_cols = cells.shape[2] - 4
    row_band = [f[:, 2:-2] for f in fields]
    deltas = [b[1:] - b[:-1] for b in row_band]
    slopes = [minmod(d[:-1], d[1:]) for d in deltas]
    left_vals = [row_band[c][1:inner_rows + 2] + 0.5 * slopes[c][:inner_rows + 1] for c in range(3)]
    right_vals = [row_band[c][2:inner_rows + 3] - 0.5 * slopes[c][1:inner_rows + 2] for c in range(3)]
    flux_row = face_flux(left_vals, right_vals, 1)
    col_band = [f[2:-2, :] for f in fields]
    deltas = [b[:, 1:] - b[:, :-1] for b in col_band]
    slopes = [minmod(d[:, :-1], d[:, 1:]) for d in deltas]
    left_vals = [col_band[c][:, 1:inner_cols + 2] + 0.5 * slopes[c][:, :inner_cols + 1] for c in range(3)]
    right_vals = [col_band[c][:, 2:inner_cols + 3] - 0.5 * slopes[c][:, 1:inner_cols + 2] for c in range(3)]
    flux_col = face_flux(left_vals, right_vals, 2)
    result = [fields[comp][2:-2, 2:-2] - RATIO * (flux_row[comp][1:] - flux_row[comp][:-1]) - RATIO * (flux_col[comp][:, 1:] - flux_col[comp][:, :-1]) for comp in range(3)]
    return jnp.stack(result)

def place_top(own_cells, slab_in, count_in):
    buffer = jnp.concatenate([slab_in, jnp.zeros_like(slab_in)], axis=1)
    aligned = lax.dynamic_slice_in_dim(buffer, (SLAB - count_in).astype(jnp.int32), SLAB, 1)
    row_ids = lax.broadcasted_iota(jnp.int32, (1, SLAB, 1), 1)
    return jnp.where(row_ids < count_in, aligned, own_cells)

def place_rows(own_cells, slab_in, count_in):
    top_rows = place_top(own_cells[:, :SLAB, :], slab_in, count_in)
    return jnp.concatenate([top_rows, own_cells[:, SLAB:, :]], axis=1)

def place_cols(own_cells, slab_in, count_in):
    buffer = jnp.concatenate([slab_in, jnp.zeros_like(slab_in)], axis=2)
    aligned = lax.dynamic_slice_in_dim(buffer, (SLAB - count_in).astype(jnp.int32), SLAB, 2)
    col_ids = lax.broadcasted_iota(jnp.int32, (1, 1, SLAB), 2)
    left_part = jnp.where(col_ids < count_in, aligned, own_cells[:, :, :SLAB])
    return jnp.concatenate([left_part, own_cells[:, :, SLAB:]], axis=2)

def refine_patch(padded, row_start, col_start, extent):
    zero_index = jnp.zeros((), jnp.int32)
    region = lax.dynamic_slice(padded, (zero_index, row_start.astype(jnp.int32), col_start.astype(jnp.int32)), (3, PATCH + 4, PATCH + 4))
    refined_cells = jnp.broadcast_to(region[:, :, None, :, None], (3, PATCH + 4, 2, PATCH + 4, 2)).reshape(3, 2 * PATCH + 8, 2 * PATCH + 8)
    halfway = muscl_step(refined_cells)
    finished = muscl_step(halfway)
    row_ids = lax.broadcasted_iota(jnp.int32, (1, 2 * PATCH, 1), 1)
    col_ids = lax.broadcasted_iota(jnp.int32, (1, 1, 2 * PATCH), 2)
    inside = (row_ids < 2 * extent[0]) & (col_ids < 2 * extent[1])
    return jnp.where(inside, finished, 0.0)

def reference(state, row_count, col_count, patch_pos, patch_ext):
    wrapped = jnp.pad(state, ((0, 0), (2, 2), (2, 2)), mode='wrap')

    def error_rows(tile_index):
        row_block = lax.dynamic_slice_in_dim(wrapped, (tile_index * TILE_R).astype(jnp.int32), TILE_R + 4, 1)
        fine_two = rusanov_step(rusanov_step(row_block))
        coarse_one = rusanov_step(coarsen(row_block))
        return richardson(fine_two, coarse_one)
    error_field = lax.map(error_rows, jnp.arange(GR, dtype=jnp.int32)).reshape(NX // 2, NY // 2)
    tile_stack = state.reshape(3, GR, TILE_R, GC, TILE_C).transpose(1, 3, 0, 2, 4)
    upper_slab = jnp.roll(tile_stack, 1, axis=0)[:, :, :, TILE_R - SLAB:, :]
    row_moved = jax.vmap(jax.vmap(place_rows))(tile_stack, upper_slab, row_count)
    left_slab = jnp.roll(row_moved, 1, axis=1)[:, :, :, :, TILE_C - SLAB:]
    moved_tiles = jax.vmap(jax.vmap(place_cols))(row_moved, left_slab, col_count)
    moved_state = moved_tiles.transpose(2, 0, 3, 1, 4).reshape(3, NX, NY)
    wrapped_moved = jnp.pad(moved_state, ((0, 0), (2, 2), (2, 2)), mode='wrap')
    flat_pos = patch_pos.reshape(GR * GC, 2)
    flat_ext = patch_ext.reshape(GR * GC, 2)

    def one_patch(inputs):
        tile_index, patch_start, extent = inputs
        row_start = tile_index // GC * TILE_R + patch_start[0]
        col_start = tile_index % GC * TILE_C + patch_start[1]
        return refine_patch(wrapped_moved, row_start, col_start, extent)
    patches = lax.map(one_patch, (jnp.arange(GR * GC, dtype=jnp.int32), flat_pos, flat_ext))
    refined = patches.reshape(GR, GC, 3, 2 * PATCH, 2 * PATCH).transpose(2, 0, 3, 1, 4).reshape(3, GR * 2 * PATCH, GC * 2 * PATCH)
    return (error_field, moved_state, refined)
```

```python
import functools

import jax
import jax.numpy as jnp
from jax import lax
from jax.experimental import pallas as pl
from jax.experimental.pallas import tpu as pltpu
from jax.sharding import PartitionSpec as P

MESH = pl.DeviceIdType.MESH
F32 = jnp.float32
SLAB = 64
HALF = 0.05
BASE = 64
ROWS = 208
N_MSG = 18


def chunk(start, size=8):
    return pl.ds(start, size)


def lanes(shape=(8, 128)):
    return lax.broadcasted_iota(jnp.int32, shape, 1)


def roll(x, by):
    return pltpu.roll(x, by % x.shape[1] if isinstance(by, int) else by, 1)


def speeds(h, m1, m2):
    return m1 / h, m2 / h, jnp.sqrt(h)


def side(u, vel, normal):
    h, m1, m2 = u
    v1, v2, wave = vel
    pressure = 0.5 * h * h
    if normal == 1:
        return u, (m1, m1 * v1 + pressure, m2 * v1), jnp.abs(v1) + wave
    return u, (m2, m1 * v2, m2 * v2 + pressure), jnp.abs(v2) + wave


def face(lower, upper):
    speed = jnp.maximum(lower[2], upper[2])
    return [
        (lower[1][c] + upper[1][c]) - speed * (upper[0][c] - lower[0][c])
        for c in range(3)
    ]


def minmod(a, b):
    chosen = jnp.where(jnp.abs(a) < jnp.abs(b), a, b)
    return jnp.where(a * b > 0, chosen, 0.0)


def from_lower(xs, lane):
    rolled = [roll(x, 1) for x in xs]
    return [jnp.where(lane == 0, rolled[g - 1], rolled[g]) for g in range(len(xs))]


def from_upper(xs, lane):
    rolled = [roll(x, 127) for x in xs]
    return [
        jnp.where(lane == 127, rolled[(g + 1) % len(xs)], rolled[g])
        for g in range(len(xs))
    ]


def speed_pass(src, vel, groups, first, last):
    def body(i, carry):
        at = chunk(pl.multiple_of(i * 8, 8))
        for g in range(groups):
            for k, value in enumerate(speeds(*(src[c, g, at, :] for c in range(3)))):
                vel[k, g, at, :] = value
        return carry

    lax.fori_loop(first, last, body, 0)


def step_pass(src, vel, dst, groups, keep, first, last):
    lane = lanes()

    def body(i, carry):
        row = pl.multiple_of(i * 8, 8)

        def load(shift, g, normal):
            at = chunk(row + shift)
            return side(
                [src[c, g, at, :] for c in range(3)],
                [vel[c, g, at, :] for c in range(3)],
                normal,
            )

        along = [load(0, g, 2) for g in range(groups)]
        flat = [[*s[0], s[1][0], s[1][1], s[1][2], s[2]] for s in along]
        shifted = [
            from_lower([flat[g][k] for g in range(groups)], lane)
            for k in (0, 1, 2, 4, 5, 6)
        ]
        low = []
        for g in range(groups):
            u = [shifted[k][g] for k in range(3)]
            lower = (u, (u[2], shifted[3][g], shifted[4][g]), shifted[5][g])
            low.append(face(lower, along[g]))
        high = [from_upper([low[g][c] for g in range(groups)], lane) for c in range(3)]
        for g in range(keep):
            here = load(0, g, 1)
            down = face(load(-1, g, 1), here)
            up = face(here, load(1, g, 1))
            for c in range(3):
                change = (up[c] - down[c]) + (high[c][g] - low[g][c])
                dst[c, g, chunk(row), :] = here[0][c] - HALF * change
        return carry

    lax.fori_loop(first, last, body, 0)


def coarse_rows(src, row, groups, c):
    lane = lanes()
    even = lax.rem(2 * lane, 128)
    out = []
    for g in range(groups):
        pair = src[c, g, pl.ds(row, 8, stride=2), :] + src[c, g, pl.ds(row + 1, 8, stride=2), :]
        pair = pair + roll(pair, 127)
        out.append(jnp.take_along_axis(pair, even, axis=1, mode="promise_in_bounds"))
    return [0.25 * jnp.where(lane < 64, out[0], out[1])] + [0.25 * x for x in out[2:]]


def exchange_kernel(
    n_row, n_col, state, row_count, col_count,
    st, lslab, ulslab, dlc, cnt, err,
    rpack, lpack, rslab, drslab, cnt_s, lr, rl, url, ulc, drc,
    vel, fine1, fine2, cgrid, cvel, cone,
    local_sem, send_sem, recv_sem,
):
    me_r, me_c = lax.axis_index("row"), lax.axis_index("col")

    def device(dr, dc):
        return (lax.rem(me_r + (dr + n_row), n_row), lax.rem(me_c + (dc + n_col), n_col))

    loads = [
        pltpu.make_async_copy(
            state.at[:, :, pl.ds(128 * g, 128)], st.at[:, g, pl.ds(BASE, 128), :], local_sem.at[g]
        )
        for g in range(2)
    ]
    loads[1].start()
    loads[0].start()
    barrier = pltpu.get_barrier_semaphore()
    around = [(a, b) for a in (-1, 0, 1) for b in (-1, 0, 1) if (a, b) != (0, 0)]
    for a, b in around:
        pl.semaphore_signal(barrier, inc=1, device_id=device(a, b), device_id_type=MESH)

    lane = lanes()
    lane1 = lanes((1, 128))
    cnt_s[...] = jnp.where(lane1 == 0, row_count[0, 0], col_count[0, 0])
    loads[1].wait()
    loads[0].wait()
    for c in range(3):
        right = left = None
        for k in range(16):
            at = chunk(BASE + 8 * k)
            mine = (lane >= 8 * k) & (lane < 8 * k + 8)
            r, l = roll(st[c, 1, at, :], 8 * k - 120), roll(st[c, 0, at, :], 8 * k)
            right = r if right is None else jnp.where(mine, r, right)
            left = l if left is None else jnp.where(mine, l, left)
        rpack[c] = right
        lpack[c] = left
        for k in range(8):
            near, far = st[c, 1, chunk(BASE + 8 * k), :], st[c, 1, chunk(BASE + 64 + 8 * k), :]
            rslab[c, chunk(8 * k), :] = jnp.where(lane < 64, roll(far, 64), near)
        for k in range(4):
            near, far = st[c, 1, chunk(BASE + 64 + 8 * k), :], st[c, 1, chunk(BASE + 96 + 8 * k), :]
            drslab[c, chunk(8 * k), :] = jnp.where(lane < 64, roll(far, 64), near)

    pl.semaphore_wait(barrier, 8)
    both = pl.ds(0, 2)
    messages = [
        ((0, 1), rpack, lr),
        ((0, -1), lpack, rl),
        ((1, 0), st.at[:, both, pl.ds(BASE + 112, 16), :], st.at[:, both, pl.ds(BASE - 16, 16), :]),
        ((-1, 0), st.at[:, both, pl.ds(BASE, 8), :], st.at[:, both, pl.ds(BASE + 128, 8), :]),
        ((1, 1), st.at[:, 1, pl.ds(BASE + 120, 8), :], ulc),
        ((1, -1), lpack, url),
        ((-1, 1), st.at[:, 1, pl.ds(BASE, 8), :], dlc),
        ((-1, -1), st.at[:, 0, pl.ds(BASE, 8), :], drc),
        ((0, 1), rslab, lslab),
        ((1, 1), drslab, ulslab),
        ((1, 0), st.at[:, both, pl.ds(BASE + 64, 48), :], st.at[:, both, pl.ds(0, 48), :]),
        ((0, 1), cnt_s, cnt.at[0]),
        ((0, -1), cnt_s, cnt.at[1]),
        ((1, 0), cnt_s, cnt.at[2]),
        ((-1, 0), cnt_s, cnt.at[3]),
        ((1, -1), cnt_s, cnt.at[4]),
        ((-1, 1), cnt_s, cnt.at[5]),
        ((-1, -1), cnt_s, cnt.at[6]),
    ]
    copies = [
        pltpu.make_async_remote_copy(
            src_ref=src, dst_ref=dst, send_sem=send_sem.at[i], recv_sem=recv_sem.at[i],
            device_id=device(*to), device_id_type=MESH,
        )
        for i, (to, src, dst) in enumerate(messages)
    ]
    for copy in copies:
        copy.start()
    for copy in copies[:8]:
        copy.wait_recv()

    for c in range(3):
        for k in range(-8, 17):
            if k < 0:
                right = roll(url[c], -8 * (k + 16))
            elif k < 16:
                right = roll(rl[c], -8 * k)
            else:
                right = drc[c]
            if k < -1:
                value = right
            else:
                left = ulc[c] if k < 0 else dlc[c] if k == 16 else roll(lr[c], 120 - 8 * k)
                value = jnp.where(lane < 64, right, left)
            st[c, 2, chunk(BASE + 8 * k), :] = value

    speed_pass(st, vel, 3, 7, 25)
    step_pass(st, vel, fine1, 3, 3, 7, 25)
    speed_pass(fine1, vel, 3, 7, 25)
    step_pass(fine1, vel, fine2, 3, 2, 8, 24)

    def coarsen(i, carry):
        for c in range(3):
            parts = coarse_rows(st, pl.multiple_of(BASE - 16 + 16 * i, 16), 3, c)
            for g in range(2):
                cgrid[c, g, chunk(pl.multiple_of(8 * i, 8)), :] = parts[g]
        return carry

    lax.fori_loop(0, 10, coarsen, 0)
    speed_pass(cgrid, cvel, 2, 0, 10)
    step_pass(cgrid, cvel, cone, 2, 1, 1, 9)

    def estimate(i, carry):
        total = None
        for c in range(3):
            fine = coarse_rows(fine2, pl.multiple_of(BASE + 16 * i, 16), 2, c)[0]
            gap = jnp.abs(fine - cone[c, 0, chunk(pl.multiple_of(8 * i + 8, 8)), :])
            total = gap if total is None else total + gap
        err[chunk(pl.multiple_of(8 * i, 8)), :] = 10.0 * total
        return carry

    lax.fori_loop(0, 8, estimate, 0)

    for copy in copies[8:]:
        copy.wait_recv()
    for copy in copies:
        copy.wait_send()


def patch_kernel(
    row_count, col_count, pos, ext, cnt, st, lslab, ulslab, dlc, err_in,
    err, moved, refined,
    lext, tiles, win, wvel, ctr, dcol, plus, base, mid, low,
):
    lane = lanes()
    row8 = lax.broadcasted_iota(jnp.int32, (8, 128), 0)
    err[...] = err_in[...]
    rc, cc = row_count[0, 0], col_count[0, 0]
    rc_of = lambda i: cnt[i, 0, 0]
    cc_of = lambda i: cnt[i, 0, 1]
    rows_in = (rc_of(0), rc, rc, rc_of(1))
    rows_below = (rc_of(5), rc_of(3), rc_of(3), rc_of(6))
    cols_in = {"up": (cc_of(2), cc_of(4)), "own": (cc, cc_of(1)), "down": (cc_of(3), cc_of(6))}

    for c in range(3):
        for k in range(8):
            x = lslab[c, chunk(8 * k), :]
            lext[c, chunk(BASE + 8 * k), :] = x
            lext[c, chunk(BASE + 64 + 8 * k), :] = roll(x, 64)
        for k in range(4):
            x = ulslab[c, chunk(8 * k), :]
            lext[c, chunk(8 * k), :] = x
            lext[c, chunk(32 + 8 * k), :] = roll(x, 64)
        lext[c, chunk(BASE + 128), :] = dlc[c]

    for c in range(3):
        columns = [lext.at[c], st.at[c, 0], st.at[c, 1], st.at[c, 2]]
        for k in range(-1, 17):
            at = chunk(BASE + 8 * k)
            values = [ref[at, :] for ref in columns]
            if 0 <= k < 8 or k == 16:
                counts = rows_below if k == 16 else rows_in
                first = 0 if k == 16 else 8 * k
                for g in range(4):
                    above = columns[g][chunk(BASE + 8 * k - counts[g]), :]
                    values[g] = jnp.where(row8 + first < counts[g], above, values[g])
            c0, c_right = cols_in["up" if k < 0 else "down" if k == 16 else "own"]
            m0 = jnp.where(lane < c0, roll(values[0], c0), values[1])
            m_right = jnp.where(lane < c_right, roll(values[2], c_right), values[3])
            put = chunk(8 * k + 8)
            for g, value in enumerate((values[0], m0, values[2], m_right)):
                tiles[g, c, put, :] = value
            if 0 <= k < 16:
                moved[c, chunk(8 * k), pl.ds(0, 128)] = m0
                moved[c, chunk(8 * k), pl.ds(128, 128)] = values[2]

    p0, p1 = pos[0, 0, 0], pos[0, 0, 1]
    group = lax.shift_right_logical(p1 + 126, 7)
    offset = lax.bitwise_and(p1 + 126, 127)
    back = lax.bitwise_and(128 - offset, 127)
    for k in range(10):
        u = []
        for c in range(3):
            at = chunk(p0 + 8 * k)
            a, b = tiles[group, c, at, :], tiles[group + 1, c, at, :]
            u.append(jnp.where(lane < 128 - offset, roll(a, back), roll(b, back)))
            win[c, chunk(8 * k + 8), :] = u[c]
        for c, value in enumerate(speeds(*u)):
            wvel[c, chunk(8 * k + 8), :] = value

    front = lane < 64
    for k in range(10):
        row = 8 * k + 8

        def load(shift, normal):
            at = chunk(row + shift)
            return side([win[c, at, :] for c in range(3)], [wvel[c, at, :] for c in range(3)], normal)

        here = load(0, 1)
        down, up = face(load(-1, 1), here), face(here, load(1, 1))
        across = load(0, 2)
        lower = (
            [roll(x, 1) for x in across[0]],
            [roll(x, 1) for x in across[1]],
            roll(across[2], 1),
        )
        left = face(lower, across)
        right = [roll(x, 127) for x in left]
        for a in range(2):
            far = []
            for c in range(3):
                twice = 2.0 * here[1][c]
                tall = up[c] - twice if a else twice - down[c]
                mid_c = here[0][c] - HALF * tall
                twice = 2.0 * across[1][c]
                e = mid_c - HALF * (twice - left[c])
                o = mid_c - HALF * (right[c] - twice)
                center = jnp.where(front, roll(e, -2), roll(o, 62))
                ctr[a, c, chunk(row), :] = center
                if 1 <= k < 9:
                    e62, o2 = roll(e, 62), roll(o, -1)
                    l1 = jnp.where(front, o2, e62)
                    r1 = jnp.where(front, roll(o, -2), roll(e, 61))
                    l2 = jnp.where(front, roll(e, -1), roll(o, 63))
                    r2 = jnp.where(front, roll(e, -3), roll(o, 61))
                    d1, d2, d3, d4 = l1 - l2, center - l1, r1 - center, r2 - r1
                    s_l, s_c, s_r = minmod(d1, d2), minmod(d2, d3), minmod(d3, d4)
                    far.append(
                        (l1 + 0.5 * s_l, center - 0.5 * s_c, center + 0.5 * s_c, r1 - 0.5 * s_r)
                    )
            if 1 <= k < 9:
                sides = [[far[c][i] for c in range(3)] for i in range(4)]
                sides = [side(s, speeds(*s), 2) for s in sides]
                f_low, f_high = face(sides[0], sides[1]), face(sides[2], sides[3])
                for c in range(3):
                    dcol[a, c, chunk(row), :] = f_high[c] - f_low[c]

    for k in range(10):
        row = 8 * k + 8
        at = chunk(row)
        l_side, r_side = [], []
        for c in range(3):
            c0, c1 = ctr[0, c, at, :], ctr[1, c, at, :]
            inner = c1 - c0
            before = c0 - ctr[1, c, chunk(row - 1), :]
            after = ctr[0, c, chunk(row + 1), :] - c1
            s0, s1 = minmod(before, inner), minmod(inner, after)
            base[c, at, :] = c0 - 0.5 * s0
            plus[c, at, :] = c1 + 0.5 * s1
            l_side.append(c0 + 0.5 * s0)
            r_side.append(c1 - 0.5 * s1)
        if 1 <= k < 9:
            f = face(side(l_side, speeds(*l_side), 1), side(r_side, speeds(*r_side), 1))
            for c in range(3):
                mid[c, at, :] = f[c]
    for k in range(1, 10):
        row = 8 * k + 8
        l_side = [plus[c, chunk(row - 1), :] for c in range(3)]
        r_side = [base[c, chunk(row), :] for c in range(3)]
        f = face(side(l_side, speeds(*l_side), 1), side(r_side, speeds(*r_side), 1))
        for c in range(3):
            low[c, chunk(row), :] = f[c]
    spread = lax.shift_right_logical(lane, 1) + 64 * lax.bitwise_and(lane, 1)
    inside_col = lax.bitwise_and(lane, 63) < ext[0, 0, 1]
    for k in range(1, 9):
        row = 8 * k + 8
        inside = inside_col & (row8 + 8 * (k - 1) < ext[0, 0, 0])
        for c in range(3):
            at = chunk(row)
            f_mid, f_low, f_next = mid[c, at, :], low[c, at, :], low[c, chunk(row + 1), :]
            for a, tall in enumerate((f_mid - f_low, f_next - f_mid)):
                done = ctr[a, c, at, :] - HALF * (tall + dcol[a, c, at, :])
                done = jnp.where(inside, done, 0.0)
                refined[c, pl.ds(16 * (k - 1) + a, 8, stride=2), :] = jnp.take_along_axis(
                    done, spread, axis=1, mode="promise_in_bounds"
                )


def solution(mesh):
    n_row, n_col = mesh.shape["row"], mesh.shape["col"]
    vmem = pl.BlockSpec(memory_space=pltpu.VMEM)
    smem = pl.BlockSpec(memory_space=pltpu.SMEM)
    buf = lambda *shape: pltpu.VMEM(shape, F32)

    def per_device(state, row_count, col_count, patch_pos, patch_ext):
        st, lslab, ulslab, dlc, cnt, err = pl.pallas_call(
            functools.partial(exchange_kernel, n_row, n_col),
            out_shape=(
                buf(3, 3, ROWS, 128),
                buf(3, 64, 128),
                buf(3, 32, 128),
                buf(3, 8, 128),
                jax.ShapeDtypeStruct((7, 1, 128), jnp.int32),
                buf(64, 128),
            ),
            in_specs=[pl.BlockSpec(memory_space=pl.ANY), smem, smem],
            out_specs=(vmem,) * 6,
            scratch_shapes=[
                buf(3, 8, 128), buf(3, 8, 128), buf(3, 64, 128), buf(3, 32, 128),
                pltpu.VMEM((1, 128), jnp.int32),
                *([buf(3, 8, 128)] * 5),
                buf(3, 3, ROWS, 128), buf(3, 3, ROWS, 128), buf(3, 2, ROWS, 128),
                buf(3, 2, 88, 128), buf(3, 2, 88, 128), buf(3, 1, 88, 128),
                pltpu.SemaphoreType.DMA((2,)),
                pltpu.SemaphoreType.DMA((N_MSG,)),
                pltpu.SemaphoreType.DMA((N_MSG,)),
            ],
            compiler_params=pltpu.CompilerParams(
                collective_id=0, has_side_effects=True, vmem_limit_bytes=24 << 20
            ),
        )(state, row_count, col_count)
        return pl.pallas_call(
            patch_kernel,
            out_shape=(
                jax.ShapeDtypeStruct((64, 128), F32),
                jax.ShapeDtypeStruct((3, 128, 256), F32),
                jax.ShapeDtypeStruct((3, 128, 128), F32),
            ),
            in_specs=[smem] * 5 + [vmem] * 5,
            out_specs=(vmem,) * 3,
            scratch_shapes=[
                buf(3, ROWS, 128), buf(4, 3, 144, 128), buf(3, 96, 128), buf(3, 96, 128),
                buf(2, 3, 96, 128), buf(2, 3, 96, 128),
                buf(3, 96, 128), buf(3, 96, 128), buf(3, 96, 128), buf(3, 96, 128),
            ],
            compiler_params=pltpu.CompilerParams(vmem_limit_bytes=24 << 20),
        )(row_count, col_count, patch_pos, patch_ext, cnt, st, lslab, ulslab, dlc, err)

    return jax.shard_map(
        per_device,
        mesh=mesh,
        in_specs=(
            P(None, "row", "col"),
            P("row", "col"),
            P("row", "col"),
            P("row", "col", None),
            P("row", "col", None),
        ),
        out_specs=(P("row", "col"), P(None, "row", "col"), P(None, "row", "col")),
        check_vma=False,
    )
```

```python
import functools

import jax
import jax.numpy as jnp
from jax import lax
from jax.experimental import pallas as pl
from jax.experimental.pallas import tpu as pltpu
from jax.sharding import PartitionSpec as P

MESH = pl.DeviceIdType.MESH
F32 = jnp.float32
SLAB = 64
HALF = 0.05
BASE = 64
ROWS = 208
N_MSG = 18


def chunk(start, size=8):
    return pl.ds(start, size)


def lanes(shape=(8, 128)):
    return lax.broadcasted_iota(jnp.int32, shape, 1)


def roll(x, by):
    return pltpu.roll(x, by % x.shape[1] if isinstance(by, int) else by, 1)


def speeds(h, m1, m2):
    return m1 / h, m2 / h, jnp.sqrt(h)


def side(u, vel, normal):
    h, m1, m2 = u
    v1, v2, wave = vel
    pressure = 0.5 * h * h
    if normal == 1:
        return u, (m1, m1 * v1 + pressure, m2 * v1), jnp.abs(v1) + wave
    return u, (m2, m1 * v2, m2 * v2 + pressure), jnp.abs(v2) + wave


def face(lower, upper):
    speed = jnp.maximum(lower[2], upper[2])
    return [
        (lower[1][c] + upper[1][c]) - speed * (upper[0][c] - lower[0][c])
        for c in range(3)
    ]


def minmod(a, b):
    chosen = jnp.where(jnp.abs(a) < jnp.abs(b), a, b)
    return jnp.where(a * b > 0, chosen, 0.0)


def from_lower(xs, lane):
    rolled = [roll(x, 1) for x in xs]
    return [jnp.where(lane == 0, rolled[g - 1], rolled[g]) for g in range(len(xs))]


def from_upper(xs, lane):
    rolled = [roll(x, 127) for x in xs]
    return [
        jnp.where(lane == 127, rolled[(g + 1) % len(xs)], rolled[g])
        for g in range(len(xs))
    ]


def speed_pass(src, vel, groups, first, last):
    def body(i, carry):
        at = chunk(pl.multiple_of(i * 8, 8))
        for g in range(groups):
            for k, value in enumerate(speeds(*(src[c, g, at, :] for c in range(3)))):
                vel[k, g, at, :] = value
        return carry

    lax.fori_loop(first, last, body, 0, unroll=True)


def step_pass(src, vel, dst, groups, keep, first, last):
    lane = lanes()

    def body(i, carry):
        row = pl.multiple_of(i * 8, 8)

        def load(shift, g, normal):
            at = chunk(row + shift)
            return side(
                [src[c, g, at, :] for c in range(3)],
                [vel[c, g, at, :] for c in range(3)],
                normal,
            )

        along = [load(0, g, 2) for g in range(groups)]
        flat = [[*s[0], s[1][0], s[1][1], s[1][2], s[2]] for s in along]
        shifted = [
            from_lower([flat[g][k] for g in range(groups)], lane)
            for k in (0, 1, 2, 4, 5, 6)
        ]
        low = []
        for g in range(groups):
            u = [shifted[k][g] for k in range(3)]
            lower = (u, (u[2], shifted[3][g], shifted[4][g]), shifted[5][g])
            low.append(face(lower, along[g]))
        high = [from_upper([low[g][c] for g in range(groups)], lane) for c in range(3)]
        for g in range(keep):
            here = load(0, g, 1)
            down = face(load(-1, g, 1), here)
            up = face(here, load(1, g, 1))
            for c in range(3):
                change = (up[c] - down[c]) + (high[c][g] - low[g][c])
                dst[c, g, chunk(row), :] = here[0][c] - HALF * change
        return carry

    lax.fori_loop(first, last, body, 0, unroll=True)


def coarse_rows(src, row, groups, c):
    lane = lanes()
    even = lax.rem(2 * lane, 128)
    out = []
    for g in range(groups):
        pair = src[c, g, pl.ds(row, 8, stride=2), :] + src[c, g, pl.ds(row + 1, 8, stride=2), :]
        pair = pair + roll(pair, 127)
        out.append(jnp.take_along_axis(pair, even, axis=1, mode="promise_in_bounds"))
    return [0.25 * jnp.where(lane < 64, out[0], out[1])] + [0.25 * x for x in out[2:]]


def exchange_kernel(
    n_row, n_col, state, row_count, col_count, pos_hbm, ext_hbm,
    st, lslab, ulslab, dlc, counts, pos, ext, err,
    rpack, lpack, rslab, drslab, cnt_s, lr, rl, url, ulc, drc,
    vel, fine1, fine2, cgrid, cvel, cone,
    cnt, local_sem, send_sem, recv_sem,
):
    me_r, me_c = lax.axis_index("row"), lax.axis_index("col")

    def device(dr, dc):
        return (lax.rem(me_r + (dr + n_row), n_row), lax.rem(me_c + (dc + n_col), n_col))

    loads = [
        pltpu.make_async_copy(
            state.at[:, :, pl.ds(128 * g, 128)], st.at[:, g, pl.ds(BASE, 128), :], local_sem.at[g]
        )
        for g in range(2)
    ]
    loads += [
        pltpu.make_async_copy(pos_hbm, pos, local_sem.at[2]),
        pltpu.make_async_copy(ext_hbm, ext, local_sem.at[3]),
    ]
    for load in loads:
        load.start()
    barrier = pltpu.get_barrier_semaphore()
    around = [(a, b) for a in (-1, 0, 1) for b in (-1, 0, 1) if (a, b) != (0, 0)]
    for a, b in around:
        pl.semaphore_signal(barrier, inc=1, device_id=device(a, b), device_id_type=MESH)

    lane = lanes()
    lane1 = lanes((1, 128))
    cnt_s[...] = jnp.where(lane1 == 0, row_count[...], col_count[...])
    for load in loads:
        load.wait()
    for c in range(3):
        right = left = None
        for k in range(16):
            at = chunk(BASE + 8 * k)
            mine = (lane >= 8 * k) & (lane < 8 * k + 8)
            r, l = roll(st[c, 1, at, :], 8 * k - 120), roll(st[c, 0, at, :], 8 * k)
            right = r if right is None else jnp.where(mine, r, right)
            left = l if left is None else jnp.where(mine, l, left)
        rpack[c] = right
        lpack[c] = left
        for k in range(8):
            near, far = st[c, 1, chunk(BASE + 8 * k), :], st[c, 1, chunk(BASE + 64 + 8 * k), :]
            rslab[c, chunk(8 * k), :] = jnp.where(lane < 64, roll(far, 64), near)
        for k in range(4):
            near, far = st[c, 1, chunk(BASE + 64 + 8 * k), :], st[c, 1, chunk(BASE + 96 + 8 * k), :]
            drslab[c, chunk(8 * k), :] = jnp.where(lane < 64, roll(far, 64), near)

    pl.semaphore_wait(barrier, 8)
    both = pl.ds(0, 2)
    messages = [
        ((0, 1), rpack, lr),
        ((0, -1), lpack, rl),
        ((1, 0), st.at[:, both, pl.ds(BASE + 112, 16), :], st.at[:, both, pl.ds(BASE - 16, 16), :]),
        ((-1, 0), st.at[:, both, pl.ds(BASE, 8), :], st.at[:, both, pl.ds(BASE + 128, 8), :]),
        ((1, 1), st.at[:, 1, pl.ds(BASE + 120, 8), :], ulc),
        ((1, -1), lpack, url),
        ((-1, 1), st.at[:, 1, pl.ds(BASE, 8), :], dlc),
        ((-1, -1), st.at[:, 0, pl.ds(BASE, 8), :], drc),
        ((0, 1), rslab, lslab),
        ((1, 1), drslab, ulslab),
        ((1, 0), st.at[:, both, pl.ds(BASE + 64, 48), :], st.at[:, both, pl.ds(0, 48), :]),
        ((0, 1), cnt_s, cnt.at[0]),
        ((0, -1), cnt_s, cnt.at[1]),
        ((1, 0), cnt_s, cnt.at[2]),
        ((-1, 0), cnt_s, cnt.at[3]),
        ((1, -1), cnt_s, cnt.at[4]),
        ((-1, 1), cnt_s, cnt.at[5]),
        ((-1, -1), cnt_s, cnt.at[6]),
    ]
    copies = [
        pltpu.make_async_remote_copy(
            src_ref=src, dst_ref=dst, send_sem=send_sem.at[i], recv_sem=recv_sem.at[i],
            device_id=device(*to), device_id_type=MESH,
        )
        for i, (to, src, dst) in enumerate(messages)
    ]
    for copy in copies:
        copy.start()
    for copy in copies[:8]:
        copy.wait_recv()

    for c in range(3):
        for k in range(-8, 17):
            if k < 0:
                right = roll(url[c], -8 * (k + 16))
            elif k < 16:
                right = roll(rl[c], -8 * k)
            else:
                right = drc[c]
            if k < -1:
                value = right
            else:
                left = ulc[c] if k < 0 else dlc[c] if k == 16 else roll(lr[c], 120 - 8 * k)
                value = jnp.where(lane < 64, right, left)
            st[c, 2, chunk(BASE + 8 * k), :] = value

    speed_pass(st, vel, 3, 7, 25)
    step_pass(st, vel, fine1, 3, 3, 7, 25)
    speed_pass(fine1, vel, 3, 7, 25)
    step_pass(fine1, vel, fine2, 3, 2, 8, 24)

    def coarsen(i, carry):
        for c in range(3):
            parts = coarse_rows(st, pl.multiple_of(BASE - 16 + 16 * i, 16), 3, c)
            for g in range(2):
                cgrid[c, g, chunk(pl.multiple_of(8 * i, 8)), :] = parts[g]
        return carry

    lax.fori_loop(0, 10, coarsen, 0, unroll=True)
    speed_pass(cgrid, cvel, 2, 0, 10)
    step_pass(cgrid, cvel, cone, 2, 1, 1, 9)

    def estimate(i, carry):
        total = None
        for c in range(3):
            fine = coarse_rows(fine2, pl.multiple_of(BASE + 16 * i, 16), 2, c)[0]
            gap = jnp.abs(fine - cone[c, 0, chunk(pl.multiple_of(8 * i + 8, 8)), :])
            total = gap if total is None else total + gap
        err[chunk(pl.multiple_of(8 * i, 8)), :] = 10.0 * total
        return carry

    lax.fori_loop(0, 8, estimate, 0, unroll=True)

    for copy in copies[8:]:
        copy.wait_recv()
    keep = [
        pltpu.make_async_copy(cnt, counts.at[pl.ds(0, 7)], local_sem.at[0]),
        pltpu.make_async_copy(cnt_s, counts.at[7], local_sem.at[1]),
    ]
    for copy in keep:
        copy.start()
    for copy in copies:
        copy.wait_send()
    for copy in keep:
        copy.wait()


def patch_kernel(
    cnt, pos, ext, st, lslab, ulslab, dlc, err_in,
    err, moved, refined,
    lext, tiles, win, wvel, ctr, dcol, plus, base, mid, low,
):
    lane = lanes()
    row8 = lax.broadcasted_iota(jnp.int32, (8, 128), 0)
    err[...] = err_in[...]
    for c in range(3):
        for k in range(8):
            x = lslab[c, chunk(8 * k), :]
            lext[c, chunk(BASE + 8 * k), :] = x
            lext[c, chunk(BASE + 64 + 8 * k), :] = roll(x, 64)
        for k in range(4):
            x = ulslab[c, chunk(8 * k), :]
            lext[c, chunk(8 * k), :] = x
            lext[c, chunk(32 + 8 * k), :] = roll(x, 64)
        lext[c, chunk(BASE + 128), :] = dlc[c]

    rc, cc = cnt[7, 0, 0], cnt[7, 0, 1]
    rc_of = lambda i: cnt[i, 0, 0]
    cc_of = lambda i: cnt[i, 0, 1]
    rows_in = (rc_of(0), rc, rc, rc_of(1))
    rows_below = (rc_of(5), rc_of(3), rc_of(3), rc_of(6))
    cols_in = {"up": (cc_of(2), cc_of(4)), "own": (cc, cc_of(1)), "down": (cc_of(3), cc_of(6))}

    for c in range(3):
        columns = [lext.at[c], st.at[c, 0], st.at[c, 1], st.at[c, 2]]
        for k in range(-1, 17):
            at = chunk(BASE + 8 * k)
            values = [ref[at, :] for ref in columns]
            if 0 <= k < 8 or k == 16:
                counts = rows_below if k == 16 else rows_in
                first = 0 if k == 16 else 8 * k
                for g in range(4):
                    above = columns[g][chunk(BASE + 8 * k - counts[g]), :]
                    values[g] = jnp.where(row8 + first < counts[g], above, values[g])
            c0, c_right = cols_in["up" if k < 0 else "down" if k == 16 else "own"]
            m0 = jnp.where(lane < c0, roll(values[0], c0), values[1])
            m_right = jnp.where(lane < c_right, roll(values[2], c_right), values[3])
            put = chunk(8 * k + 8)
            for g, value in enumerate((values[0], m0, values[2], m_right)):
                tiles[g, c, put, :] = value
            if 0 <= k < 16:
                moved[c, chunk(8 * k), pl.ds(0, 128)] = m0
                moved[c, chunk(8 * k), pl.ds(128, 128)] = values[2]

    p0, p1 = pos[0, 0, 0], pos[0, 0, 1]
    group = lax.shift_right_logical(p1 + 126, 7)
    offset = lax.bitwise_and(p1 + 126, 127)
    back = lax.bitwise_and(128 - offset, 127)
    for k in range(10):
        u = []
        for c in range(3):
            at = chunk(p0 + 8 * k)
            a, b = tiles[group, c, at, :], tiles[group + 1, c, at, :]
            u.append(jnp.where(lane < 128 - offset, roll(a, back), roll(b, back)))
            win[c, chunk(8 * k + 8), :] = u[c]
        for c, value in enumerate(speeds(*u)):
            wvel[c, chunk(8 * k + 8), :] = value

    front = lane < 64
    for k in range(10):
        row = 8 * k + 8

        def load(shift, normal):
            at = chunk(row + shift)
            return side([win[c, at, :] for c in range(3)], [wvel[c, at, :] for c in range(3)], normal)

        here = load(0, 1)
        down, up = face(load(-1, 1), here), face(here, load(1, 1))
        across = load(0, 2)
        lower = (
            [roll(x, 1) for x in across[0]],
            [roll(x, 1) for x in across[1]],
            roll(across[2], 1),
        )
        left = face(lower, across)
        right = [roll(x, 127) for x in left]
        for a in range(2):
            far = []
            for c in range(3):
                twice = 2.0 * here[1][c]
                tall = up[c] - twice if a else twice - down[c]
                mid_c = here[0][c] - HALF * tall
                twice = 2.0 * across[1][c]
                e = mid_c - HALF * (twice - left[c])
                o = mid_c - HALF * (right[c] - twice)
                center = jnp.where(front, roll(e, -2), roll(o, 62))
                ctr[a, c, chunk(row), :] = center
                if 1 <= k < 9:
                    e62, o2 = roll(e, 62), roll(o, -1)
                    l1 = jnp.where(front, o2, e62)
                    r1 = jnp.where(front, roll(o, -2), roll(e, 61))
                    l2 = jnp.where(front, roll(e, -1), roll(o, 63))
                    r2 = jnp.where(front, roll(e, -3), roll(o, 61))
                    d1, d2, d3, d4 = l1 - l2, center - l1, r1 - center, r2 - r1
                    s_l, s_c, s_r = minmod(d1, d2), minmod(d2, d3), minmod(d3, d4)
                    far.append(
                        (l1 + 0.5 * s_l, center - 0.5 * s_c, center + 0.5 * s_c, r1 - 0.5 * s_r)
                    )
            if 1 <= k < 9:
                sides = [[far[c][i] for c in range(3)] for i in range(4)]
                sides = [side(s, speeds(*s), 2) for s in sides]
                f_low, f_high = face(sides[0], sides[1]), face(sides[2], sides[3])
                for c in range(3):
                    dcol[a, c, chunk(row), :] = f_high[c] - f_low[c]

    for k in range(10):
        row = 8 * k + 8
        at = chunk(row)
        l_side, r_side = [], []
        for c in range(3):
            c0, c1 = ctr[0, c, at, :], ctr[1, c, at, :]
            inner = c1 - c0
            before = c0 - ctr[1, c, chunk(row - 1), :]
            after = ctr[0, c, chunk(row + 1), :] - c1
            s0, s1 = minmod(before, inner), minmod(inner, after)
            base[c, at, :] = c0 - 0.5 * s0
            plus[c, at, :] = c1 + 0.5 * s1
            l_side.append(c0 + 0.5 * s0)
            r_side.append(c1 - 0.5 * s1)
        if 1 <= k < 9:
            f = face(side(l_side, speeds(*l_side), 1), side(r_side, speeds(*r_side), 1))
            for c in range(3):
                mid[c, at, :] = f[c]
    for k in range(1, 10):
        row = 8 * k + 8
        l_side = [plus[c, chunk(row - 1), :] for c in range(3)]
        r_side = [base[c, chunk(row), :] for c in range(3)]
        f = face(side(l_side, speeds(*l_side), 1), side(r_side, speeds(*r_side), 1))
        for c in range(3):
            low[c, chunk(row), :] = f[c]
    spread = lax.shift_right_logical(lane, 1) + 64 * lax.bitwise_and(lane, 1)
    inside_col = lax.bitwise_and(lane, 63) < ext[0, 0, 1]
    for k in range(1, 9):
        row = 8 * k + 8
        inside = inside_col & (row8 + 8 * (k - 1) < ext[0, 0, 0])
        for c in range(3):
            at = chunk(row)
            f_mid, f_low, f_next = mid[c, at, :], low[c, at, :], low[c, chunk(row + 1), :]
            for a, tall in enumerate((f_mid - f_low, f_next - f_mid)):
                done = ctr[a, c, at, :] - HALF * (tall + dcol[a, c, at, :])
                done = jnp.where(inside, done, 0.0)
                refined[c, pl.ds(16 * (k - 1) + a, 8, stride=2), :] = jnp.take_along_axis(
                    done, spread, axis=1, mode="promise_in_bounds"
                )


def solution(mesh):
    n_row, n_col = mesh.shape["row"], mesh.shape["col"]
    vmem = pl.BlockSpec(memory_space=pltpu.VMEM)
    smem = pl.BlockSpec(memory_space=pltpu.SMEM)
    hbm = pl.BlockSpec(memory_space=pltpu.HBM)
    buf = lambda *shape: pltpu.VMEM(shape, F32)

    def per_device(state, row_count, col_count, patch_pos, patch_ext):
        in_hbm = [
            x if x.ndim == 2 else pltpu.with_memory_space_constraint(x, pltpu.HBM)
            for x in (state, row_count, col_count, patch_pos, patch_ext)
        ]
        st, lslab, ulslab, dlc, cnt, pos, ext, err = pl.pallas_call(
            functools.partial(exchange_kernel, n_row, n_col),
            out_shape=(
                buf(3, 3, ROWS, 128),
                buf(3, 64, 128),
                buf(3, 32, 128),
                buf(3, 8, 128),
                pltpu.SMEM((8, 1, 128), jnp.int32),
                pltpu.SMEM((1, 1, 2), jnp.int32),
                pltpu.SMEM((1, 1, 2), jnp.int32),
                buf(64, 128),
            ),
            in_specs=[hbm, vmem, vmem, hbm, hbm],
            out_specs=(vmem,) * 4 + (smem,) * 3 + (vmem,),
            scratch_shapes=[
                buf(3, 8, 128), buf(3, 8, 128), buf(3, 64, 128), buf(3, 32, 128),
                pltpu.VMEM((1, 128), jnp.int32),
                *([buf(3, 8, 128)] * 5),
                buf(3, 3, ROWS, 128), buf(3, 3, ROWS, 128), buf(3, 2, ROWS, 128),
                buf(3, 2, 88, 128), buf(3, 2, 88, 128), buf(3, 1, 88, 128),
                pltpu.VMEM((7, 1, 128), jnp.int32),
                pltpu.SemaphoreType.DMA((4,)),
                pltpu.SemaphoreType.DMA((N_MSG,)),
                pltpu.SemaphoreType.DMA((N_MSG,)),
            ],
            compiler_params=pltpu.CompilerParams(
                collective_id=0, has_side_effects=True, vmem_limit_bytes=24 << 20
            ),
        )(*in_hbm)
        return pl.pallas_call(
            patch_kernel,
            out_shape=(
                jax.ShapeDtypeStruct((64, 128), F32),
                jax.ShapeDtypeStruct((3, 128, 256), F32),
                jax.ShapeDtypeStruct((3, 128, 128), F32),
            ),
            in_specs=[smem] * 3 + [vmem] * 5,
            out_specs=(vmem,) * 3,
            scratch_shapes=[
                buf(3, ROWS, 128), buf(4, 3, 144, 128), buf(3, 96, 128), buf(3, 96, 128),
                buf(2, 3, 96, 128), buf(2, 3, 96, 128),
                buf(3, 96, 128), buf(3, 96, 128), buf(3, 96, 128), buf(3, 96, 128),
            ],
            compiler_params=pltpu.CompilerParams(vmem_limit_bytes=24 << 20),
        )(cnt, pos, ext, st, lslab, ulslab, dlc, err)

    return jax.shard_map(
        per_device,
        mesh=mesh,
        in_specs=(
            P(None, "row", "col"),
            P("row", "col"),
            P("row", "col"),
            P("row", "col", None),
            P("row", "col", None),
        ),
        out_specs=(P("row", "col"), P(None, "row", "col"), P(None, "row", "col")),
        check_vma=False,
    )
```

```python
import functools

import jax
import jax.numpy as jnp
from jax import lax
from jax.experimental import pallas as pl
from jax.experimental.pallas import tpu as pltpu
from jax.sharding import PartitionSpec as P

MESH = pl.DeviceIdType.MESH
F32 = jnp.float32
HALF = 0.05
BASE = 64
ROWS = 208
N_MSG = 18


def chunk(start, size=8):
    return pl.ds(start, size)


def lanes(shape=(8, 128)):
    return lax.broadcasted_iota(jnp.int32, shape, 1)


def roll(x, by):
    return pltpu.roll(x, by % x.shape[1] if isinstance(by, int) else by, 1)


def speeds(h, m1, m2):
    return m1 / h, m2 / h, jnp.sqrt(h)


def side(u, vel, normal):
    h, m1, m2 = u
    v1, v2, wave = vel
    pressure = 0.5 * h * h
    if normal == 1:
        return u, (m1, m1 * v1 + pressure, m2 * v1), jnp.abs(v1) + wave
    return u, (m2, m1 * v2, m2 * v2 + pressure), jnp.abs(v2) + wave


def face(lower, upper):
    speed = jnp.maximum(lower[2], upper[2])
    return [
        (lower[1][c] + upper[1][c]) - speed * (upper[0][c] - lower[0][c])
        for c in range(3)
    ]


def minmod(a, b):
    chosen = jnp.where(jnp.abs(a) < jnp.abs(b), a, b)
    return jnp.where(a * b > 0, chosen, 0.0)


def from_lower(xs, lane):
    rolled = [roll(x, 1) for x in xs]
    return [jnp.where(lane == 0, rolled[g - 1], rolled[g]) for g in range(len(xs))]


def from_upper(xs, lane):
    rolled = [roll(x, 127) for x in xs]
    return [
        jnp.where(lane == 127, rolled[(g + 1) % len(xs)], rolled[g])
        for g in range(len(xs))
    ]


def speed_pass(src, vel, groups, first, last):
    for i in range(first, last):
        at = chunk(8 * i)
        for g in groups:
            for k, value in enumerate(speeds(*(src[c, g, at, :] for c in range(3)))):
                vel[k, g, at, :] = value


def step_pass(src, vel, dst, groups, first, last):
    lane = lanes()
    for i in range(first, last):
        row = 8 * i

        def load(shift, g, normal):
            at = chunk(row + shift)
            return side(
                [src[c, g, at, :] for c in range(3)],
                [vel[c, g, at, :] for c in range(3)],
                normal,
            )

        along = [load(0, g, 2) for g in groups]
        shifted = [from_lower([a[0][k] for a in along], lane) for k in range(3)]
        low = []
        for n in range(len(groups)):
            u = [x[n] for x in shifted]
            low.append(face(side(u, speeds(*u), 2), along[n]))
        high = [from_upper([f[c] for f in low], lane) for c in range(3)]
        for n, g in enumerate(groups):
            here = load(0, g, 1)
            down = face(load(-1, g, 1), here)
            up = face(here, load(1, g, 1))
            for c in range(3):
                change = (up[c] - down[c]) + (high[c][n] - low[n][c])
                dst[c, g, chunk(row), :] = here[0][c] - HALF * change


def coarse_rows(src, row, g, c, even):
    pair = src[c, g, pl.ds(row, 8, stride=2), :] + src[c, g, pl.ds(row + 1, 8, stride=2), :]
    pair = pair + roll(pair, 127)
    return 0.25 * jnp.take_along_axis(pair, even, axis=1, mode="promise_in_bounds")


def exchange_kernel(
    n_row, n_col, state, row_count, col_count, pos_hbm, ext_hbm,
    st, rm, l_low, l_high, ulc, dlc, drc, counts, pos, ext, err,
    rpack, lpack, low_s, high_s, cnt_s, lr, rl, url, up_low, ahead,
    vel, rim, fine1, fine2, cgrid, cvel, cone,
    cnt, local_sem, send_sem, recv_sem,
):
    me_r, me_c = lax.axis_index("row"), lax.axis_index("col")

    def device(dr, dc):
        return (lax.rem(me_r + (dr + n_row), n_row), lax.rem(me_c + (dc + n_col), n_col))

    loads = [
        pltpu.make_async_copy(
            state.at[:, :, pl.ds(128 * g, 128)], st.at[:, g, pl.ds(BASE, 128), :], local_sem.at[g]
        )
        for g in range(2)
    ]
    loads += [
        pltpu.make_async_copy(pos_hbm, pos, local_sem.at[2]),
        pltpu.make_async_copy(ext_hbm, ext, local_sem.at[3]),
    ]
    for load in loads:
        load.start()
    barrier = pltpu.get_barrier_semaphore()
    around = [(a, b) for a in (-1, 0, 1) for b in (-1, 0, 1) if (a, b) != (0, 0)]
    for a, b in around:
        pl.semaphore_signal(barrier, inc=1, device_id=device(a, b), device_id_type=MESH)

    lane = lanes()
    row8 = lax.broadcasted_iota(jnp.int32, (8, 128), 0)
    rc = row_count[0, 0]
    cnt_s[...] = jnp.where(lanes((1, 128)) == 0, rc, col_count[0, 0])
    for load in loads:
        load.wait()

    def edge(columns, lane_at):
        tile = None
        for c in range(3):
            for k in range(16):
                to = 32 * c + 2 * k
                x = roll(columns(c, k), to - lane_at)
                tile = x if tile is None else jnp.where(lane >= to, x, tile)
        return tile

    def fold(low, high):
        return jnp.where(lane < 64, roll(high, 64), low)

    rpack[...] = edge(lambda c, k: st[c, 1, chunk(BASE + 8 * k), :], 126)
    lpack[...] = edge(lambda c, k: st[c, 0, chunk(BASE + 8 * k), :], 0)
    for c in range(3):
        for k in range(4):
            low_s[c, chunk(8 * k), :] = fold(
                st[c, 1, chunk(BASE + 64 + 8 * k), :], st[c, 1, chunk(BASE + 96 + 8 * k), :]
            )

    pl.semaphore_wait(barrier, 8)
    both = pl.ds(0, 2)
    head, tail = pl.ds(0, 2), pl.ds(6, 2)
    messages = [
        ((1, 0), low_s, up_low),
        ((0, 1), rpack, lr),
        ((0, -1), lpack, rl),
        ((1, 0), st.at[:, both, pl.ds(BASE + 112, 16), :], st.at[:, both, pl.ds(BASE - 16, 16), :]),
        ((-1, 0), st.at[:, both, pl.ds(BASE, 8), :], st.at[:, both, pl.ds(BASE + 128, 8), :]),
        ((1, 1), st.at[:, 1, pl.ds(BASE + 126, 2), :], ulc.at[:, tail, :]),
        ((1, -1), lpack, url),
        ((-1, 1), st.at[:, 1, pl.ds(BASE, 2), :], dlc.at[:, head, :]),
        ((-1, -1), st.at[:, 0, pl.ds(BASE, 2), :], drc.at[:, head, :]),
        ((0, 1), low_s, l_low),
        ((1, 0), st.at[:, both, pl.ds(BASE + 64, 48), :], st.at[:, both, pl.ds(0, 48), :]),
        ((0, -1), cnt_s, cnt.at[0]),
        ((1, 0), cnt_s, cnt.at[1]),
        ((-1, 0), cnt_s, cnt.at[2]),
        ((1, -1), cnt_s, cnt.at[3]),
        ((-1, 1), cnt_s, cnt.at[4]),
        ((-1, -1), cnt_s, cnt.at[5]),
        ((0, 1), high_s, l_high),
    ]
    copies = [
        pltpu.make_async_remote_copy(
            src_ref=src, dst_ref=dst, send_sem=send_sem.at[i], recv_sem=recv_sem.at[i],
            device_id=device(*to), device_id_type=MESH,
        )
        for i, (to, src, dst) in enumerate(messages)
    ]
    for copy in copies[:17]:
        copy.start()

    even = lax.rem(2 * lane, 128)
    own = (0, 1)
    speed_pass(st, vel, own, 8, 24)
    step_pass(st, vel, fine1, own, 9, 23)

    copies[0].wait_recv()
    for c in range(3):
        for k in range(4):
            x = up_low[c, chunk(8 * k), :]
            ahead[c, chunk(8 * k), :] = x
            ahead[c, chunk(32 + 8 * k), :] = roll(x, 64)
        for k in range(8):
            ahead[c, chunk(64 + 8 * k), :] = st[c, 1, chunk(BASE + 8 * k), :]
    for c in range(3):
        top = [
            jnp.where(
                row8 + 8 * k < rc,
                ahead[c, chunk(64 + 8 * k - rc), :],
                ahead[c, chunk(64 + 8 * k), :],
            )
            for k in range(8)
        ]
        for k in range(4):
            high_s[c, chunk(8 * k), :] = fold(top[k], top[k + 4])
    copies[17].start()

    def coarse_own(i):
        for c in range(3):
            halves = [coarse_rows(st, BASE - 16 + 16 * i, g, c, even) for g in range(2)]
            cgrid[c, 0, chunk(8 * i), :] = jnp.where(lane < 64, *halves)
        speed_pass(cgrid, cvel, (0,), i, i + 1)

    def estimate(i):
        total = None
        for c in range(3):
            halves = [coarse_rows(fine2, BASE + 16 * i, g, c, even) for g in range(2)]
            gap = jnp.abs(jnp.where(lane < 64, *halves) - cone[c, 0, chunk(8 * i + 8), :])
            total = gap if total is None else total + gap
        err[chunk(8 * i), :] = 10.0 * total

    speed_pass(fine1, vel, own, 9, 23)
    step_pass(fine1, vel, fine2, own, 10, 22)
    for i in range(1, 9):
        coarse_own(i)
    step_pass(cgrid, cvel, cone, (0,), 2, 8)
    for i in range(1, 7):
        estimate(i)

    for copy in copies[1:9]:
        copy.wait_recv()
    speed_pass(st, rim, own, 7, 10)
    speed_pass(st, rim, own, 22, 25)
    step_pass(st, rim, fine1, own, 7, 9)
    step_pass(st, rim, fine1, own, 23, 25)
    speed_pass(fine1, rim, own, 7, 11)
    speed_pass(fine1, rim, own, 21, 25)
    step_pass(fine1, rim, fine2, own, 8, 10)
    step_pass(fine1, rim, fine2, own, 22, 24)
    coarse_own(0)
    coarse_own(9)
    step_pass(cgrid, cvel, cone, (0,), 1, 2)
    step_pass(cgrid, cvel, cone, (0,), 8, 9)
    estimate(0)
    estimate(7)

    left, right, corner = lr[...], rl[...], url[...]
    for c in range(3):
        for k in range(-8, 17):
            at = chunk(BASE + 8 * k)
            col = 32 * c + 2 * k
            r = roll(corner, -(col + 32)) if k < 0 else drc[c] if k == 16 else roll(right, -col)
            if k >= -1:
                ends = ulc[c] if k < 0 else dlc[c]
                x = roll(left, 62 - col) if 0 <= k < 16 else roll(ends, 64)
                x = jnp.where(lane < 64, x, roll(st[c, 0, at, :], 64))
                r = jnp.where(lane < 32, r, jnp.where(lane < 124, x, st[c, 1, at, :]))
            st[c, 2, at, :] = r
    strip = (2,)
    speed_pass(st, vel, strip, 7, 25)
    step_pass(st, vel, fine1, strip, 7, 25)
    speed_pass(fine1, vel, strip, 7, 25)
    step_pass(fine1, vel, fine2, strip, 8, 24)
    for i in range(10):
        for c in range(3):
            cgrid[c, 1, chunk(8 * i), :] = coarse_rows(st, BASE - 16 + 16 * i, 2, c, even)
    speed_pass(cgrid, cvel, (1,), 0, 10)
    step_pass(cgrid, cvel, cone, (1,), 1, 9)
    for i in range(8):
        total = None
        for c in range(3):
            fine = coarse_rows(fine2, BASE + 16 * i, 2, c, even)
            gap = jnp.abs(fine - cone[c, 1, chunk(8 * i + 8), :])
            total = gap if total is None else total + gap
        total = 10.0 * total
        at = chunk(8 * i)
        value = jnp.where(lane == 127, total, err[at, :])
        err[at, :] = jnp.where(lane == 0, roll(total, 96), value)

    for copy in copies[9:17]:
        copy.wait_recv()
    for c in range(3):
        for g in range(2):
            for k in range(8):
                here = st[c, g, chunk(BASE + 8 * k), :]
                above = st[c, g, chunk(BASE + 8 * k - rc), :]
                rm[c, g, chunk(8 * k), :] = jnp.where(row8 + 8 * k < rc, above, here)
    copies[17].wait_recv()
    keep = [
        pltpu.make_async_copy(cnt, counts.at[pl.ds(0, 6)], local_sem.at[0]),
        pltpu.make_async_copy(cnt_s, counts.at[6], local_sem.at[1]),
    ]
    for copy in keep:
        copy.start()
    for copy in copies:
        copy.wait_send()
    for copy in keep:
        copy.wait()


def patch_kernel(
    cnt, pos, ext, st, rm, l_low, l_high, ulc, dlc, err_in,
    err, moved, refined,
    tiles, win, wvel, ctr, dcol, plus, base, mid, low,
):
    lane = lanes()
    row8 = lax.broadcasted_iota(jnp.int32, (8, 128), 0)
    err[...] = err_in[...]
    rc_of = lambda i: cnt[i, 0, 0]
    cc_of = lambda i: cnt[i, 0, 1]
    rows_below = (rc_of(4), rc_of(2), rc_of(2), rc_of(5))
    cols_in = {"up": (cc_of(1), cc_of(3)), "own": (cc_of(6), cc_of(0)), "down": (cc_of(2), cc_of(5))}

    rc_right = rc_of(0)
    for c in range(3):
        for k in range(4):
            for start, half in ((0, l_high), (64, l_low)):
                x = half[c, chunk(8 * k), :]
                tiles[0, c, chunk(8 + start + 8 * k), :] = x
                tiles[0, c, chunk(40 + start + 8 * k), :] = roll(x, 64)
        tiles[0, c, chunk(0), :] = ulc[c]

    for c in range(3):
        for k in range(-1, 17):
            at = chunk(BASE + 8 * k)
            if k < 0:
                values = [ulc[c], st[c, 0, at, :], st[c, 1, at, :], st[c, 2, at, :]]
            elif k < 16:
                own = [rm[c, g, chunk(8 * k), :] if k < 8 else st[c, g, at, :] for g in range(2)]
                beside = st[c, 2, at, :]
                if k < 8:
                    above = st[c, 2, chunk(BASE + 8 * k - rc_right), :]
                    beside = jnp.where(row8 + 8 * k < rc_right, above, beside)
                values = [tiles[0, c, chunk(8 * k + 8), :], *own, beside]
            else:
                above = [
                    tiles[0, c, chunk(136 - rows_below[0]), :],
                    st[c, 0, chunk(BASE + 128 - rows_below[1]), :],
                    st[c, 1, chunk(BASE + 128 - rows_below[2]), :],
                    st[c, 2, chunk(BASE + 128 - rows_below[3]), :],
                ]
                below = [dlc[c], st[c, 0, at, :], st[c, 1, at, :], st[c, 2, at, :]]
                values = [jnp.where(row8 < rows_below[g], above[g], below[g]) for g in range(4)]
                tiles[0, c, chunk(136), :] = values[0]
            c0, c_right = cols_in["up" if k < 0 else "down" if k == 16 else "own"]
            m0 = jnp.where(lane < c0, roll(values[0], c0), values[1])
            m_right = jnp.where(lane < c_right, roll(values[2], c_right), values[3])
            put = chunk(8 * k + 8)
            for g, value in enumerate((m0, values[2], m_right)):
                tiles[g + 1, c, put, :] = value
            if 0 <= k < 16:
                moved[c, chunk(8 * k), pl.ds(0, 128)] = m0
                moved[c, chunk(8 * k), pl.ds(128, 128)] = values[2]

    p0, p1 = pos[0, 0, 0], pos[0, 0, 1]
    group = lax.shift_right_logical(p1 + 126, 7)
    offset = lax.bitwise_and(p1 + 126, 127)
    back = lax.bitwise_and(128 - offset, 127)
    for k in range(10):
        u = []
        for c in range(3):
            at = chunk(p0 + 8 * k)
            a, b = tiles[group, c, at, :], tiles[group + 1, c, at, :]
            u.append(jnp.where(lane < 128 - offset, roll(a, back), roll(b, back)))
            win[c, chunk(8 * k + 8), :] = u[c]
        for c, value in enumerate(speeds(*u)):
            wvel[c, chunk(8 * k + 8), :] = value

    front = lane < 64
    for k in range(10):
        row = 8 * k + 8

        def load(shift, normal):
            at = chunk(row + shift)
            return side([win[c, at, :] for c in range(3)], [wvel[c, at, :] for c in range(3)], normal)

        here = load(0, 1)
        down, up = face(load(-1, 1), here), face(here, load(1, 1))
        across = load(0, 2)
        lower = (
            [roll(x, 1) for x in across[0]],
            [roll(x, 1) for x in across[1]],
            roll(across[2], 1),
        )
        left = face(lower, across)
        right = [roll(x, 127) for x in left]
        for a in range(2):
            far = []
            for c in range(3):
                twice = 2.0 * here[1][c]
                tall = up[c] - twice if a else twice - down[c]
                mid_c = here[0][c] - HALF * tall
                twice = 2.0 * across[1][c]
                e = mid_c - HALF * (twice - left[c])
                o = mid_c - HALF * (right[c] - twice)
                center = jnp.where(front, roll(e, -2), roll(o, 62))
                ctr[a, c, chunk(row), :] = center
                if 1 <= k < 9:
                    e62, o2 = roll(e, 62), roll(o, -1)
                    l1 = jnp.where(front, o2, e62)
                    r1 = jnp.where(front, roll(o, -2), roll(e, 61))
                    l2 = jnp.where(front, roll(e, -1), roll(o, 63))
                    r2 = jnp.where(front, roll(e, -3), roll(o, 61))
                    d1, d2, d3, d4 = l1 - l2, center - l1, r1 - center, r2 - r1
                    s_l, s_c, s_r = minmod(d1, d2), minmod(d2, d3), minmod(d3, d4)
                    far.append(
                        (l1 + 0.5 * s_l, center - 0.5 * s_c, center + 0.5 * s_c, r1 - 0.5 * s_r)
                    )
            if 1 <= k < 9:
                sides = [[far[c][i] for c in range(3)] for i in range(4)]
                sides = [side(s, speeds(*s), 2) for s in sides]
                f_low, f_high = face(sides[0], sides[1]), face(sides[2], sides[3])
                for c in range(3):
                    dcol[a, c, chunk(row), :] = f_high[c] - f_low[c]

    for k in range(10):
        row = 8 * k + 8
        at = chunk(row)
        l_side, r_side = [], []
        for c in range(3):
            c0, c1 = ctr[0, c, at, :], ctr[1, c, at, :]
            inner = c1 - c0
            before = c0 - ctr[1, c, chunk(row - 1), :]
            after = ctr[0, c, chunk(row + 1), :] - c1
            s0, s1 = minmod(before, inner), minmod(inner, after)
            base[c, at, :] = c0 - 0.5 * s0
            plus[c, at, :] = c1 + 0.5 * s1
            l_side.append(c0 + 0.5 * s0)
            r_side.append(c1 - 0.5 * s1)
        if 1 <= k < 9:
            f = face(side(l_side, speeds(*l_side), 1), side(r_side, speeds(*r_side), 1))
            for c in range(3):
                mid[c, at, :] = f[c]
    for k in range(1, 10):
        row = 8 * k + 8
        l_side = [plus[c, chunk(row - 1), :] for c in range(3)]
        r_side = [base[c, chunk(row), :] for c in range(3)]
        f = face(side(l_side, speeds(*l_side), 1), side(r_side, speeds(*r_side), 1))
        for c in range(3):
            low[c, chunk(row), :] = f[c]
    spread = lax.shift_right_logical(lane, 1) + 64 * lax.bitwise_and(lane, 1)
    inside_col = lax.bitwise_and(lane, 63) < ext[0, 0, 1]
    for k in range(1, 9):
        row = 8 * k + 8
        inside = inside_col & (row8 + 8 * (k - 1) < ext[0, 0, 0])
        for c in range(3):
            at = chunk(row)
            f_mid, f_low, f_next = mid[c, at, :], low[c, at, :], low[c, chunk(row + 1), :]
            for a, tall in enumerate((f_mid - f_low, f_next - f_mid)):
                done = ctr[a, c, at, :] - HALF * (tall + dcol[a, c, at, :])
                done = jnp.where(inside, done, 0.0)
                refined[c, pl.ds(16 * (k - 1) + a, 8, stride=2), :] = jnp.take_along_axis(
                    done, spread, axis=1, mode="promise_in_bounds"
                )


def solution(mesh):
    n_row, n_col = mesh.shape["row"], mesh.shape["col"]
    vmem = pl.BlockSpec(memory_space=pltpu.VMEM)
    smem = pl.BlockSpec(memory_space=pltpu.SMEM)
    hbm = pl.BlockSpec(memory_space=pltpu.HBM)
    buf = lambda *shape: pltpu.VMEM(shape, F32)

    def per_device(state, row_count, col_count, patch_pos, patch_ext):
        in_hbm = [
            x if x.ndim == 2 else pltpu.with_memory_space_constraint(x, pltpu.HBM)
            for x in (state, row_count, col_count, patch_pos, patch_ext)
        ]
        corner = buf(3, 8, 128)
        half = buf(3, 32, 128)
        *parts, _, cnt, pos, ext, err = pl.pallas_call(
            functools.partial(exchange_kernel, n_row, n_col),
            out_shape=(
                buf(3, 3, ROWS, 128), buf(3, 2, 64, 128), half, half, *([corner] * 3),
                pltpu.SMEM((7, 1, 128), jnp.int32),
                pltpu.SMEM((1, 1, 2), jnp.int32),
                pltpu.SMEM((1, 1, 2), jnp.int32),
                buf(64, 128),
            ),
            in_specs=[hbm, smem, smem, hbm, hbm],
            out_specs=(vmem,) * 7 + (smem,) * 3 + (vmem,),
            scratch_shapes=[
                buf(8, 128), buf(8, 128), half, half, pltpu.VMEM((1, 128), jnp.int32),
                buf(8, 128), buf(8, 128), buf(8, 128), half, buf(3, 128, 128),
                *([buf(3, 3, ROWS, 128)] * 4), *([buf(3, 2, 88, 128)] * 3),
                pltpu.VMEM((6, 1, 128), jnp.int32),
                pltpu.SemaphoreType.DMA((4,)),
                pltpu.SemaphoreType.DMA((N_MSG,)),
                pltpu.SemaphoreType.DMA((N_MSG,)),
            ],
            compiler_params=pltpu.CompilerParams(
                collective_id=0, has_side_effects=True, vmem_limit_bytes=24 << 20
            ),
        )(*in_hbm)
        return pl.pallas_call(
            patch_kernel,
            out_shape=(
                jax.ShapeDtypeStruct((64, 128), F32),
                jax.ShapeDtypeStruct((3, 128, 256), F32),
                jax.ShapeDtypeStruct((3, 128, 128), F32),
            ),
            in_specs=[smem] * 3 + [vmem] * 7,
            out_specs=(vmem,) * 3,
            scratch_shapes=[
                buf(4, 3, 144, 128), buf(3, 96, 128), buf(3, 96, 128),
                buf(2, 3, 96, 128), buf(2, 3, 96, 128),
                buf(3, 96, 128), buf(3, 96, 128), buf(3, 96, 128), buf(3, 96, 128),
            ],
            compiler_params=pltpu.CompilerParams(vmem_limit_bytes=24 << 20),
        )(cnt, pos, ext, *parts, err)

    return jax.shard_map(
        per_device,
        mesh=mesh,
        in_specs=(
            P(None, "row", "col"),
            P("row", "col"),
            P("row", "col"),
            P("row", "col", None),
            P("row", "col", None),
        ),
        out_specs=(P("row", "col"), P(None, "row", "col"), P(None, "row", "col")),
        check_vma=False,
    )
```

```python
import functools

import jax
import jax.numpy as jnp
from jax import lax
from jax.experimental import pallas as pl
from jax.experimental.pallas import tpu as pltpu
from jax.sharding import PartitionSpec as P

MESH = pl.DeviceIdType.MESH
F32 = jnp.float32
HALF = 0.05
BASE = 64
ROWS = 208
N_MSG = 18


def chunk(start, size=8):
    return pl.ds(start, size)


def lanes(shape=(8, 128)):
    return lax.broadcasted_iota(jnp.int32, shape, 1)


def roll(x, by):
    return pltpu.roll(x, by % x.shape[1] if isinstance(by, int) else by, 1)


def speeds(h, m1, m2):
    return m1 / h, m2 / h, jnp.sqrt(h)


def side(u, vel, normal):
    h, m1, m2 = u
    v1, v2, wave = vel
    pressure = 0.5 * h * h
    if normal == 1:
        return u, (m1, m1 * v1 + pressure, m2 * v1), jnp.abs(v1) + wave
    return u, (m2, m1 * v2, m2 * v2 + pressure), jnp.abs(v2) + wave


def face(lower, upper):
    speed = jnp.maximum(lower[2], upper[2])
    return [
        (lower[1][c] + upper[1][c]) - speed * (upper[0][c] - lower[0][c])
        for c in range(3)
    ]


def minmod(a, b):
    chosen = jnp.where(jnp.abs(a) < jnp.abs(b), a, b)
    return jnp.where(a * b > 0, chosen, 0.0)


def from_lower(xs, lane, hop=1):
    rolled = [roll(x, hop) for x in xs]
    if len(xs) == 1:
        return rolled
    return [jnp.where(lane == 0, rolled[g - 1], rolled[g]) for g in range(len(xs))]


def from_upper(xs, lane, hop=1):
    rolled = [roll(x, -hop) for x in xs]
    if len(xs) == 1:
        return rolled
    return [
        jnp.where(lane == 127, rolled[(g + 1) % len(xs)], rolled[g])
        for g in range(len(xs))
    ]


def speed_pass(src, vel, groups, first, last):
    for i in range(first, last):
        at = chunk(8 * i)
        for g in groups:
            for k, value in enumerate(speeds(*(src[c, g, at, :] for c in range(3)))):
                vel[k, g, at, :] = value


def step_pass(src, vel, dst, groups, first, last, hop=1):
    lane = lanes()
    for i in range(first, last):
        row = 8 * i

        def load(shift, g, normal):
            at = chunk(row + shift)
            return side(
                [src[c, g, at, :] for c in range(3)],
                [vel[c, g, at, :] for c in range(3)],
                normal,
            )

        along = [load(0, g, 2) for g in groups]
        shifted = [from_lower([a[0][k] for a in along], lane, hop) for k in range(3)]
        low = []
        for n in range(len(groups)):
            u = [x[n] for x in shifted]
            low.append(face(side(u, speeds(*u), 2), along[n]))
        high = [from_upper([f[c] for f in low], lane, hop) for c in range(3)]
        for n, g in enumerate(groups):
            here = load(0, g, 1)
            down = face(load(-1, g, 1), here)
            up = face(here, load(1, g, 1))
            for c in range(3):
                change = (up[c] - down[c]) + (high[c][n] - low[n][c])
                dst[c, g, chunk(row), :] = here[0][c] - HALF * change


def block_means(src, row, g, c):
    pair = src[c, g, pl.ds(row, 8, stride=2), :] + src[c, g, pl.ds(row + 1, 8, stride=2), :]
    return 0.25 * (pair + roll(pair, 127))


def pick(x, index):
    return jnp.take_along_axis(x, index, axis=1, mode="promise_in_bounds")


def exchange_kernel(
    n_row, n_col, state, row_count, col_count, pos_hbm, ext_hbm,
    st, rm, l_low, l_high, ulc, dlc, drc, counts, pos, ext, err,
    rpack, lpack, low_s, high_s, cnt_s, lr, rl, url, up_low, ahead, sides,
    vel, rim, fine1, fine2, cgrid, cvel, cone,
    strip, svel, strip1, svel1, strip2, sgrid, sgvel, sone,
    cnt, local_sem, send_sem, recv_sem,
):
    me_r, me_c = lax.axis_index("row"), lax.axis_index("col")

    def device(dr, dc):
        return (lax.rem(me_r + (dr + n_row), n_row), lax.rem(me_c + (dc + n_col), n_col))

    loads = [
        pltpu.make_async_copy(
            state.at[:, :, pl.ds(128 * g, 128)], st.at[:, g, pl.ds(BASE, 128), :], local_sem.at[g]
        )
        for g in range(2)
    ]
    loads += [
        pltpu.make_async_copy(pos_hbm, pos, local_sem.at[2]),
        pltpu.make_async_copy(ext_hbm, ext, local_sem.at[3]),
    ]
    for load in loads:
        load.start()
    barrier = pltpu.get_barrier_semaphore()
    around = [(a, b) for a in (-1, 0, 1) for b in (-1, 0, 1) if (a, b) != (0, 0)]
    for a, b in around:
        pl.semaphore_signal(barrier, inc=1, device_id=device(a, b), device_id_type=MESH)

    lane = lanes()
    row8 = lax.broadcasted_iota(jnp.int32, (8, 128), 0)
    rc = row_count[0, 0]
    cnt_s[...] = jnp.where(lanes((1, 128)) == 0, rc, col_count[0, 0])
    for load in loads:
        load.wait()

    def edge(columns, lane_at):
        tile = None
        for c in range(3):
            for k in range(16):
                to = 32 * c + 2 * k
                x = roll(columns(c, k), to - lane_at)
                tile = x if tile is None else jnp.where(lane >= to, x, tile)
        return tile

    def fold(low, high):
        return jnp.where(lane < 64, roll(high, 64), low)

    rpack[...] = edge(lambda c, k: st[c, 1, chunk(BASE + 8 * k), :], 126)
    lpack[...] = edge(lambda c, k: st[c, 0, chunk(BASE + 8 * k), :], 0)
    for c in range(3):
        for k in range(4):
            low_s[c, chunk(8 * k), :] = fold(
                st[c, 1, chunk(BASE + 64 + 8 * k), :], st[c, 1, chunk(BASE + 96 + 8 * k), :]
            )

    pl.semaphore_wait(barrier, 8)
    both = pl.ds(0, 2)
    head, tail = pl.ds(0, 2), pl.ds(6, 2)
    messages = [
        ((1, 0), low_s, up_low),
        ((0, 1), rpack, lr),
        ((0, -1), lpack, rl),
        ((1, 0), st.at[:, both, pl.ds(BASE + 112, 16), :], st.at[:, both, pl.ds(BASE - 16, 16), :]),
        ((-1, 0), st.at[:, both, pl.ds(BASE, 8), :], st.at[:, both, pl.ds(BASE + 128, 8), :]),
        ((1, 1), st.at[:, 1, pl.ds(BASE + 126, 2), :], ulc.at[:, tail, :]),
        ((1, -1), lpack, url),
        ((-1, 1), st.at[:, 1, pl.ds(BASE, 2), :], dlc.at[:, head, :]),
        ((-1, -1), st.at[:, 0, pl.ds(BASE, 2), :], drc.at[:, head, :]),
        ((0, 1), low_s, l_low),
        ((1, 0), st.at[:, both, pl.ds(BASE + 64, 48), :], st.at[:, both, pl.ds(0, 48), :]),
        ((0, -1), cnt_s, cnt.at[0]),
        ((1, 0), cnt_s, cnt.at[1]),
        ((-1, 0), cnt_s, cnt.at[2]),
        ((1, -1), cnt_s, cnt.at[3]),
        ((-1, 1), cnt_s, cnt.at[4]),
        ((-1, -1), cnt_s, cnt.at[5]),
        ((0, 1), high_s, l_high),
    ]
    copies = [
        pltpu.make_async_remote_copy(
            src_ref=src, dst_ref=dst, send_sem=send_sem.at[i], recv_sem=recv_sem.at[i],
            device_id=device(*to), device_id_type=MESH,
        )
        for i, (to, src, dst) in enumerate(messages)
    ]
    for copy in copies[:17]:
        copy.start()

    for c in range(3):
        tile = None
        for g, from_lane in ((0, 0), (1, 124)):
            for k in range(16):
                to = 64 * g + 4 * k
                x = roll(st[c, g, chunk(BASE + 8 * k), :], to - from_lane)
                tile = x if tile is None else jnp.where(lane >= to, x, tile)
        sides[c] = tile

    even = lax.rem(2 * lane, 128)
    own = (0, 1)
    speed_pass(st, vel, own, 8, 24)
    step_pass(st, vel, fine1, own, 9, 23)

    copies[0].wait_recv()
    for c in range(3):
        for k in range(4):
            x = up_low[c, chunk(8 * k), :]
            ahead[c, chunk(8 * k), :] = x
            ahead[c, chunk(32 + 8 * k), :] = roll(x, 64)
        for k in range(8):
            ahead[c, chunk(64 + 8 * k), :] = st[c, 1, chunk(BASE + 8 * k), :]
    for c in range(3):
        top = [
            jnp.where(
                row8 + 8 * k < rc,
                ahead[c, chunk(64 + 8 * k - rc), :],
                ahead[c, chunk(64 + 8 * k), :],
            )
            for k in range(8)
        ]
        for k in range(4):
            high_s[c, chunk(8 * k), :] = fold(top[k], top[k + 4])
    copies[17].start()

    def coarse_own(i):
        for c in range(3):
            halves = [pick(block_means(st, BASE - 16 + 16 * i, g, c), even) for g in range(2)]
            cgrid[c, 0, chunk(8 * i), :] = jnp.where(lane < 64, *halves)
        speed_pass(cgrid, cvel, (0,), i, i + 1)

    def estimate(i):
        total = None
        for c in range(3):
            halves = [pick(block_means(fine2, BASE + 16 * i, g, c), even) for g in range(2)]
            gap = jnp.abs(jnp.where(lane < 64, *halves) - cone[c, 0, chunk(8 * i + 8), :])
            total = gap if total is None else total + gap
        err[chunk(8 * i), :] = 10.0 * total

    speed_pass(fine1, vel, own, 9, 23)
    step_pass(fine1, vel, fine2, own, 10, 22)
    for i in range(1, 9):
        coarse_own(i)
    step_pass(cgrid, cvel, cone, (0,), 2, 8)
    for i in range(1, 7):
        estimate(i)

    for copy in copies[1:9]:
        copy.wait_recv()
    speed_pass(st, rim, own, 7, 10)
    speed_pass(st, rim, own, 22, 25)
    step_pass(st, rim, fine1, own, 7, 9)
    step_pass(st, rim, fine1, own, 23, 25)
    speed_pass(fine1, rim, own, 7, 11)
    speed_pass(fine1, rim, own, 21, 25)
    step_pass(fine1, rim, fine2, own, 8, 10)
    step_pass(fine1, rim, fine2, own, 22, 24)
    coarse_own(0)
    coarse_own(9)
    step_pass(cgrid, cvel, cone, (0,), 1, 2)
    step_pass(cgrid, cvel, cone, (0,), 8, 9)
    estimate(0)
    estimate(7)

    left, right, corner = lr[...], rl[...], url[...]
    part, place = lax.shift_right_logical(lane, 4), lax.bitwise_and(lane, 15)

    def folded(a, b, c, d):
        return jnp.where(place < 2, a, jnp.where(place < 8, b, jnp.where(place < 12, c, d)))

    for j in range(4):
        block = 2 * part + (j - 1)
        own_at = lax.bitwise_and(4 * block + jnp.where(place < 8, place - 2, place + 56), 127)
        for c in range(3):
            at = lax.bitwise_and(32 * c + 2 * block + lax.bitwise_and(place, 1), 127)
            own_cells = pick(sides[c], own_at)
            x = folded(pick(left, at), own_cells, own_cells, pick(right, at))
            if j == 0:
                rows = chunk(BASE - 8)
                above = folded(
                    roll(ulc[c], 2), roll(st[c, 0, rows, :], 2),
                    roll(st[c, 1, rows, :], 12), roll(corner, -18 - 32 * c),
                )
                x = jnp.where(part == 0, above, x)
            if j == 3:
                rows = chunk(BASE + 128)
                below = folded(
                    roll(dlc[c], -14), roll(st[c, 0, rows, :], 114),
                    roll(st[c, 1, rows, :], -4), roll(drc[c], 124),
                )
                x = jnp.where(part == 7, below, x)
            strip[c, 0, chunk(8 + 8 * j), :] = x
    one = (0,)
    speed_pass(strip, svel, one, 1, 5)
    step_pass(strip, svel, strip1, one, 1, 5)
    speed_pass(strip1, svel1, one, 1, 5)
    step_pass(strip1, svel1, strip2, one, 2, 4)
    for i in range(3):
        for c in range(3):
            sgrid[c, 0, chunk(8 * i), :] = block_means(strip, 16 * i, 0, c)
    speed_pass(sgrid, sgvel, one, 0, 3)
    step_pass(sgrid, sgvel, sone, one, 1, 2, 2)
    total = None
    for c in range(3):
        gap = jnp.abs(block_means(strip2, 16, 0, c) - sone[c, 0, chunk(8), :])
        total = gap if total is None else total + gap
    total = 10.0 * total
    for i in range(8):
        at = chunk(8 * i)
        value = jnp.where(lane == 127, roll(total, 117 - 16 * i), err[at, :])
        err[at, :] = jnp.where(lane == 0, roll(total, -(16 * i + 2)), value)

    for c in range(3):
        for k in range(-8, 17):
            col = 32 * c + 2 * k
            x = roll(corner, -(col + 32)) if k < 0 else drc[c] if k == 16 else roll(right, -col)
            st[c, 2, chunk(BASE + 8 * k), :] = x

    for copy in copies[9:17]:
        copy.wait_recv()
    for c in range(3):
        for g in range(2):
            for k in range(8):
                here = st[c, g, chunk(BASE + 8 * k), :]
                above = st[c, g, chunk(BASE + 8 * k - rc), :]
                rm[c, g, chunk(8 * k), :] = jnp.where(row8 + 8 * k < rc, above, here)
    copies[17].wait_recv()
    keep = [
        pltpu.make_async_copy(cnt, counts.at[pl.ds(0, 6)], local_sem.at[0]),
        pltpu.make_async_copy(cnt_s, counts.at[6], local_sem.at[1]),
    ]
    for copy in keep:
        copy.start()
    for copy in copies:
        copy.wait_send()
    for copy in keep:
        copy.wait()


def patch_kernel(
    cnt, pos, ext, st, rm, l_low, l_high, ulc, dlc, err_in,
    err, moved, refined,
    tiles, win, wvel, ctr, dcol, plus, base, mid, low,
):
    lane = lanes()
    row8 = lax.broadcasted_iota(jnp.int32, (8, 128), 0)
    err[...] = err_in[...]
    rc_of = lambda i: cnt[i, 0, 0]
    cc_of = lambda i: cnt[i, 0, 1]
    rows_below = (rc_of(4), rc_of(2), rc_of(2), rc_of(5))
    cols_in = {"up": (cc_of(1), cc_of(3)), "own": (cc_of(6), cc_of(0)), "down": (cc_of(2), cc_of(5))}

    rc_right = rc_of(0)
    for c in range(3):
        for k in range(4):
            for start, half in ((0, l_high), (64, l_low)):
                x = half[c, chunk(8 * k), :]
                tiles[0, c, chunk(8 + start + 8 * k), :] = x
                tiles[0, c, chunk(40 + start + 8 * k), :] = roll(x, 64)
        tiles[0, c, chunk(0), :] = ulc[c]

    for c in range(3):
        for k in range(-1, 17):
            at = chunk(BASE + 8 * k)
            if k < 0:
                values = [ulc[c], st[c, 0, at, :], st[c, 1, at, :], st[c, 2, at, :]]
            elif k < 16:
                own = [rm[c, g, chunk(8 * k), :] if k < 8 else st[c, g, at, :] for g in range(2)]
                beside = st[c, 2, at, :]
                if k < 8:
                    above = st[c, 2, chunk(BASE + 8 * k - rc_right), :]
                    beside = jnp.where(row8 + 8 * k < rc_right, above, beside)
                values = [tiles[0, c, chunk(8 * k + 8), :], *own, beside]
            else:
                above = [
                    tiles[0, c, chunk(136 - rows_below[0]), :],
                    st[c, 0, chunk(BASE + 128 - rows_below[1]), :],
                    st[c, 1, chunk(BASE + 128 - rows_below[2]), :],
                    st[c, 2, chunk(BASE + 128 - rows_below[3]), :],
                ]
                below = [dlc[c], st[c, 0, at, :], st[c, 1, at, :], st[c, 2, at, :]]
                values = [jnp.where(row8 < rows_below[g], above[g], below[g]) for g in range(4)]
                tiles[0, c, chunk(136), :] = values[0]
            c0, c_right = cols_in["up" if k < 0 else "down" if k == 16 else "own"]
            m0 = jnp.where(lane < c0, roll(values[0], c0), values[1])
            m_right = jnp.where(lane < c_right, roll(values[2], c_right), values[3])
            put = chunk(8 * k + 8)
            for g, value in enumerate((m0, values[2], m_right)):
                tiles[g + 1, c, put, :] = value
            if 0 <= k < 16:
                moved[c, chunk(8 * k), pl.ds(0, 128)] = m0
                moved[c, chunk(8 * k), pl.ds(128, 128)] = values[2]

    p0, p1 = pos[0, 0, 0], pos[0, 0, 1]
    group = lax.shift_right_logical(p1 + 126, 7)
    offset = lax.bitwise_and(p1 + 126, 127)
    back = lax.bitwise_and(128 - offset, 127)
    for k in range(10):
        u = []
        for c in range(3):
            at = chunk(p0 + 8 * k)
            a, b = tiles[group, c, at, :], tiles[group + 1, c, at, :]
            u.append(jnp.where(lane < 128 - offset, roll(a, back), roll(b, back)))
            win[c, chunk(8 * k + 8), :] = u[c]
        for c, value in enumerate(speeds(*u)):
            wvel[c, chunk(8 * k + 8), :] = value

    for k in range(10):
        row = 8 * k + 8

        def load(shift, normal):
            at = chunk(row + shift)
            return side([win[c, at, :] for c in range(3)], [wvel[c, at, :] for c in range(3)], normal)

        here = load(0, 1)
        down, up = face(load(-1, 1), here), face(here, load(1, 1))
        across = load(0, 2)
        lower = [roll(x, 1) for x in across[0]]
        left = face(side(lower, speeds(*lower), 2), across)
        right = [roll(x, 127) for x in left]
        for a in range(2):
            near = [[] for _ in range(4)]
            for c in range(3):
                twice = 2.0 * here[1][c]
                tall = up[c] - twice if a else twice - down[c]
                half_way = here[0][c] - HALF * tall
                twice = 2.0 * across[1][c]
                e = half_way - HALF * (twice - left[c])
                o = half_way - HALF * (right[c] - twice)
                ctr[2 * a, c, chunk(row), :] = e
                ctr[2 * a + 1, c, chunk(row), :] = o
                if 1 <= k < 9:
                    inner, outer = o - e, e - roll(o, 1)
                    s_e, s_o = 0.5 * minmod(outer, inner), 0.5 * minmod(inner, roll(outer, 127))
                    for i, x in enumerate((roll(o + s_o, 1), e - s_e, e + s_e, o - s_o)):
                        near[i].append(x)
            if 1 <= k < 9:
                sides = [side(u, speeds(*u), 2) for u in near]
                f_out, f_in = face(sides[0], sides[1]), face(sides[2], sides[3])
                for c in range(3):
                    dcol[2 * a, c, chunk(row), :] = f_in[c] - f_out[c]
                    dcol[2 * a + 1, c, chunk(row), :] = roll(f_out[c], 127) - f_in[c]

    for k in range(10):
        row = 8 * k + 8
        at = chunk(row)
        for b in range(2):
            l_side, r_side = [], []
            for c in range(3):
                c0, c1 = ctr[b, c, at, :], ctr[2 + b, c, at, :]
                inner = c1 - c0
                before = c0 - ctr[2 + b, c, chunk(row - 1), :]
                after = ctr[b, c, chunk(row + 1), :] - c1
                s0, s1 = 0.5 * minmod(before, inner), 0.5 * minmod(inner, after)
                base[b, c, at, :] = c0 - s0
                plus[b, c, at, :] = c1 + s1
                l_side.append(c0 + s0)
                r_side.append(c1 - s1)
            if 1 <= k < 9:
                f = face(side(l_side, speeds(*l_side), 1), side(r_side, speeds(*r_side), 1))
                for c in range(3):
                    mid[b, c, at, :] = f[c]
    for k in range(1, 10):
        row = 8 * k + 8
        for b in range(2):
            l_side = [plus[b, c, chunk(row - 1), :] for c in range(3)]
            r_side = [base[b, c, chunk(row), :] for c in range(3)]
            f = face(side(l_side, speeds(*l_side), 1), side(r_side, speeds(*r_side), 1))
            for c in range(3):
                low[b, c, chunk(row), :] = f[c]
    source = lax.shift_right_logical(lane, 1)
    odd = lax.bitwise_and(lane, 1) == 1
    inside_col = source < ext[0, 0, 1]
    for k in range(1, 9):
        row = 8 * k + 8
        at = chunk(row)
        inside = inside_col & (row8 + 8 * (k - 1) < ext[0, 0, 0])
        for c in range(3):
            done = [[], []]
            for b in range(2):
                f_mid, f_low, f_next = mid[b, c, at, :], low[b, c, at, :], low[b, c, chunk(row + 1), :]
                for a, tall in enumerate((f_mid - f_low, f_next - f_mid)):
                    x = ctr[2 * a + b, c, at, :] - HALF * (tall + dcol[2 * a + b, c, at, :])
                    done[a].append(
                        pick(x, source + 2)
                    )
            for a in range(2):
                x = jnp.where(odd, done[a][1], done[a][0])
                refined[c, pl.ds(16 * (k - 1) + a, 8, stride=2), :] = jnp.where(inside, x, 0.0)


def solution(mesh):
    n_row, n_col = mesh.shape["row"], mesh.shape["col"]
    vmem = pl.BlockSpec(memory_space=pltpu.VMEM)
    smem = pl.BlockSpec(memory_space=pltpu.SMEM)
    hbm = pl.BlockSpec(memory_space=pltpu.HBM)
    buf = lambda *shape: pltpu.VMEM(shape, F32)

    def per_device(state, row_count, col_count, patch_pos, patch_ext):
        in_hbm = [
            x if x.ndim == 2 else pltpu.with_memory_space_constraint(x, pltpu.HBM)
            for x in (state, row_count, col_count, patch_pos, patch_ext)
        ]
        corner = buf(3, 8, 128)
        half = buf(3, 32, 128)
        *parts, _, cnt, pos, ext, err = pl.pallas_call(
            functools.partial(exchange_kernel, n_row, n_col),
            out_shape=(
                buf(3, 3, ROWS, 128), buf(3, 2, 64, 128), half, half, *([corner] * 3),
                pltpu.SMEM((7, 1, 128), jnp.int32),
                pltpu.SMEM((1, 1, 2), jnp.int32),
                pltpu.SMEM((1, 1, 2), jnp.int32),
                buf(64, 128),
            ),
            in_specs=[hbm, smem, smem, hbm, hbm],
            out_specs=(vmem,) * 7 + (smem,) * 3 + (vmem,),
            scratch_shapes=[
                buf(8, 128), buf(8, 128), half, half, pltpu.VMEM((1, 128), jnp.int32),
                buf(8, 128), buf(8, 128), buf(8, 128), half, buf(3, 128, 128), corner,
                *([buf(3, 2, ROWS, 128)] * 4), *([buf(3, 1, 88, 128)] * 3),
                *([buf(3, 1, 48, 128)] * 8),
                pltpu.VMEM((6, 1, 128), jnp.int32),
                pltpu.SemaphoreType.DMA((4,)),
                pltpu.SemaphoreType.DMA((N_MSG,)),
                pltpu.SemaphoreType.DMA((N_MSG,)),
            ],
            compiler_params=pltpu.CompilerParams(
                collective_id=0, has_side_effects=True, vmem_limit_bytes=24 << 20
            ),
        )(*in_hbm)
        return pl.pallas_call(
            patch_kernel,
            out_shape=(
                jax.ShapeDtypeStruct((64, 128), F32),
                jax.ShapeDtypeStruct((3, 128, 256), F32),
                jax.ShapeDtypeStruct((3, 128, 128), F32),
            ),
            in_specs=[smem] * 3 + [vmem] * 7,
            out_specs=(vmem,) * 3,
            scratch_shapes=[
                buf(4, 3, 144, 128), buf(3, 96, 128), buf(3, 96, 128),
                buf(4, 3, 96, 128), buf(4, 3, 96, 128), *([buf(2, 3, 96, 128)] * 4),
            ],
            compiler_params=pltpu.CompilerParams(vmem_limit_bytes=24 << 20),
        )(cnt, pos, ext, *parts, err)

    return jax.shard_map(
        per_device,
        mesh=mesh,
        in_specs=(
            P(None, "row", "col"),
            P("row", "col"),
            P("row", "col"),
            P("row", "col", None),
            P("row", "col", None),
        ),
        out_specs=(P("row", "col"), P(None, "row", "col"), P(None, "row", "col")),
        check_vma=False,
    )
```

```python
import functools

import jax
import jax.numpy as jnp
from jax import lax
from jax.experimental import pallas as pl
from jax.experimental.pallas import tpu as pltpu
from jax.sharding import PartitionSpec as P

MESH = pl.DeviceIdType.MESH
F32 = jnp.float32
HALF = 0.05
BASE = 64
ROWS = 208
N_MSG = 13


def chunk(start, size=8):
    return pl.ds(start, size)


def lanes(shape=(8, 128)):
    return lax.broadcasted_iota(jnp.int32, shape, 1)


def roll(x, by):
    return pltpu.roll(x, by % x.shape[1] if isinstance(by, int) else by, 1)


def speeds(h, m1, m2):
    return m1 / h, m2 / h, jnp.sqrt(h)


def side(u, vel, normal):
    h, m1, m2 = u
    v1, v2, wave = vel
    pressure = 0.5 * h * h
    if normal == 1:
        return u, (m1, m1 * v1 + pressure, m2 * v1), jnp.abs(v1) + wave
    return u, (m2, m1 * v2, m2 * v2 + pressure), jnp.abs(v2) + wave


def face(lower, upper):
    speed = jnp.maximum(lower[2], upper[2])
    return [
        (lower[1][c] + upper[1][c]) - speed * (upper[0][c] - lower[0][c])
        for c in range(3)
    ]


def minmod(a, b):
    chosen = jnp.where(jnp.abs(a) < jnp.abs(b), a, b)
    return jnp.where(a * b > 0, chosen, 0.0)


def from_lower(xs, lane, hop=1):
    rolled = [roll(x, hop) for x in xs]
    if len(xs) == 1:
        return rolled
    return [jnp.where(lane == 0, rolled[g - 1], rolled[g]) for g in range(len(xs))]


def from_upper(xs, lane, hop=1):
    rolled = [roll(x, -hop) for x in xs]
    if len(xs) == 1:
        return rolled
    return [
        jnp.where(lane == 127, rolled[(g + 1) % len(xs)], rolled[g])
        for g in range(len(xs))
    ]


def speed_pass(src, vel, groups, first, last):
    for i in range(first, last):
        at = chunk(8 * i)
        for g in groups:
            for k, value in enumerate(speeds(*(src[c, g, at, :] for c in range(3)))):
                vel[k, g, at, :] = value


def step_pass(src, vel, dst, groups, first, last, hop=1):
    lane = lanes()
    for i in range(first, last):
        row = 8 * i

        def load(shift, g, normal):
            at = chunk(row + shift)
            return side(
                [src[c, g, at, :] for c in range(3)],
                [vel[c, g, at, :] for c in range(3)],
                normal,
            )

        along = [load(0, g, 2) for g in groups]
        shifted = [from_lower([a[0][k] for a in along], lane, hop) for k in range(3)]
        low = []
        for n in range(len(groups)):
            u = [x[n] for x in shifted]
            low.append(face(side(u, speeds(*u), 2), along[n]))
        high = [from_upper([f[c] for f in low], lane, hop) for c in range(3)]
        for n, g in enumerate(groups):
            here = load(0, g, 1)
            down = face(load(-1, g, 1), here)
            up = face(here, load(1, g, 1))
            for c in range(3):
                change = (up[c] - down[c]) + (high[c][n] - low[n][c])
                dst[c, g, chunk(row), :] = here[0][c] - HALF * change


def block_means(src, row, g, c):
    pair = src[c, g, pl.ds(row, 8, stride=2), :] + src[c, g, pl.ds(row + 1, 8, stride=2), :]
    return 0.25 * (pair + roll(pair, 127))


def pick(x, index):
    return jnp.take_along_axis(x, index, axis=1, mode="promise_in_bounds")


def exchange_kernel(
    n_row, n_col, state, row_count, col_count, pos_hbm, ext_hbm,
    st, rm, l_low, l_high, ulc, dl, counts, pos, ext, err,
    rpack, lpack, low_s, high_s, dtile, cnt, lr, rl, url, dr, dn, up_low, ahead, sides,
    vel, rim, fine1, fine2, cgrid, cvel, cone,
    strip, svel, strip1, svel1, strip2, sgrid, sgvel, sone,
    local_sem, send_sem, recv_sem,
):
    me_r, me_c = lax.axis_index("row"), lax.axis_index("col")

    def device(dr, dc):
        return (lax.rem(me_r + (dr + n_row), n_row), lax.rem(me_c + (dc + n_col), n_col))

    loads = [
        pltpu.make_async_copy(
            state.at[:, :, pl.ds(128 * g, 128)], st.at[:, g, pl.ds(BASE, 128), :], local_sem.at[g]
        )
        for g in range(2)
    ]
    loads += [
        pltpu.make_async_copy(pos_hbm, pos, local_sem.at[2]),
        pltpu.make_async_copy(ext_hbm, ext, local_sem.at[3]),
    ]
    for load in loads:
        load.start()
    barrier = pltpu.get_barrier_semaphore()
    around = [(a, b) for a in (-1, 0, 1) for b in (-1, 0, 1) if (a, b) != (0, 0)]
    for a, b in around:
        pl.semaphore_signal(barrier, inc=1, device_id=device(a, b), device_id_type=MESH)

    lane = lanes()
    row8 = lax.broadcasted_iota(jnp.int32, (8, 128), 0)
    rc = row_count[0, 0]
    both_counts = jnp.where(lane == 96, rc, col_count[0, 0]).astype(F32)
    for load in loads:
        load.wait()

    def edge(columns, lane_at):
        tile = None
        for c in range(3):
            for k in range(16):
                to = 32 * c + 2 * k
                x = roll(columns(c, k), to - lane_at)
                tile = x if tile is None else jnp.where(lane >= to, x, tile)
        return jnp.where(lane >= 96, both_counts, tile)

    def fold(low, high):
        return jnp.where(lane < 64, roll(high, 64), low)

    rpack[...] = edge(lambda c, k: st[c, 1, chunk(BASE + 8 * k), :], 126)
    lpack[...] = edge(lambda c, k: st[c, 0, chunk(BASE + 8 * k), :], 0)
    for c in range(3):
        for k in range(4):
            low_s[chunk(32 * c + 8 * k), :] = fold(
                st[c, 1, chunk(BASE + 64 + 8 * k), :], st[c, 1, chunk(BASE + 96 + 8 * k), :]
            )

        dtile[pl.ds(2 * c, 2), :] = st[c, 1, pl.ds(BASE, 2), :]
    low_s[chunk(96), :] = both_counts
    dtile[pl.ds(6, 2), :] = both_counts[:2]

    pl.semaphore_wait(barrier, 8)
    both = pl.ds(0, 2)
    messages = [
        ((1, 0), low_s, up_low),
        ((0, 1), rpack, lr),
        ((0, -1), lpack, rl),
        ((1, 0), st.at[:, both, pl.ds(BASE + 112, 16), :], st.at[:, both, pl.ds(BASE - 16, 16), :]),
        ((-1, 0), st.at[:, both, pl.ds(BASE, 8), :], st.at[:, both, pl.ds(BASE + 128, 8), :]),
        ((1, 1), st.at[:, 1, pl.ds(BASE + 126, 2), :], ulc.at[:, pl.ds(6, 2), :]),
        ((1, -1), lpack, url),
        ((-1, 1), dtile, dl.at[chunk(0), :]),
        ((-1, -1), lpack, dr),
        ((-1, 0), lpack, dn),
        ((0, 1), low_s, l_low),
        ((1, 0), st.at[:, both, pl.ds(BASE + 64, 48), :], st.at[:, both, pl.ds(0, 48), :]),
        ((0, 1), high_s, l_high),
    ]
    copies = [
        pltpu.make_async_remote_copy(
            src_ref=src, dst_ref=dst, send_sem=send_sem.at[i], recv_sem=recv_sem.at[i],
            device_id=device(*to), device_id_type=MESH,
        )
        for i, (to, src, dst) in enumerate(messages)
    ]
    for copy in copies[:12]:
        copy.start()

    for c in range(3):
        tile = None
        for g, from_lane in ((0, 0), (1, 124)):
            for k in range(16):
                to = 64 * g + 4 * k
                x = roll(st[c, g, chunk(BASE + 8 * k), :], to - from_lane)
                tile = x if tile is None else jnp.where(lane >= to, x, tile)
        sides[c] = tile

    even = lax.rem(2 * lane, 128)
    own = (0, 1)
    speed_pass(st, vel, own, 8, 24)
    step_pass(st, vel, fine1, own, 9, 23)

    copies[0].wait_recv()
    for c in range(3):
        for k in range(4):
            x = up_low[chunk(32 * c + 8 * k), :]
            ahead[c, chunk(8 * k), :] = x
            ahead[c, chunk(32 + 8 * k), :] = roll(x, 64)
        for k in range(8):
            ahead[c, chunk(64 + 8 * k), :] = st[c, 1, chunk(BASE + 8 * k), :]
    for c in range(3):
        top = [
            jnp.where(
                row8 + 8 * k < rc,
                ahead[c, chunk(64 + 8 * k - rc), :],
                ahead[c, chunk(64 + 8 * k), :],
            )
            for k in range(8)
        ]
        for k in range(4):
            high_s[c, chunk(8 * k), :] = fold(top[k], top[k + 4])
    copies[12].start()

    def coarse_own(i):
        for c in range(3):
            halves = [pick(block_means(st, BASE - 16 + 16 * i, g, c), even) for g in range(2)]
            cgrid[c, 0, chunk(8 * i), :] = jnp.where(lane < 64, *halves)
        speed_pass(cgrid, cvel, (0,), i, i + 1)

    def estimate(i):
        total = None
        for c in range(3):
            halves = [pick(block_means(fine2, BASE + 16 * i, g, c), even) for g in range(2)]
            gap = jnp.abs(jnp.where(lane < 64, *halves) - cone[c, 0, chunk(8 * i + 8), :])
            total = gap if total is None else total + gap
        err[chunk(8 * i), :] = 10.0 * total

    speed_pass(fine1, vel, own, 9, 23)
    step_pass(fine1, vel, fine2, own, 10, 22)
    for i in range(1, 9):
        coarse_own(i)
    step_pass(cgrid, cvel, cone, (0,), 2, 8)
    for i in range(1, 7):
        estimate(i)

    for copy in copies[1:9]:
        copy.wait_recv()
    speed_pass(st, rim, own, 7, 10)
    speed_pass(st, rim, own, 22, 25)
    step_pass(st, rim, fine1, own, 7, 9)
    step_pass(st, rim, fine1, own, 23, 25)
    speed_pass(fine1, rim, own, 7, 11)
    speed_pass(fine1, rim, own, 21, 25)
    step_pass(fine1, rim, fine2, own, 8, 10)
    step_pass(fine1, rim, fine2, own, 22, 24)
    coarse_own(0)
    coarse_own(9)
    step_pass(cgrid, cvel, cone, (0,), 1, 2)
    step_pass(cgrid, cvel, cone, (0,), 8, 9)
    estimate(0)
    estimate(7)

    left, right, corner, lower_right = lr[...], rl[...], url[...], dr[...]
    part, place = lax.shift_right_logical(lane, 4), lax.bitwise_and(lane, 15)

    def folded(a, b, c, d):
        return jnp.where(place < 2, a, jnp.where(place < 8, b, jnp.where(place < 12, c, d)))

    for j in range(4):
        block = 2 * part + (j - 1)
        own_at = lax.bitwise_and(4 * block + jnp.where(place < 8, place - 2, place + 56), 127)
        for c in range(3):
            at = lax.bitwise_and(32 * c + 2 * block + lax.bitwise_and(place, 1), 127)
            own_cells = pick(sides[c], own_at)
            x = folded(pick(left, at), own_cells, own_cells, pick(right, at))
            if j == 0:
                rows = chunk(BASE - 8)
                above = folded(
                    roll(ulc[c], 2), roll(st[c, 0, rows, :], 2),
                    roll(st[c, 1, rows, :], 12), roll(corner, -18 - 32 * c),
                )
                x = jnp.where(part == 0, above, x)
            if j == 3:
                rows = chunk(BASE + 128)
                below = folded(
                    roll(dl[chunk(2 * c), :], -14), roll(st[c, 0, rows, :], 114),
                    roll(st[c, 1, rows, :], -4), roll(lower_right, 124 - 32 * c),
                )
                x = jnp.where(part == 7, below, x)
            strip[c, 0, chunk(8 + 8 * j), :] = x
    one = (0,)
    speed_pass(strip, svel, one, 1, 5)
    step_pass(strip, svel, strip1, one, 1, 5)
    speed_pass(strip1, svel1, one, 1, 5)
    step_pass(strip1, svel1, strip2, one, 2, 4)
    for i in range(3):
        for c in range(3):
            sgrid[c, 0, chunk(8 * i), :] = block_means(strip, 16 * i, 0, c)
    speed_pass(sgrid, sgvel, one, 0, 3)
    step_pass(sgrid, sgvel, sone, one, 1, 2, 2)
    total = None
    for c in range(3):
        gap = jnp.abs(block_means(strip2, 16, 0, c) - sone[c, 0, chunk(8), :])
        total = gap if total is None else total + gap
    total = 10.0 * total
    for i in range(8):
        at = chunk(8 * i)
        value = jnp.where(lane == 127, roll(total, 117 - 16 * i), err[at, :])
        err[at, :] = jnp.where(lane == 0, roll(total, -(16 * i + 2)), value)

    for c in range(3):
        for k in range(-8, 17):
            col = 32 * c + 2 * k
            if k < 0:
                x = roll(corner, -(col + 32))
            else:
                x = roll(lower_right, -32 * c) if k == 16 else roll(right, -col)
            st[c, 2, chunk(BASE + 8 * k), :] = x

    for copy in copies[9:12]:
        copy.wait_recv()
    for c in range(3):
        for g in range(2):
            for k in range(8):
                here = st[c, g, chunk(BASE + 8 * k), :]
                above = st[c, g, chunk(BASE + 8 * k - rc), :]
                rm[c, g, chunk(8 * k), :] = jnp.where(row8 + 8 * k < rc, above, here)
    given = (rl[:1], up_low[pl.ds(96, 1)], dn[:1], url[:1], dl[pl.ds(6, 1)], dr[:1], lpack[:1])
    for i, x in enumerate(given):
        cnt[pl.ds(i, 1), :] = x
    keep = pltpu.make_async_copy(cnt, counts, local_sem.at[0])
    keep.start()
    copies[12].wait_recv()
    for copy in copies:
        copy.wait_send()
    keep.wait()


def patch_kernel(
    cnt, pos, ext, st, rm, l_low, l_high, ulc, dl, err_in,
    err, moved, refined,
    tiles, win, wvel, ctr, dcol, plus, base, mid, low,
):
    lane = lanes()
    row8 = lax.broadcasted_iota(jnp.int32, (8, 128), 0)
    err[...] = err_in[...]
    rc_of = lambda i: cnt[i, 96].astype(jnp.int32)
    cc_of = lambda i: cnt[i, 97].astype(jnp.int32)
    rows_below = (rc_of(4), rc_of(2), rc_of(2), rc_of(5))
    cols_in = {"up": (cc_of(1), cc_of(3)), "own": (cc_of(6), cc_of(0)), "down": (cc_of(2), cc_of(5))}

    rc_right = rc_of(0)
    for c in range(3):
        for k in range(4):
            for start, x in ((0, l_high[c, chunk(8 * k), :]), (64, l_low[chunk(32 * c + 8 * k), :])):
                tiles[0, c, chunk(8 + start + 8 * k), :] = x
                tiles[0, c, chunk(40 + start + 8 * k), :] = roll(x, 64)
        tiles[0, c, chunk(0), :] = ulc[c]

    for c in range(3):
        for k in range(-1, 17):
            at = chunk(BASE + 8 * k)
            if k < 0:
                values = [ulc[c], st[c, 0, at, :], st[c, 1, at, :], st[c, 2, at, :]]
            elif k < 16:
                own = [rm[c, g, chunk(8 * k), :] if k < 8 else st[c, g, at, :] for g in range(2)]
                beside = st[c, 2, at, :]
                if k < 8:
                    above = st[c, 2, chunk(BASE + 8 * k - rc_right), :]
                    beside = jnp.where(row8 + 8 * k < rc_right, above, beside)
                values = [tiles[0, c, chunk(8 * k + 8), :], *own, beside]
            else:
                above = [
                    tiles[0, c, chunk(136 - rows_below[0]), :],
                    st[c, 0, chunk(BASE + 128 - rows_below[1]), :],
                    st[c, 1, chunk(BASE + 128 - rows_below[2]), :],
                    st[c, 2, chunk(BASE + 128 - rows_below[3]), :],
                ]
                below = [dl[chunk(2 * c), :], st[c, 0, at, :], st[c, 1, at, :], st[c, 2, at, :]]
                values = [jnp.where(row8 < rows_below[g], above[g], below[g]) for g in range(4)]
                tiles[0, c, chunk(136), :] = values[0]
            c0, c_right = cols_in["up" if k < 0 else "down" if k == 16 else "own"]
            m0 = jnp.where(lane < c0, roll(values[0], c0), values[1])
            m_right = jnp.where(lane < c_right, roll(values[2], c_right), values[3])
            put = chunk(8 * k + 8)
            for g, value in enumerate((m0, values[2], m_right)):
                tiles[g + 1, c, put, :] = value
            if 0 <= k < 16:
                moved[c, chunk(8 * k), pl.ds(0, 128)] = m0
                moved[c, chunk(8 * k), pl.ds(128, 128)] = values[2]

    p0, p1 = pos[0, 0, 0], pos[0, 0, 1]
    group = lax.shift_right_logical(p1 + 126, 7)
    offset = lax.bitwise_and(p1 + 126, 127)
    back = lax.bitwise_and(128 - offset, 127)
    for k in range(10):
        u = []
        for c in range(3):
            at = chunk(p0 + 8 * k)
            a, b = tiles[group, c, at, :], tiles[group + 1, c, at, :]
            u.append(jnp.where(lane < 128 - offset, roll(a, back), roll(b, back)))
            win[c, chunk(8 * k + 8), :] = u[c]
        for c, value in enumerate(speeds(*u)):
            wvel[c, chunk(8 * k + 8), :] = value

    for k in range(10):
        row = 8 * k + 8

        def load(shift, normal):
            at = chunk(row + shift)
            return side([win[c, at, :] for c in range(3)], [wvel[c, at, :] for c in range(3)], normal)

        here = load(0, 1)
        down, up = face(load(-1, 1), here), face(here, load(1, 1))
        across = load(0, 2)
        lower = [roll(x, 1) for x in across[0]]
        left = face(side(lower, speeds(*lower), 2), across)
        right = [roll(x, 127) for x in left]
        for a in range(2):
            near = [[] for _ in range(4)]
            for c in range(3):
                twice = 2.0 * here[1][c]
                tall = up[c] - twice if a else twice - down[c]
                half_way = here[0][c] - HALF * tall
                twice = 2.0 * across[1][c]
                e = half_way - HALF * (twice - left[c])
                o = half_way - HALF * (right[c] - twice)
                ctr[2 * a, c, chunk(row), :] = e
                ctr[2 * a + 1, c, chunk(row), :] = o
                if 1 <= k < 9:
                    inner, outer = o - e, e - roll(o, 1)
                    s_e, s_o = 0.5 * minmod(outer, inner), 0.5 * minmod(inner, roll(outer, 127))
                    for i, x in enumerate((roll(o + s_o, 1), e - s_e, e + s_e, o - s_o)):
                        near[i].append(x)
            if 1 <= k < 9:
                sides = [side(u, speeds(*u), 2) for u in near]
                f_out, f_in = face(sides[0], sides[1]), face(sides[2], sides[3])
                for c in range(3):
                    dcol[2 * a, c, chunk(row), :] = f_in[c] - f_out[c]
                    dcol[2 * a + 1, c, chunk(row), :] = roll(f_out[c], 127) - f_in[c]

    for k in range(10):
        row = 8 * k + 8
        at = chunk(row)
        for b in range(2):
            l_side, r_side = [], []
            for c in range(3):
                c0, c1 = ctr[b, c, at, :], ctr[2 + b, c, at, :]
                inner = c1 - c0
                before = c0 - ctr[2 + b, c, chunk(row - 1), :]
                after = ctr[b, c, chunk(row + 1), :] - c1
                s0, s1 = 0.5 * minmod(before, inner), 0.5 * minmod(inner, after)
                base[b, c, at, :] = c0 - s0
                plus[b, c, at, :] = c1 + s1
                l_side.append(c0 + s0)
                r_side.append(c1 - s1)
            if 1 <= k < 9:
                f = face(side(l_side, speeds(*l_side), 1), side(r_side, speeds(*r_side), 1))
                for c in range(3):
                    mid[b, c, at, :] = f[c]
    for k in range(1, 10):
        row = 8 * k + 8
        for b in range(2):
            l_side = [plus[b, c, chunk(row - 1), :] for c in range(3)]
            r_side = [base[b, c, chunk(row), :] for c in range(3)]
            f = face(side(l_side, speeds(*l_side), 1), side(r_side, speeds(*r_side), 1))
            for c in range(3):
                low[b, c, chunk(row), :] = f[c]
    source = lax.shift_right_logical(lane, 1)
    odd = lax.bitwise_and(lane, 1) == 1
    inside_col = source < ext[0, 0, 1]
    for k in range(1, 9):
        row = 8 * k + 8
        at = chunk(row)
        inside = inside_col & (row8 + 8 * (k - 1) < ext[0, 0, 0])
        for c in range(3):
            done = [[], []]
            for b in range(2):
                f_mid, f_low, f_next = mid[b, c, at, :], low[b, c, at, :], low[b, c, chunk(row + 1), :]
                for a, tall in enumerate((f_mid - f_low, f_next - f_mid)):
                    x = ctr[2 * a + b, c, at, :] - HALF * (tall + dcol[2 * a + b, c, at, :])
                    done[a].append(
                        pick(x, source + 2)
                    )
            for a in range(2):
                x = jnp.where(odd, done[a][1], done[a][0])
                refined[c, pl.ds(16 * (k - 1) + a, 8, stride=2), :] = jnp.where(inside, x, 0.0)


def solution(mesh):
    n_row, n_col = mesh.shape["row"], mesh.shape["col"]
    vmem = pl.BlockSpec(memory_space=pltpu.VMEM)
    smem = pl.BlockSpec(memory_space=pltpu.SMEM)
    hbm = pl.BlockSpec(memory_space=pltpu.HBM)
    buf = lambda *shape: pltpu.VMEM(shape, F32)

    def per_device(state, row_count, col_count, patch_pos, patch_ext):
        in_hbm = [
            x if x.ndim == 2 else pltpu.with_memory_space_constraint(x, pltpu.HBM)
            for x in (state, row_count, col_count, patch_pos, patch_ext)
        ]
        corner = buf(3, 8, 128)
        half = buf(3, 32, 128)
        *parts, cnt, pos, ext, err = pl.pallas_call(
            functools.partial(exchange_kernel, n_row, n_col),
            out_shape=(
                buf(3, 3, ROWS, 128), buf(3, 2, 64, 128), buf(104, 128), half, corner, buf(16, 128),
                pltpu.SMEM((8, 128), F32),
                pltpu.SMEM((1, 1, 2), jnp.int32),
                pltpu.SMEM((1, 1, 2), jnp.int32),
                buf(64, 128),
            ),
            in_specs=[hbm, smem, smem, hbm, hbm],
            out_specs=(vmem,) * 6 + (smem,) * 3 + (vmem,),
            scratch_shapes=[
                buf(8, 128), buf(8, 128), buf(104, 128), half, *([buf(8, 128)] * 7),
                buf(104, 128), buf(3, 128, 128), corner,
                *([buf(3, 2, ROWS, 128)] * 4), *([buf(3, 1, 88, 128)] * 3),
                *([buf(3, 1, 48, 128)] * 8),
                pltpu.SemaphoreType.DMA((4,)),
                pltpu.SemaphoreType.DMA((N_MSG,)),
                pltpu.SemaphoreType.DMA((N_MSG,)),
            ],
            compiler_params=pltpu.CompilerParams(
                collective_id=0, has_side_effects=True, vmem_limit_bytes=24 << 20
            ),
        )(*in_hbm)
        return pl.pallas_call(
            patch_kernel,
            out_shape=(
                jax.ShapeDtypeStruct((64, 128), F32),
                jax.ShapeDtypeStruct((3, 128, 256), F32),
                jax.ShapeDtypeStruct((3, 128, 128), F32),
            ),
            in_specs=[smem] * 3 + [vmem] * 7,
            out_specs=(vmem,) * 3,
            scratch_shapes=[
                buf(4, 3, 144, 128), buf(3, 96, 128), buf(3, 96, 128),
                buf(4, 3, 96, 128), buf(4, 3, 96, 128), *([buf(2, 3, 96, 128)] * 4),
            ],
            compiler_params=pltpu.CompilerParams(vmem_limit_bytes=24 << 20),
        )(cnt, pos, ext, *parts, err)

    return jax.shard_map(
        per_device,
        mesh=mesh,
        in_specs=(
            P(None, "row", "col"),
            P("row", "col"),
            P("row", "col"),
            P("row", "col", None),
            P("row", "col", None),
        ),
        out_specs=(P("row", "col"), P(None, "row", "col"), P(None, "row", "col")),
        check_vma=False,
    )
```

```python
import functools

import jax
import jax.numpy as jnp
from jax import lax
from jax.experimental import pallas as pl
from jax.experimental.pallas import tpu as pltpu
from jax.sharding import PartitionSpec as P

MESH = pl.DeviceIdType.MESH
F32 = jnp.float32
HALF = 0.05
BASE = 80
ROWS = 224
N_MSG = 11


def chunk(start, size=8):
    return pl.ds(start, size)


def lanes(shape=(8, 128)):
    return lax.broadcasted_iota(jnp.int32, shape, 1)


def roll(x, by):
    return pltpu.roll(x, by % x.shape[1] if isinstance(by, int) else by, 1)


def speeds(h, m1, m2):
    return m1 / h, m2 / h, jnp.sqrt(h)


def side(u, vel, normal):
    h, m1, m2 = u
    v1, v2, wave = vel
    pressure = 0.5 * h * h
    if normal == 1:
        return u, (m1, m1 * v1 + pressure, m2 * v1), jnp.abs(v1) + wave
    return u, (m2, m1 * v2, m2 * v2 + pressure), jnp.abs(v2) + wave


def face(lower, upper):
    speed = jnp.maximum(lower[2], upper[2])
    return [
        (lower[1][c] + upper[1][c]) - speed * (upper[0][c] - lower[0][c])
        for c in range(3)
    ]


def minmod(a, b):
    chosen = jnp.where(jnp.abs(a) < jnp.abs(b), a, b)
    return jnp.where(a * b > 0, chosen, 0.0)


def from_lower(xs, lane, hop=1):
    rolled = [roll(x, hop) for x in xs]
    if len(xs) == 1:
        return rolled
    return [jnp.where(lane == 0, rolled[g - 1], rolled[g]) for g in range(len(xs))]


def from_upper(xs, lane, hop=1):
    rolled = [roll(x, -hop) for x in xs]
    if len(xs) == 1:
        return rolled
    return [
        jnp.where(lane == 127, rolled[(g + 1) % len(xs)], rolled[g])
        for g in range(len(xs))
    ]


def speed_pass(src, vel, groups, first, last):
    for i in range(first, last):
        at = chunk(8 * i)
        for g in groups:
            for k, value in enumerate(speeds(*(src[c, g, at, :] for c in range(3)))):
                vel[k, g, at, :] = value


def step_pass(src, vel, dst, groups, first, last, hop=1):
    lane = lanes()
    for i in range(first, last):
        row = 8 * i

        def load(shift, g, normal):
            at = chunk(row + shift)
            return side(
                [src[c, g, at, :] for c in range(3)],
                [vel[c, g, at, :] for c in range(3)],
                normal,
            )

        along = [load(0, g, 2) for g in groups]
        shifted = [from_lower([a[0][k] for a in along], lane, hop) for k in range(3)]
        low = []
        for n in range(len(groups)):
            u = [x[n] for x in shifted]
            low.append(face(side(u, speeds(*u), 2), along[n]))
        high = [from_upper([f[c] for f in low], lane, hop) for c in range(3)]
        for n, g in enumerate(groups):
            here = load(0, g, 1)
            down = face(load(-1, g, 1), here)
            up = face(here, load(1, g, 1))
            for c in range(3):
                change = (up[c] - down[c]) + (high[c][n] - low[n][c])
                dst[c, g, chunk(row), :] = here[0][c] - HALF * change


def block_means(src, row, g, c, n=8):
    pair = src[c, g, pl.ds(row, n, stride=2), :] + src[c, g, pl.ds(row + 1, n, stride=2), :]
    return 0.25 * (pair + roll(pair, 127))


def pick(x, index):
    return jnp.take_along_axis(x, index, axis=1, mode="promise_in_bounds")


def exchange_kernel(
    n_row, n_col, state, row_count, col_count, pos_hbm, ext_hbm,
    st, rm, l_low, l_high, ul, dl, counts, pos, ext, err,
    lpack, low_s, high_s, utile, cnt, rl, url, dr, dn, up_low, ahead, sides,
    vel, rim, fine1, fine2, cgrid, cvel, cone,
    strip, svel, strip1, svel1, strip2, sgrid, sgvel, sone,
    local_sem, send_sem, recv_sem,
):
    me_r, me_c = lax.axis_index("row"), lax.axis_index("col")

    def device(dr, dc):
        return (lax.rem(me_r + (dr + n_row), n_row), lax.rem(me_c + (dc + n_col), n_col))

    loads = [
        pltpu.make_async_copy(
            state.at[:, :, pl.ds(128 * g, 128)], st.at[:, g, pl.ds(BASE, 128), :], local_sem.at[g]
        )
        for g in range(2)
    ]
    loads += [
        pltpu.make_async_copy(pos_hbm, pos, local_sem.at[2]),
        pltpu.make_async_copy(ext_hbm, ext, local_sem.at[3]),
    ]
    for load in loads:
        load.start()
    barrier = pltpu.get_barrier_semaphore()
    around = [(a, b) for a in (-1, 0, 1) for b in (-1, 0, 1) if (a, b) != (0, 0)]
    for a, b in around:
        pl.semaphore_signal(barrier, inc=1, device_id=device(a, b), device_id_type=MESH)

    lane = lanes()
    row8 = lax.broadcasted_iota(jnp.int32, (8, 128), 0)
    rc = row_count[0, 0]
    both_counts = jnp.where(lane == 96, rc, col_count[0, 0]).astype(F32)
    for load in loads:
        load.wait()

    def edge(columns, lane_at):
        tile = None
        for c in range(3):
            for k in range(16):
                to = 32 * c + 2 * k
                x = roll(columns(c, k), to - lane_at)
                tile = x if tile is None else jnp.where(lane >= to, x, tile)
        return jnp.where(lane >= 96, both_counts, tile)

    def fold(low, high):
        return jnp.where(lane < 64, roll(high, 64), low)

    low_s[chunk(104), :] = edge(lambda c, k: st[c, 1, chunk(BASE + 8 * k), :], 126)
    lpack[...] = edge(lambda c, k: st[c, 0, chunk(BASE + 8 * k), :], 0)
    for c in range(3):
        for k in range(4):
            low_s[chunk(32 * c + 8 * k), :] = fold(
                st[c, 1, chunk(BASE + 64 + 8 * k), :], st[c, 1, chunk(BASE + 96 + 8 * k), :]
            )

        for g in range(2):
            utile[pl.ds(4 * c + 2 * g, 2), :] = st[c, g, pl.ds(BASE, 2), :]
            low_s[pl.ds(112 + 4 * c + 2 * g, 2), :] = st[c, g, pl.ds(BASE + 126, 2), :]
    low_s[chunk(96), :] = both_counts
    low_s[pl.ds(124, 4), :] = both_counts[:4]
    utile[pl.ds(12, 4), :] = both_counts[:4]

    pl.semaphore_wait(barrier, 8)
    both = pl.ds(0, 2)
    messages = [
        ((1, 0), low_s, up_low),
        ((0, 1), low_s.at[pl.ds(104, 8), :], l_low.at[pl.ds(104, 8), :]),
        ((0, -1), lpack, rl),
        ((-1, 0), utile, dn),
        ((1, 1), low_s.at[pl.ds(112, 16), :], ul.at[pl.ds(8, 16), :]),
        ((1, -1), lpack, url),
        ((-1, 1), utile, dl.at[pl.ds(0, 16), :]),
        ((-1, -1), lpack, dr),
        ((0, 1), low_s.at[pl.ds(0, 104), :], l_low.at[pl.ds(0, 104), :]),
        ((1, 0), st.at[:, both, pl.ds(BASE + 64, 64), :], st.at[:, both, pl.ds(0, 64), :]),
        ((0, 1), high_s, l_high),
    ]
    copies = [
        pltpu.make_async_remote_copy(
            src_ref=src, dst_ref=dst, send_sem=send_sem.at[i], recv_sem=recv_sem.at[i],
            device_id=device(*to), device_id_type=MESH,
        )
        for i, (to, src, dst) in enumerate(messages)
    ]
    for copy in copies[:9]:
        copy.start()

    for c in range(3):
        tile = None
        for g, from_lane in ((0, 0), (1, 124)):
            for k in range(16):
                to = 64 * g + 4 * k
                x = roll(st[c, g, chunk(BASE + 8 * k), :], to - from_lane)
                tile = x if tile is None else jnp.where(lane >= to, x, tile)
        sides[c] = tile

    even = lax.rem(2 * lane, 128)
    own = (0, 1)
    speed_pass(st, vel, own, 10, 26)
    step_pass(st, vel, fine1, own, 11, 25)

    copies[0].wait_recv()
    for c in range(3):
        for k in range(4):
            x = up_low[chunk(32 * c + 8 * k), :]
            ahead[c, chunk(8 * k), :] = x
            ahead[c, chunk(32 + 8 * k), :] = roll(x, 64)
        for k in range(8):
            ahead[c, chunk(64 + 8 * k), :] = st[c, 1, chunk(BASE + 8 * k), :]
    for c in range(3):
        top = [
            jnp.where(
                row8 + 8 * k < rc,
                ahead[c, chunk(64 + 8 * k - rc), :],
                ahead[c, chunk(64 + 8 * k), :],
            )
            for k in range(8)
        ]
        for k in range(4):
            high_s[c, chunk(8 * k), :] = fold(top[k], top[k + 4])
    copies[10].start()
    copies[9].start()

    def coarse_own(i):
        n = 8 if i else 4
        for c in range(3):
            row = BASE - 2 * n + 16 * i
            halves = [pick(block_means(st, row, g, c, n), even[:n]) for g in range(2)]
            cgrid[c, 0, pl.ds(8 * i + 8 - n, n), :] = jnp.where(lane[:n] < 64, *halves)
        speed_pass(cgrid, cvel, (0,), i, i + 1)

    def estimate(i):
        total = None
        for c in range(3):
            halves = [pick(block_means(fine2, BASE + 16 * i, g, c), even) for g in range(2)]
            gap = jnp.abs(jnp.where(lane < 64, *halves) - cone[c, 0, chunk(8 * i + 8), :])
            total = gap if total is None else total + gap
        err[chunk(8 * i), :] = 10.0 * total

    speed_pass(fine1, vel, own, 11, 25)
    step_pass(fine1, vel, fine2, own, 12, 24)
    for i in range(1, 9):
        coarse_own(i)
    step_pass(cgrid, cvel, cone, (0,), 2, 8)
    for i in range(1, 7):
        estimate(i)

    for copy in copies[1:8]:
        copy.wait_recv()
    for c in range(3):
        for g in range(2):
            st[c, g, pl.ds(BASE - 2, 2), :] = up_low[pl.ds(112 + 4 * c + 2 * g, 2), :]
            st[c, g, pl.ds(BASE + 128, 2), :] = dn[pl.ds(4 * c + 2 * g, 2), :]
    speed_pass(st, rim, own, 9, 12)
    speed_pass(st, rim, own, 24, 27)
    step_pass(st, rim, fine1, own, 9, 11)
    step_pass(st, rim, fine1, own, 25, 27)
    speed_pass(fine1, rim, own, 9, 13)
    speed_pass(fine1, rim, own, 23, 27)
    step_pass(fine1, rim, fine2, own, 10, 12)
    step_pass(fine1, rim, fine2, own, 24, 26)
    coarse_own(0)
    coarse_own(9)
    step_pass(cgrid, cvel, cone, (0,), 1, 2)
    step_pass(cgrid, cvel, cone, (0,), 8, 9)
    estimate(0)
    estimate(7)

    left, right, corner, lower_right = l_low[chunk(104), :], rl[...], url[...], dr[...]
    part, place = lax.shift_right_logical(lane, 4), lax.bitwise_and(lane, 15)

    def folded(a, b, c, d):
        return jnp.where(place < 2, a, jnp.where(place < 8, b, jnp.where(place < 12, c, d)))

    for j in range(4):
        block = 2 * part + (j - 1)
        own_at = lax.bitwise_and(4 * block + jnp.where(place < 8, place - 2, place + 56), 127)
        for c in range(3):
            at = lax.bitwise_and(32 * c + 2 * block + lax.bitwise_and(place, 1), 127)
            own_cells = pick(sides[c], own_at)
            x = folded(pick(left, at), own_cells, own_cells, pick(right, at))
            if j == 0:
                rows = chunk(BASE - 8)
                above = folded(
                    roll(ul[chunk(4 + 4 * c), :], 2), roll(st[c, 0, rows, :], 2),
                    roll(st[c, 1, rows, :], 12), roll(corner, -18 - 32 * c),
                )
                x = jnp.where(part == 0, above, x)
            if j == 3:
                rows = chunk(BASE + 128)
                below = folded(
                    roll(dl[chunk(2 + 4 * c), :], -14), roll(st[c, 0, rows, :], 114),
                    roll(st[c, 1, rows, :], -4), roll(lower_right, 124 - 32 * c),
                )
                x = jnp.where(part == 7, below, x)
            strip[c, 0, chunk(8 + 8 * j), :] = x
    one = (0,)
    speed_pass(strip, svel, one, 1, 5)
    step_pass(strip, svel, strip1, one, 1, 5)
    speed_pass(strip1, svel1, one, 1, 5)
    step_pass(strip1, svel1, strip2, one, 2, 4)
    for i in range(3):
        for c in range(3):
            sgrid[c, 0, chunk(8 * i), :] = block_means(strip, 16 * i, 0, c)
    speed_pass(sgrid, sgvel, one, 0, 3)
    step_pass(sgrid, sgvel, sone, one, 1, 2, 2)
    total = None
    for c in range(3):
        gap = jnp.abs(block_means(strip2, 16, 0, c) - sone[c, 0, chunk(8), :])
        total = gap if total is None else total + gap
    total = 10.0 * total
    for i in range(8):
        at = chunk(8 * i)
        value = jnp.where(lane == 127, roll(total, 117 - 16 * i), err[at, :])
        err[at, :] = jnp.where(lane == 0, roll(total, -(16 * i + 2)), value)

    for c in range(3):
        for k in range(-8, 17):
            col = 32 * c + 2 * k
            if k < 0:
                x = roll(corner, -(col + 32))
            else:
                x = roll(lower_right, -32 * c) if k == 16 else roll(right, -col)
            st[c, 2, chunk(BASE + 8 * k), :] = x

    for copy in copies[8:10]:
        copy.wait_recv()
    for c in range(3):
        for g in range(2):
            for k in range(8):
                here = st[c, g, chunk(BASE + 8 * k), :]
                above = st[c, g, chunk(64 + 8 * k - rc), :]
                rm[c, g, chunk(8 * k), :] = jnp.where(row8 + 8 * k < rc, above, here)
    given = (rl[:1], up_low[pl.ds(96, 1)], dn[pl.ds(12, 1)], url[:1], dl[pl.ds(12, 1)], dr[:1], lpack[:1])
    for i, x in enumerate(given):
        cnt[pl.ds(i, 1), :] = x
    keep = pltpu.make_async_copy(cnt, counts, local_sem.at[0])
    keep.start()
    copies[10].wait_recv()
    for copy in copies:
        copy.wait_send()
    keep.wait()


def patch_kernel(
    cnt, pos, ext, st, rm, l_low, l_high, ul, dl, err_in,
    err, moved, refined,
    tiles, win, wvel, ctr, dcol, plus, base, mid, low,
):
    lane = lanes()
    row8 = lax.broadcasted_iota(jnp.int32, (8, 128), 0)
    err[...] = err_in[...]
    rc_of = lambda i: cnt[i, 96].astype(jnp.int32)
    cc_of = lambda i: cnt[i, 97].astype(jnp.int32)
    rows_below = (rc_of(4), rc_of(2), rc_of(2), rc_of(5))
    cols_in = {"up": (cc_of(1), cc_of(3)), "own": (cc_of(6), cc_of(0)), "down": (cc_of(2), cc_of(5))}

    rc_right = rc_of(0)
    for c in range(3):
        for k in range(4):
            for start, x in ((0, l_high[c, chunk(8 * k), :]), (64, l_low[chunk(32 * c + 8 * k), :])):
                tiles[0, c, chunk(8 + start + 8 * k), :] = x
                tiles[0, c, chunk(40 + start + 8 * k), :] = roll(x, 64)
        tiles[0, c, chunk(0), :] = ul[chunk(4 + 4 * c), :]

    for c in range(3):
        for k in range(-1, 17):
            at = chunk(BASE + 8 * k)
            if k < 0:
                values = [ul[chunk(4 + 4 * c), :], st[c, 0, at, :], st[c, 1, at, :], st[c, 2, at, :]]
            elif k < 16:
                own = [rm[c, g, chunk(8 * k), :] if k < 8 else st[c, g, at, :] for g in range(2)]
                beside = st[c, 2, at, :]
                if k < 8:
                    above = st[c, 2, chunk(BASE + 8 * k - rc_right), :]
                    beside = jnp.where(row8 + 8 * k < rc_right, above, beside)
                values = [tiles[0, c, chunk(8 * k + 8), :], *own, beside]
            else:
                above = [
                    tiles[0, c, chunk(136 - rows_below[0]), :],
                    st[c, 0, chunk(BASE + 128 - rows_below[1]), :],
                    st[c, 1, chunk(BASE + 128 - rows_below[2]), :],
                    st[c, 2, chunk(BASE + 128 - rows_below[3]), :],
                ]
                below = [dl[chunk(2 + 4 * c), :], st[c, 0, at, :], st[c, 1, at, :], st[c, 2, at, :]]
                values = [jnp.where(row8 < rows_below[g], above[g], below[g]) for g in range(4)]
                tiles[0, c, chunk(136), :] = values[0]
            c0, c_right = cols_in["up" if k < 0 else "down" if k == 16 else "own"]
            m0 = jnp.where(lane < c0, roll(values[0], c0), values[1])
            m_right = jnp.where(lane < c_right, roll(values[2], c_right), values[3])
            put = chunk(8 * k + 8)
            for g, value in enumerate((m0, values[2], m_right)):
                tiles[g + 1, c, put, :] = value
            if 0 <= k < 16:
                moved[c, chunk(8 * k), pl.ds(0, 128)] = m0
                moved[c, chunk(8 * k), pl.ds(128, 128)] = values[2]

    p0, p1 = pos[0, 0, 0], pos[0, 0, 1]
    group = lax.shift_right_logical(p1 + 126, 7)
    offset = lax.bitwise_and(p1 + 126, 127)
    back = lax.bitwise_and(128 - offset, 127)
    for k in range(10):
        u = []
        for c in range(3):
            at = chunk(p0 + 8 * k)
            a, b = tiles[group, c, at, :], tiles[group + 1, c, at, :]
            u.append(jnp.where(lane < 128 - offset, roll(a, back), roll(b, back)))
            win[c, chunk(8 * k + 8), :] = u[c]
        for c, value in enumerate(speeds(*u)):
            wvel[c, chunk(8 * k + 8), :] = value

    for k in range(10):
        row = 8 * k + 8

        def load(shift, normal):
            at = chunk(row + shift)
            return side([win[c, at, :] for c in range(3)], [wvel[c, at, :] for c in range(3)], normal)

        here = load(0, 1)
        down, up = face(load(-1, 1), here), face(here, load(1, 1))
        across = load(0, 2)
        lower = [roll(x, 1) for x in across[0]]
        left = face(side(lower, speeds(*lower), 2), across)
        right = [roll(x, 127) for x in left]
        for a in range(2):
            near = [[] for _ in range(4)]
            for c in range(3):
                twice = 2.0 * here[1][c]
                tall = up[c] - twice if a else twice - down[c]
                half_way = here[0][c] - HALF * tall
                twice = 2.0 * across[1][c]
                e = half_way - HALF * (twice - left[c])
                o = half_way - HALF * (right[c] - twice)
                ctr[2 * a, c, chunk(row), :] = e
                ctr[2 * a + 1, c, chunk(row), :] = o
                if 1 <= k < 9:
                    inner, outer = o - e, e - roll(o, 1)
                    s_e, s_o = 0.5 * minmod(outer, inner), 0.5 * minmod(inner, roll(outer, 127))
                    for i, x in enumerate((roll(o + s_o, 1), e - s_e, e + s_e, o - s_o)):
                        near[i].append(x)
            if 1 <= k < 9:
                sides = [side(u, speeds(*u), 2) for u in near]
                f_out, f_in = face(sides[0], sides[1]), face(sides[2], sides[3])
                for c in range(3):
                    dcol[2 * a, c, chunk(row), :] = f_in[c] - f_out[c]
                    dcol[2 * a + 1, c, chunk(row), :] = roll(f_out[c], 127) - f_in[c]

    for k in range(10):
        row = 8 * k + 8
        at = chunk(row)
        for b in range(2):
            l_side, r_side = [], []
            for c in range(3):
                c0, c1 = ctr[b, c, at, :], ctr[2 + b, c, at, :]
                inner = c1 - c0
                before = c0 - ctr[2 + b, c, chunk(row - 1), :]
                after = ctr[b, c, chunk(row + 1), :] - c1
                s0, s1 = 0.5 * minmod(before, inner), 0.5 * minmod(inner, after)
                base[b, c, at, :] = c0 - s0
                plus[b, c, at, :] = c1 + s1
                l_side.append(c0 + s0)
                r_side.append(c1 - s1)
            if 1 <= k < 9:
                f = face(side(l_side, speeds(*l_side), 1), side(r_side, speeds(*r_side), 1))
                for c in range(3):
                    mid[b, c, at, :] = f[c]
    for k in range(1, 10):
        row = 8 * k + 8
        for b in range(2):
            l_side = [plus[b, c, chunk(row - 1), :] for c in range(3)]
            r_side = [base[b, c, chunk(row), :] for c in range(3)]
            f = face(side(l_side, speeds(*l_side), 1), side(r_side, speeds(*r_side), 1))
            for c in range(3):
                low[b, c, chunk(row), :] = f[c]
    source = lax.shift_right_logical(lane, 1)
    odd = lax.bitwise_and(lane, 1) == 1
    inside_col = source < ext[0, 0, 1]
    for k in range(1, 9):
        row = 8 * k + 8
        at = chunk(row)
        inside = inside_col & (row8 + 8 * (k - 1) < ext[0, 0, 0])
        for c in range(3):
            done = [[], []]
            for b in range(2):
                f_mid, f_low, f_next = mid[b, c, at, :], low[b, c, at, :], low[b, c, chunk(row + 1), :]
                for a, tall in enumerate((f_mid - f_low, f_next - f_mid)):
                    x = ctr[2 * a + b, c, at, :] - HALF * (tall + dcol[2 * a + b, c, at, :])
                    done[a].append(
                        pick(x, source + 2)
                    )
            for a in range(2):
                x = jnp.where(odd, done[a][1], done[a][0])
                refined[c, pl.ds(16 * (k - 1) + a, 8, stride=2), :] = jnp.where(inside, x, 0.0)


def solution(mesh):
    n_row, n_col = mesh.shape["row"], mesh.shape["col"]
    vmem = pl.BlockSpec(memory_space=pltpu.VMEM)
    smem = pl.BlockSpec(memory_space=pltpu.SMEM)
    hbm = pl.BlockSpec(memory_space=pltpu.HBM)
    buf = lambda *shape: pltpu.VMEM(shape, F32)

    def per_device(state, row_count, col_count, patch_pos, patch_ext):
        in_hbm = [
            x if x.ndim == 2 else pltpu.with_memory_space_constraint(x, pltpu.HBM)
            for x in (state, row_count, col_count, patch_pos, patch_ext)
        ]
        corner = buf(3, 8, 128)
        half = buf(3, 32, 128)
        *parts, cnt, pos, ext, err = pl.pallas_call(
            functools.partial(exchange_kernel, n_row, n_col),
            out_shape=(
                buf(3, 3, ROWS, 128), buf(3, 2, 64, 128), buf(112, 128), half, buf(32, 128), buf(24, 128),
                pltpu.SMEM((8, 128), F32),
                pltpu.SMEM((1, 1, 2), jnp.int32),
                pltpu.SMEM((1, 1, 2), jnp.int32),
                buf(64, 128),
            ),
            in_specs=[hbm, smem, smem, hbm, hbm],
            out_specs=(vmem,) * 6 + (smem,) * 3 + (vmem,),
            scratch_shapes=[
                buf(8, 128), buf(128, 128), half, buf(16, 128), *([buf(8, 128)] * 4), buf(16, 128),
                buf(128, 128), buf(3, 128, 128), corner,
                *([buf(3, 2, ROWS, 128)] * 4), *([buf(3, 1, 88, 128)] * 3),
                *([buf(3, 1, 48, 128)] * 8),
                pltpu.SemaphoreType.DMA((4,)),
                pltpu.SemaphoreType.DMA((N_MSG,)),
                pltpu.SemaphoreType.DMA((N_MSG,)),
            ],
            compiler_params=pltpu.CompilerParams(
                collective_id=0, has_side_effects=True, vmem_limit_bytes=24 << 20
            ),
        )(*in_hbm)
        return pl.pallas_call(
            patch_kernel,
            out_shape=(
                jax.ShapeDtypeStruct((64, 128), F32),
                jax.ShapeDtypeStruct((3, 128, 256), F32),
                jax.ShapeDtypeStruct((3, 128, 128), F32),
            ),
            in_specs=[smem] * 3 + [vmem] * 7,
            out_specs=(vmem,) * 3,
            scratch_shapes=[
                buf(4, 3, 144, 128), buf(3, 96, 128), buf(3, 96, 128),
                buf(4, 3, 96, 128), buf(4, 3, 96, 128), *([buf(2, 3, 96, 128)] * 4),
            ],
            compiler_params=pltpu.CompilerParams(vmem_limit_bytes=24 << 20),
        )(cnt, pos, ext, *parts, err)

    return jax.shard_map(
        per_device,
        mesh=mesh,
        in_specs=(
            P(None, "row", "col"),
            P("row", "col"),
            P("row", "col"),
            P("row", "col", None),
            P("row", "col", None),
        ),
        out_specs=(P("row", "col"), P(None, "row", "col"), P(None, "row", "col")),
        check_vma=False,
    )
```

```python
import functools

import jax
import jax.numpy as jnp
from jax import lax
from jax.experimental import pallas as pl
from jax.experimental.pallas import tpu as pltpu
from jax.sharding import PartitionSpec as P

MESH = pl.DeviceIdType.MESH
F32 = jnp.float32
HALF = 0.05
BASE = 80
ROWS = 224
N_MSG = 11


def chunk(start, size=8):
    return pl.ds(start, size)


def lanes(shape=(8, 128)):
    return lax.broadcasted_iota(jnp.int32, shape, 1)


def roll(x, by):
    return pltpu.roll(x, by % x.shape[1] if isinstance(by, int) else by, 1)


def speeds(h, m1, m2):
    return m1 / h, m2 / h, jnp.sqrt(h)


def side(u, vel, normal):
    h, m1, m2 = u
    v1, v2, wave = vel
    pressure = 0.5 * h * h
    if normal == 1:
        return u, (m1, m1 * v1 + pressure, m2 * v1), jnp.abs(v1) + wave
    return u, (m2, m1 * v2, m2 * v2 + pressure), jnp.abs(v2) + wave


def face(lower, upper):
    speed = jnp.maximum(lower[2], upper[2])
    return [
        (lower[1][c] + upper[1][c]) - speed * (upper[0][c] - lower[0][c])
        for c in range(3)
    ]


def minmod(a, b):
    chosen = jnp.where(jnp.abs(a) < jnp.abs(b), a, b)
    return jnp.where(a * b > 0, chosen, 0.0)


def from_lower(xs, lane, hop=1):
    rolled = [roll(x, hop) for x in xs]
    if len(xs) == 1:
        return rolled
    return [jnp.where(lane == 0, rolled[g - 1], rolled[g]) for g in range(len(xs))]


def from_upper(xs, lane, hop=1):
    rolled = [roll(x, -hop) for x in xs]
    if len(xs) == 1:
        return rolled
    return [
        jnp.where(lane == 127, rolled[(g + 1) % len(xs)], rolled[g])
        for g in range(len(xs))
    ]


def speed_pass(src, vel, groups, first, last):
    for i in range(first, last):
        at = chunk(8 * i)
        for g in groups:
            for k, value in enumerate(speeds(*(src[c, g, at, :] for c in range(3)))):
                vel[k, g, at, :] = value


def step_pass(src, vel, dst, groups, first, last, hop=1):
    lane = lanes()
    for i in range(first, last):
        row = 8 * i

        def load(shift, g, normal):
            at = chunk(row + shift)
            return side(
                [src[c, g, at, :] for c in range(3)],
                [vel[c, g, at, :] for c in range(3)],
                normal,
            )

        along = [load(0, g, 2) for g in groups]
        shifted = [from_lower([a[0][k] for a in along], lane, hop) for k in range(3)]
        low = []
        for n in range(len(groups)):
            u = [x[n] for x in shifted]
            low.append(face(side(u, speeds(*u), 2), along[n]))
        high = [from_upper([f[c] for f in low], lane, hop) for c in range(3)]
        for n, g in enumerate(groups):
            here = load(0, g, 1)
            down = face(load(-1, g, 1), here)
            up = face(here, load(1, g, 1))
            for c in range(3):
                change = (up[c] - down[c]) + (high[c][n] - low[n][c])
                dst[c, g, chunk(row), :] = here[0][c] - HALF * change


def block_means(src, row, g, c, n=8):
    pair = src[c, g, pl.ds(row, n, stride=2), :] + src[c, g, pl.ds(row + 1, n, stride=2), :]
    return 0.25 * (pair + roll(pair, 127))


def pick(x, index):
    return jnp.take_along_axis(x, index, axis=1, mode="promise_in_bounds")


def exchange_kernel(
    n_row, n_col, state, row_count, col_count, pos_hbm, ext_hbm,
    st, rm, l_low, l_high, ul, dl, counts, pos, ext, err,
    lpack, low_s, high_s, utile, cnt, rl, url, dr, dn, up_low, ahead, sides,
    vel, rim, fine1, fine2, cgrid, cvel, cone,
    strip, svel, strip1, svel1, strip2, sgrid, sgvel, sone,
    local_sem, send_sem, recv_sem,
):
    me_r, me_c = lax.axis_index("row"), lax.axis_index("col")

    def device(dr, dc):
        return (lax.rem(me_r + (dr + n_row), n_row), lax.rem(me_c + (dc + n_col), n_col))

    loads = [
        pltpu.make_async_copy(
            state.at[:, :, pl.ds(128 * g, 128)], st.at[:, g, pl.ds(BASE, 128), :], local_sem.at[g]
        )
        for g in range(2)
    ]
    loads += [
        pltpu.make_async_copy(pos_hbm, pos, local_sem.at[2]),
        pltpu.make_async_copy(ext_hbm, ext, local_sem.at[3]),
    ]
    barrier = pltpu.get_barrier_semaphore()
    around = [(a, b) for a in (-1, 0, 1) for b in (-1, 0, 1) if (a, b) != (0, 0)]
    for a, b in around:
        pl.semaphore_signal(barrier, inc=1, device_id=device(a, b), device_id_type=MESH)
    for load in loads[:2]:
        load.start()

    lane = lanes()
    row8 = lax.broadcasted_iota(jnp.int32, (8, 128), 0)
    rc = row_count[0, 0]
    both_counts = jnp.where(lane == 96, rc, col_count[0, 0]).astype(F32)
    for load in loads[:2]:
        load.wait()

    def edge(columns, lane_at):
        tile = None
        for c in range(3):
            for k in range(16):
                to = 32 * c + 2 * k
                x = roll(columns(c, k), to - lane_at)
                tile = x if tile is None else jnp.where(lane >= to, x, tile)
        return jnp.where(lane >= 96, both_counts, tile)

    def fold(low, high):
        return jnp.where(lane < 64, roll(high, 64), low)

    low_s[chunk(104), :] = edge(lambda c, k: st[c, 1, chunk(BASE + 8 * k), :], 126)
    lpack[...] = edge(lambda c, k: st[c, 0, chunk(BASE + 8 * k), :], 0)
    for c in range(3):
        for k in range(4):
            low_s[chunk(32 * c + 8 * k), :] = fold(
                st[c, 1, chunk(BASE + 64 + 8 * k), :], st[c, 1, chunk(BASE + 96 + 8 * k), :]
            )

        for g in range(2):
            utile[pl.ds(4 * c + 2 * g, 2), :] = st[c, g, pl.ds(BASE, 2), :]
            low_s[pl.ds(112 + 4 * c + 2 * g, 2), :] = st[c, g, pl.ds(BASE + 126, 2), :]
    low_s[chunk(96), :] = both_counts
    low_s[pl.ds(124, 4), :] = both_counts[:4]
    utile[pl.ds(12, 4), :] = both_counts[:4]

    pl.semaphore_wait(barrier, 8)
    both = pl.ds(0, 2)
    messages = [
        ((1, 0), low_s, up_low),
        ((0, 1), low_s.at[pl.ds(104, 8), :], l_low.at[pl.ds(104, 8), :]),
        ((0, -1), lpack, rl),
        ((-1, 0), utile, dn),
        ((1, 1), low_s.at[pl.ds(112, 16), :], ul.at[pl.ds(8, 16), :]),
        ((1, -1), lpack, url),
        ((-1, 1), utile, dl.at[pl.ds(0, 16), :]),
        ((-1, -1), lpack, dr),
        ((0, 1), low_s.at[pl.ds(0, 104), :], l_low.at[pl.ds(0, 104), :]),
        ((1, 0), st.at[:, both, pl.ds(BASE + 64, 64), :], st.at[:, both, pl.ds(0, 64), :]),
        ((0, 1), high_s, l_high),
    ]
    copies = [
        pltpu.make_async_remote_copy(
            src_ref=src, dst_ref=dst, send_sem=send_sem.at[i], recv_sem=recv_sem.at[i],
            device_id=device(*to), device_id_type=MESH,
        )
        for i, (to, src, dst) in enumerate(messages)
    ]
    for copy in copies[:9]:
        copy.start()
    for load in loads[2:]:
        load.start()

    for c in range(3):
        tile = None
        for g, from_lane in ((0, 0), (1, 124)):
            for k in range(16):
                to = 64 * g + 4 * k
                x = roll(st[c, g, chunk(BASE + 8 * k), :], to - from_lane)
                tile = x if tile is None else jnp.where(lane >= to, x, tile)
        sides[c] = tile

    even = lax.rem(2 * lane, 128)
    own = (0, 1)
    speed_pass(st, vel, own, 10, 26)
    step_pass(st, vel, fine1, own, 11, 25)

    copies[0].wait_recv()
    for c in range(3):
        for k in range(4):
            x = up_low[chunk(32 * c + 8 * k), :]
            ahead[c, chunk(8 * k), :] = x
            ahead[c, chunk(32 + 8 * k), :] = roll(x, 64)
        for k in range(8):
            ahead[c, chunk(64 + 8 * k), :] = st[c, 1, chunk(BASE + 8 * k), :]
    for c in range(3):
        top = [
            jnp.where(
                row8 + 8 * k < rc,
                ahead[c, chunk(64 + 8 * k - rc), :],
                ahead[c, chunk(64 + 8 * k), :],
            )
            for k in range(8)
        ]
        for k in range(4):
            high_s[c, chunk(8 * k), :] = fold(top[k], top[k + 4])
    copies[10].start()
    copies[9].start()

    def coarse_own(i):
        n = 8 if i else 4
        for c in range(3):
            row = BASE - 2 * n + 16 * i
            halves = [pick(block_means(st, row, g, c, n), even[:n]) for g in range(2)]
            cgrid[c, 0, pl.ds(8 * i + 8 - n, n), :] = jnp.where(lane[:n] < 64, *halves)
        speed_pass(cgrid, cvel, (0,), i, i + 1)

    def estimate(i):
        total = None
        for c in range(3):
            halves = [pick(block_means(fine2, BASE + 16 * i, g, c), even) for g in range(2)]
            gap = jnp.abs(jnp.where(lane < 64, *halves) - cone[c, 0, chunk(8 * i + 8), :])
            total = gap if total is None else total + gap
        err[chunk(8 * i), :] = 10.0 * total

    speed_pass(fine1, vel, own, 11, 25)
    step_pass(fine1, vel, fine2, own, 12, 24)
    for i in range(1, 9):
        coarse_own(i)
    step_pass(cgrid, cvel, cone, (0,), 2, 8)
    for i in range(1, 7):
        estimate(i)

    for copy in copies[1:8]:
        copy.wait_recv()
    for load in loads[2:]:
        load.wait()
    for c in range(3):
        for g in range(2):
            st[c, g, pl.ds(BASE - 2, 2), :] = up_low[pl.ds(112 + 4 * c + 2 * g, 2), :]
            st[c, g, pl.ds(BASE + 128, 2), :] = dn[pl.ds(4 * c + 2 * g, 2), :]
    speed_pass(st, rim, own, 9, 12)
    speed_pass(st, rim, own, 24, 27)
    step_pass(st, rim, fine1, own, 9, 11)
    step_pass(st, rim, fine1, own, 25, 27)
    speed_pass(fine1, rim, own, 9, 13)
    speed_pass(fine1, rim, own, 23, 27)
    step_pass(fine1, rim, fine2, own, 10, 12)
    step_pass(fine1, rim, fine2, own, 24, 26)
    coarse_own(0)
    coarse_own(9)
    step_pass(cgrid, cvel, cone, (0,), 1, 2)
    step_pass(cgrid, cvel, cone, (0,), 8, 9)
    estimate(0)
    estimate(7)

    left, right, corner, lower_right = l_low[chunk(104), :], rl[...], url[...], dr[...]
    part, place = lax.shift_right_logical(lane, 4), lax.bitwise_and(lane, 15)

    def folded(a, b, c, d):
        return jnp.where(place < 2, a, jnp.where(place < 8, b, jnp.where(place < 12, c, d)))

    for j in range(4):
        block = 2 * part + (j - 1)
        own_at = lax.bitwise_and(4 * block + jnp.where(place < 8, place - 2, place + 56), 127)
        for c in range(3):
            at = lax.bitwise_and(32 * c + 2 * block + lax.bitwise_and(place, 1), 127)
            own_cells = pick(sides[c], own_at)
            x = folded(pick(left, at), own_cells, own_cells, pick(right, at))
            if j == 0:
                rows = chunk(BASE - 8)
                above = folded(
                    roll(ul[chunk(4 + 4 * c), :], 2), roll(st[c, 0, rows, :], 2),
                    roll(st[c, 1, rows, :], 12), roll(corner, -18 - 32 * c),
                )
                x = jnp.where(part == 0, above, x)
            if j == 3:
                rows = chunk(BASE + 128)
                below = folded(
                    roll(dl[chunk(2 + 4 * c), :], -14), roll(st[c, 0, rows, :], 114),
                    roll(st[c, 1, rows, :], -4), roll(lower_right, 124 - 32 * c),
                )
                x = jnp.where(part == 7, below, x)
            strip[c, 0, chunk(8 + 8 * j), :] = x
    one = (0,)
    speed_pass(strip, svel, one, 1, 5)
    step_pass(strip, svel, strip1, one, 1, 5)
    speed_pass(strip1, svel1, one, 1, 5)
    step_pass(strip1, svel1, strip2, one, 2, 4)
    for i in range(3):
        for c in range(3):
            sgrid[c, 0, chunk(8 * i), :] = block_means(strip, 16 * i, 0, c)
    speed_pass(sgrid, sgvel, one, 0, 3)
    step_pass(sgrid, sgvel, sone, one, 1, 2, 2)
    total = None
    for c in range(3):
        gap = jnp.abs(block_means(strip2, 16, 0, c) - sone[c, 0, chunk(8), :])
        total = gap if total is None else total + gap
    total = 10.0 * total
    for i in range(8):
        at = chunk(8 * i)
        value = jnp.where(lane == 127, roll(total, 117 - 16 * i), err[at, :])
        err[at, :] = jnp.where(lane == 0, roll(total, -(16 * i + 2)), value)

    for c in range(3):
        for k in range(-8, 17):
            col = 32 * c + 2 * k
            if k < 0:
                x = roll(corner, -(col + 32))
            else:
                x = roll(lower_right, -32 * c) if k == 16 else roll(right, -col)
            st[c, 2, chunk(BASE + 8 * k), :] = x

    for copy in copies[8:10]:
        copy.wait_recv()
    for c in range(3):
        for g in range(2):
            for k in range(8):
                here = st[c, g, chunk(BASE + 8 * k), :]
                above = st[c, g, chunk(64 + 8 * k - rc), :]
                rm[c, g, chunk(8 * k), :] = jnp.where(row8 + 8 * k < rc, above, here)
    given = (rl[:1], up_low[pl.ds(96, 1)], dn[pl.ds(12, 1)], url[:1], dl[pl.ds(12, 1)], dr[:1], lpack[:1])
    for i, x in enumerate(given):
        cnt[pl.ds(i, 1), :] = x
    keep = pltpu.make_async_copy(cnt, counts, local_sem.at[0])
    keep.start()
    copies[10].wait_recv()
    for copy in copies:
        copy.wait_send()
    keep.wait()


def patch_kernel(
    cnt, pos, ext, st, rm, l_low, l_high, ul, dl, err_in,
    err, moved_out, refined,
    tiles, win, wvel, ctr, dcol, plus, base, mid, low, moved, sem,
):
    lane = lanes()
    row8 = lax.broadcasted_iota(jnp.int32, (8, 128), 0)
    writes = [
        pltpu.make_async_copy(err_in, err, sem.at[0]),
        pltpu.make_async_copy(moved, moved_out, sem.at[1]),
    ]
    writes[0].start()
    rc_of = lambda i: cnt[i, 96].astype(jnp.int32)
    cc_of = lambda i: cnt[i, 97].astype(jnp.int32)
    rows_below = (rc_of(4), rc_of(2), rc_of(2), rc_of(5))
    cols_in = {"up": (cc_of(1), cc_of(3)), "own": (cc_of(6), cc_of(0)), "down": (cc_of(2), cc_of(5))}

    rc_right = rc_of(0)
    for c in range(3):
        for k in range(4):
            for start, x in ((0, l_high[c, chunk(8 * k), :]), (64, l_low[chunk(32 * c + 8 * k), :])):
                tiles[0, c, chunk(8 + start + 8 * k), :] = x
                tiles[0, c, chunk(40 + start + 8 * k), :] = roll(x, 64)
        tiles[0, c, chunk(0), :] = ul[chunk(4 + 4 * c), :]

    for c in range(3):
        for k in range(-1, 17):
            at = chunk(BASE + 8 * k)
            if k < 0:
                values = [ul[chunk(4 + 4 * c), :], st[c, 0, at, :], st[c, 1, at, :], st[c, 2, at, :]]
            elif k < 16:
                own = [rm[c, g, chunk(8 * k), :] if k < 8 else st[c, g, at, :] for g in range(2)]
                beside = st[c, 2, at, :]
                if k < 8:
                    above = st[c, 2, chunk(BASE + 8 * k - rc_right), :]
                    beside = jnp.where(row8 + 8 * k < rc_right, above, beside)
                values = [tiles[0, c, chunk(8 * k + 8), :], *own, beside]
            else:
                above = [
                    tiles[0, c, chunk(136 - rows_below[0]), :],
                    st[c, 0, chunk(BASE + 128 - rows_below[1]), :],
                    st[c, 1, chunk(BASE + 128 - rows_below[2]), :],
                    st[c, 2, chunk(BASE + 128 - rows_below[3]), :],
                ]
                below = [dl[chunk(2 + 4 * c), :], st[c, 0, at, :], st[c, 1, at, :], st[c, 2, at, :]]
                values = [jnp.where(row8 < rows_below[g], above[g], below[g]) for g in range(4)]
                tiles[0, c, chunk(136), :] = values[0]
            c0, c_right = cols_in["up" if k < 0 else "down" if k == 16 else "own"]
            m0 = jnp.where(lane < c0, roll(values[0], c0), values[1])
            m_right = jnp.where(lane < c_right, roll(values[2], c_right), values[3])
            put = chunk(8 * k + 8)
            for g, value in enumerate((m0, values[2], m_right)):
                tiles[g + 1, c, put, :] = value
            if 0 <= k < 16:
                moved[c, chunk(8 * k), pl.ds(0, 128)] = m0
                moved[c, chunk(8 * k), pl.ds(128, 128)] = values[2]

    writes[1].start()

    p0, p1 = pos[0, 0, 0], pos[0, 0, 1]
    group = lax.shift_right_logical(p1 + 126, 7)
    offset = lax.bitwise_and(p1 + 126, 127)
    back = lax.bitwise_and(128 - offset, 127)
    for k in range(10):
        u = []
        for c in range(3):
            at = chunk(p0 + 8 * k)
            a, b = tiles[group, c, at, :], tiles[group + 1, c, at, :]
            u.append(jnp.where(lane < 128 - offset, roll(a, back), roll(b, back)))
            win[c, chunk(8 * k + 8), :] = u[c]
        for c, value in enumerate(speeds(*u)):
            wvel[c, chunk(8 * k + 8), :] = value

    for k in range(10):
        row = 8 * k + 8

        def load(shift, normal):
            at = chunk(row + shift)
            return side([win[c, at, :] for c in range(3)], [wvel[c, at, :] for c in range(3)], normal)

        here = load(0, 1)
        down, up = face(load(-1, 1), here), face(here, load(1, 1))
        across = load(0, 2)
        lower = [roll(x, 1) for x in across[0]]
        left = face(side(lower, speeds(*lower), 2), across)
        right = [roll(x, 127) for x in left]
        for a in range(2):
            near = [[] for _ in range(4)]
            for c in range(3):
                twice = 2.0 * here[1][c]
                tall = up[c] - twice if a else twice - down[c]
                half_way = here[0][c] - HALF * tall
                twice = 2.0 * across[1][c]
                e = half_way - HALF * (twice - left[c])
                o = half_way - HALF * (right[c] - twice)
                ctr[2 * a, c, chunk(row), :] = e
                ctr[2 * a + 1, c, chunk(row), :] = o
                if 1 <= k < 9:
                    inner, outer = o - e, e - roll(o, 1)
                    s_e, s_o = 0.5 * minmod(outer, inner), 0.5 * minmod(inner, roll(outer, 127))
                    for i, x in enumerate((roll(o + s_o, 1), e - s_e, e + s_e, o - s_o)):
                        near[i].append(x)
            if 1 <= k < 9:
                sides = [side(u, speeds(*u), 2) for u in near]
                f_out, f_in = face(sides[0], sides[1]), face(sides[2], sides[3])
                for c in range(3):
                    dcol[2 * a, c, chunk(row), :] = f_in[c] - f_out[c]
                    dcol[2 * a + 1, c, chunk(row), :] = roll(f_out[c], 127) - f_in[c]

    for k in range(10):
        row = 8 * k + 8
        at = chunk(row)
        for b in range(2):
            l_side, r_side = [], []
            for c in range(3):
                c0, c1 = ctr[b, c, at, :], ctr[2 + b, c, at, :]
                inner = c1 - c0
                before = c0 - ctr[2 + b, c, chunk(row - 1), :]
                after = ctr[b, c, chunk(row + 1), :] - c1
                s0, s1 = 0.5 * minmod(before, inner), 0.5 * minmod(inner, after)
                base[b, c, at, :] = c0 - s0
                plus[b, c, at, :] = c1 + s1
                l_side.append(c0 + s0)
                r_side.append(c1 - s1)
            if 1 <= k < 9:
                f = face(side(l_side, speeds(*l_side), 1), side(r_side, speeds(*r_side), 1))
                for c in range(3):
                    mid[b, c, at, :] = f[c]
    for k in range(1, 10):
        row = 8 * k + 8
        for b in range(2):
            l_side = [plus[b, c, chunk(row - 1), :] for c in range(3)]
            r_side = [base[b, c, chunk(row), :] for c in range(3)]
            f = face(side(l_side, speeds(*l_side), 1), side(r_side, speeds(*r_side), 1))
            for c in range(3):
                low[b, c, chunk(row), :] = f[c]
    source = lax.shift_right_logical(lane, 1)
    odd = lax.bitwise_and(lane, 1) == 1
    inside_col = source < ext[0, 0, 1]
    for k in range(1, 9):
        row = 8 * k + 8
        at = chunk(row)
        inside = inside_col & (row8 + 8 * (k - 1) < ext[0, 0, 0])
        for c in range(3):
            done = [[], []]
            for b in range(2):
                f_mid, f_low, f_next = mid[b, c, at, :], low[b, c, at, :], low[b, c, chunk(row + 1), :]
                for a, tall in enumerate((f_mid - f_low, f_next - f_mid)):
                    x = ctr[2 * a + b, c, at, :] - HALF * (tall + dcol[2 * a + b, c, at, :])
                    done[a].append(
                        pick(x, source + 2)
                    )
            for a in range(2):
                x = jnp.where(odd, done[a][1], done[a][0])
                refined[c, pl.ds(16 * (k - 1) + a, 8, stride=2), :] = jnp.where(inside, x, 0.0)
    for write in writes:
        write.wait()


def solution(mesh):
    n_row, n_col = mesh.shape["row"], mesh.shape["col"]
    vmem = pl.BlockSpec(memory_space=pltpu.VMEM)
    smem = pl.BlockSpec(memory_space=pltpu.SMEM)
    hbm = pl.BlockSpec(memory_space=pltpu.HBM)
    buf = lambda *shape: pltpu.VMEM(shape, F32)

    def per_device(state, row_count, col_count, patch_pos, patch_ext):
        in_hbm = [
            x if x.ndim == 2 else pltpu.with_memory_space_constraint(x, pltpu.HBM)
            for x in (state, row_count, col_count, patch_pos, patch_ext)
        ]
        corner = buf(3, 8, 128)
        half = buf(3, 32, 128)
        *parts, cnt, pos, ext, err = pl.pallas_call(
            functools.partial(exchange_kernel, n_row, n_col),
            out_shape=(
                buf(3, 3, ROWS, 128), buf(3, 2, 64, 128), buf(112, 128), half, buf(32, 128), buf(24, 128),
                pltpu.SMEM((8, 128), F32),
                pltpu.SMEM((1, 1, 2), jnp.int32),
                pltpu.SMEM((1, 1, 2), jnp.int32),
                buf(64, 128),
            ),
            in_specs=[hbm, smem, smem, hbm, hbm],
            out_specs=(vmem,) * 6 + (smem,) * 3 + (vmem,),
            scratch_shapes=[
                buf(8, 128), buf(128, 128), half, buf(16, 128), *([buf(8, 128)] * 4), buf(16, 128),
                buf(128, 128), buf(3, 128, 128), corner,
                *([buf(3, 2, ROWS, 128)] * 4), *([buf(3, 1, 88, 128)] * 3),
                *([buf(3, 1, 48, 128)] * 8),
                pltpu.SemaphoreType.DMA((4,)),
                pltpu.SemaphoreType.DMA((N_MSG,)),
                pltpu.SemaphoreType.DMA((N_MSG,)),
            ],
            compiler_params=pltpu.CompilerParams(
                collective_id=0, has_side_effects=True, vmem_limit_bytes=24 << 20
            ),
        )(*in_hbm)
        return pl.pallas_call(
            patch_kernel,
            out_shape=(
                jax.ShapeDtypeStruct((64, 128), F32),
                jax.ShapeDtypeStruct((3, 128, 256), F32),
                jax.ShapeDtypeStruct((3, 128, 128), F32),
            ),
            in_specs=[smem] * 3 + [vmem] * 7,
            out_specs=(hbm, hbm, vmem),
            scratch_shapes=[
                buf(4, 3, 144, 128), buf(3, 96, 128), buf(3, 96, 128),
                buf(4, 3, 96, 128), buf(4, 3, 96, 128), *([buf(2, 3, 96, 128)] * 4),
                buf(3, 128, 256), pltpu.SemaphoreType.DMA((2,)),
            ],
            compiler_params=pltpu.CompilerParams(vmem_limit_bytes=24 << 20),
        )(cnt, pos, ext, *parts, err)

    return jax.shard_map(
        per_device,
        mesh=mesh,
        in_specs=(
            P(None, "row", "col"),
            P("row", "col"),
            P("row", "col"),
            P("row", "col", None),
            P("row", "col", None),
        ),
        out_specs=(P("row", "col"), P(None, "row", "col"), P(None, "row", "col")),
        check_vma=False,
    )
```

```python
import functools

import jax
import jax.numpy as jnp
from jax import lax
from jax.experimental import pallas as pl
from jax.experimental.pallas import tpu as pltpu
from jax.sharding import PartitionSpec as P

MESH = pl.DeviceIdType.MESH
F32 = jnp.float32
HALF = 0.05
BASE = 80
ROWS = 224
N_MSG = 11


def chunk(start, size=8):
    return pl.ds(start, size)


def lanes(shape=(8, 128)):
    return lax.broadcasted_iota(jnp.int32, shape, 1)


def roll(x, by):
    return pltpu.roll(x, by % x.shape[1] if isinstance(by, int) else by, 1)


def speeds(h, m1, m2):
    r = lax.rsqrt(h)
    inverse = r * r
    return m1 * inverse, m2 * inverse, h * r


def side(u, vel, normal):
    h, m1, m2 = u
    v1, v2, wave = vel
    pressure = 0.5 * h * h
    if normal == 1:
        return u, (m1, m1 * v1 + pressure, m2 * v1), jnp.abs(v1) + wave
    return u, (m2, m1 * v2, m2 * v2 + pressure), jnp.abs(v2) + wave


def face(lower, upper):
    speed = jnp.maximum(lower[2], upper[2])
    return [
        (lower[1][c] + upper[1][c]) - speed * (upper[0][c] - lower[0][c])
        for c in range(3)
    ]


def minmod(a, b):
    chosen = jnp.where(jnp.abs(a) < jnp.abs(b), a, b)
    return jnp.where(a * b > 0, chosen, 0.0)


def from_lower(xs, lane, hop=1):
    rolled = [roll(x, hop) for x in xs]
    if len(xs) == 1:
        return rolled
    return [jnp.where(lane == 0, rolled[g - 1], rolled[g]) for g in range(len(xs))]


def from_upper(xs, lane, hop=1):
    rolled = [roll(x, -hop) for x in xs]
    if len(xs) == 1:
        return rolled
    return [
        jnp.where(lane == 127, rolled[(g + 1) % len(xs)], rolled[g])
        for g in range(len(xs))
    ]


def speed_pass(src, vel, groups, first, last):
    for i in range(first, last):
        at = chunk(8 * i)
        for g in groups:
            for k, value in enumerate(speeds(*(src[c, g, at, :] for c in range(3)))):
                vel[k, g, at, :] = value


def step_pass(src, vel, dst, groups, first, last, hop=1):
    lane = lanes()
    for i in range(first, last):
        row = 8 * i

        def load(shift, g, normal):
            at = chunk(row + shift)
            return side(
                [src[c, g, at, :] for c in range(3)],
                [vel[c, g, at, :] for c in range(3)],
                normal,
            )

        along = [load(0, g, 2) for g in groups]
        shifted = [from_lower([a[0][k] for a in along], lane, hop) for k in range(3)]
        low = []
        for n in range(len(groups)):
            u = [x[n] for x in shifted]
            low.append(face(side(u, speeds(*u), 2), along[n]))
        high = [from_upper([f[c] for f in low], lane, hop) for c in range(3)]
        for n, g in enumerate(groups):
            here = load(0, g, 1)
            down = face(load(-1, g, 1), here)
            up = face(here, load(1, g, 1))
            for c in range(3):
                change = (up[c] - down[c]) + (high[c][n] - low[n][c])
                dst[c, g, chunk(row), :] = here[0][c] - HALF * change


def block_means(src, row, g, c, n=8):
    pair = src[c, g, pl.ds(row, n, stride=2), :] + src[c, g, pl.ds(row + 1, n, stride=2), :]
    return 0.25 * (pair + roll(pair, 127))


def pick(x, index):
    return jnp.take_along_axis(x, index, axis=1, mode="promise_in_bounds")


def exchange_kernel(
    n_row, n_col, state, row_count, col_count, pos_hbm, ext_hbm,
    st, rm, l_low, l_high, ul, dl, counts, pos, ext, err,
    lpack, low_s, high_s, utile, cnt, rl, url, dr, dn, up_low, ahead, sides,
    vel, rim, fine1, fine2, cgrid, cvel, cone,
    strip, svel, strip1, svel1, strip2, sgrid, sgvel, sone,
    local_sem, send_sem, recv_sem,
):
    me_r, me_c = lax.axis_index("row"), lax.axis_index("col")

    def device(dr, dc):
        return (lax.rem(me_r + (dr + n_row), n_row), lax.rem(me_c + (dc + n_col), n_col))

    loads = [
        pltpu.make_async_copy(
            state.at[:, :, pl.ds(128 * g, 128)], st.at[:, g, pl.ds(BASE, 128), :], local_sem.at[g]
        )
        for g in range(2)
    ]
    loads += [
        pltpu.make_async_copy(pos_hbm, pos, local_sem.at[2]),
        pltpu.make_async_copy(ext_hbm, ext, local_sem.at[3]),
    ]
    barrier = pltpu.get_barrier_semaphore()
    around = [(a, b) for a in (-1, 0, 1) for b in (-1, 0, 1) if (a, b) != (0, 0)]
    for a, b in around:
        pl.semaphore_signal(barrier, inc=1, device_id=device(a, b), device_id_type=MESH)
    for load in loads[:2]:
        load.start()

    lane = lanes()
    row8 = lax.broadcasted_iota(jnp.int32, (8, 128), 0)
    rc = row_count[0, 0]
    both_counts = jnp.where(lane == 96, rc, col_count[0, 0]).astype(F32)
    for load in loads[:2]:
        load.wait()

    def edge(columns, lane_at):
        tile = None
        for c in range(3):
            for k in range(16):
                to = 32 * c + 2 * k
                x = roll(columns(c, k), to - lane_at)
                tile = x if tile is None else jnp.where(lane >= to, x, tile)
        return jnp.where(lane >= 96, both_counts, tile)

    def fold(low, high):
        return jnp.where(lane < 64, roll(high, 64), low)

    low_s[chunk(104), :] = edge(lambda c, k: st[c, 1, chunk(BASE + 8 * k), :], 126)
    lpack[...] = edge(lambda c, k: st[c, 0, chunk(BASE + 8 * k), :], 0)
    for c in range(3):
        for k in range(4):
            low_s[chunk(32 * c + 8 * k), :] = fold(
                st[c, 1, chunk(BASE + 64 + 8 * k), :], st[c, 1, chunk(BASE + 96 + 8 * k), :]
            )

        for g in range(2):
            utile[pl.ds(4 * c + 2 * g, 2), :] = st[c, g, pl.ds(BASE, 2), :]
            low_s[pl.ds(112 + 4 * c + 2 * g, 2), :] = st[c, g, pl.ds(BASE + 126, 2), :]
    low_s[chunk(96), :] = both_counts
    low_s[pl.ds(124, 4), :] = both_counts[:4]
    utile[pl.ds(12, 4), :] = both_counts[:4]

    pl.semaphore_wait(barrier, 8)
    both = pl.ds(0, 2)
    messages = [
        ((1, 0), low_s, up_low),
        ((0, 1), low_s.at[pl.ds(104, 8), :], l_low.at[pl.ds(104, 8), :]),
        ((0, -1), lpack, rl),
        ((-1, 0), utile, dn),
        ((1, 1), low_s.at[pl.ds(112, 16), :], ul.at[pl.ds(8, 16), :]),
        ((1, -1), lpack, url),
        ((-1, 1), utile, dl.at[pl.ds(0, 16), :]),
        ((-1, -1), lpack, dr),
        ((0, 1), low_s.at[pl.ds(0, 104), :], l_low.at[pl.ds(0, 104), :]),
        ((1, 0), st.at[:, both, pl.ds(BASE + 64, 64), :], st.at[:, both, pl.ds(0, 64), :]),
        ((0, 1), high_s, l_high),
    ]
    copies = [
        pltpu.make_async_remote_copy(
            src_ref=src, dst_ref=dst, send_sem=send_sem.at[i], recv_sem=recv_sem.at[i],
            device_id=device(*to), device_id_type=MESH,
        )
        for i, (to, src, dst) in enumerate(messages)
    ]
    for copy in copies[:9]:
        copy.start()
    for load in loads[2:]:
        load.start()

    for c in range(3):
        tile = None
        for g, from_lane in ((0, 0), (1, 124)):
            for k in range(16):
                to = 64 * g + 4 * k
                x = roll(st[c, g, chunk(BASE + 8 * k), :], to - from_lane)
                tile = x if tile is None else jnp.where(lane >= to, x, tile)
        sides[c] = tile

    even = lax.rem(2 * lane, 128)
    own = (0, 1)
    speed_pass(st, vel, own, 10, 26)
    step_pass(st, vel, fine1, own, 11, 25)

    copies[0].wait_recv()
    for c in range(3):
        for k in range(4):
            x = up_low[chunk(32 * c + 8 * k), :]
            ahead[c, chunk(8 * k), :] = x
            ahead[c, chunk(32 + 8 * k), :] = roll(x, 64)
        for k in range(8):
            ahead[c, chunk(64 + 8 * k), :] = st[c, 1, chunk(BASE + 8 * k), :]
    for c in range(3):
        top = [
            jnp.where(
                row8 + 8 * k < rc,
                ahead[c, chunk(64 + 8 * k - rc), :],
                ahead[c, chunk(64 + 8 * k), :],
            )
            for k in range(8)
        ]
        for k in range(4):
            high_s[c, chunk(8 * k), :] = fold(top[k], top[k + 4])
    copies[10].start()
    copies[9].start()

    def coarse_own(i):
        n = 8 if i else 4
        for c in range(3):
            row = BASE - 2 * n + 16 * i
            halves = [pick(block_means(st, row, g, c, n), even[:n]) for g in range(2)]
            cgrid[c, 0, pl.ds(8 * i + 8 - n, n), :] = jnp.where(lane[:n] < 64, *halves)
        speed_pass(cgrid, cvel, (0,), i, i + 1)

    def estimate(i):
        total = None
        for c in range(3):
            halves = [pick(block_means(fine2, BASE + 16 * i, g, c), even) for g in range(2)]
            gap = jnp.abs(jnp.where(lane < 64, *halves) - cone[c, 0, chunk(8 * i + 8), :])
            total = gap if total is None else total + gap
        err[chunk(8 * i), :] = 10.0 * total

    speed_pass(fine1, vel, own, 11, 25)
    step_pass(fine1, vel, fine2, own, 12, 24)
    for i in range(1, 9):
        coarse_own(i)
    step_pass(cgrid, cvel, cone, (0,), 2, 8)
    for i in range(1, 7):
        estimate(i)

    for copy in copies[1:8]:
        copy.wait_recv()
    for load in loads[2:]:
        load.wait()
    for c in range(3):
        for g in range(2):
            st[c, g, pl.ds(BASE - 2, 2), :] = up_low[pl.ds(112 + 4 * c + 2 * g, 2), :]
            st[c, g, pl.ds(BASE + 128, 2), :] = dn[pl.ds(4 * c + 2 * g, 2), :]
    speed_pass(st, rim, own, 9, 12)
    speed_pass(st, rim, own, 24, 27)
    step_pass(st, rim, fine1, own, 9, 11)
    step_pass(st, rim, fine1, own, 25, 27)
    speed_pass(fine1, rim, own, 9, 13)
    speed_pass(fine1, rim, own, 23, 27)
    step_pass(fine1, rim, fine2, own, 10, 12)
    step_pass(fine1, rim, fine2, own, 24, 26)
    coarse_own(0)
    coarse_own(9)
    step_pass(cgrid, cvel, cone, (0,), 1, 2)
    step_pass(cgrid, cvel, cone, (0,), 8, 9)
    estimate(0)
    estimate(7)

    left, right, corner, lower_right = l_low[chunk(104), :], rl[...], url[...], dr[...]
    part, place = lax.shift_right_logical(lane, 4), lax.bitwise_and(lane, 15)

    def folded(a, b, c, d):
        return jnp.where(place < 2, a, jnp.where(place < 8, b, jnp.where(place < 12, c, d)))

    for j in range(4):
        block = 2 * part + (j - 1)
        own_at = lax.bitwise_and(4 * block + jnp.where(place < 8, place - 2, place + 56), 127)
        for c in range(3):
            at = lax.bitwise_and(32 * c + 2 * block + lax.bitwise_and(place, 1), 127)
            own_cells = pick(sides[c], own_at)
            x = folded(pick(left, at), own_cells, own_cells, pick(right, at))
            if j == 0:
                rows = chunk(BASE - 8)
                above = folded(
                    roll(ul[chunk(4 + 4 * c), :], 2), roll(st[c, 0, rows, :], 2),
                    roll(st[c, 1, rows, :], 12), roll(corner, -18 - 32 * c),
                )
                x = jnp.where(part == 0, above, x)
            if j == 3:
                rows = chunk(BASE + 128)
                below = folded(
                    roll(dl[chunk(2 + 4 * c), :], -14), roll(st[c, 0, rows, :], 114),
                    roll(st[c, 1, rows, :], -4), roll(lower_right, 124 - 32 * c),
                )
                x = jnp.where(part == 7, below, x)
            strip[c, 0, chunk(8 + 8 * j), :] = x
    one = (0,)
    speed_pass(strip, svel, one, 1, 5)
    step_pass(strip, svel, strip1, one, 1, 5)
    speed_pass(strip1, svel1, one, 1, 5)
    step_pass(strip1, svel1, strip2, one, 2, 4)
    for i in range(3):
        for c in range(3):
            sgrid[c, 0, chunk(8 * i), :] = block_means(strip, 16 * i, 0, c)
    speed_pass(sgrid, sgvel, one, 0, 3)
    step_pass(sgrid, sgvel, sone, one, 1, 2, 2)
    total = None
    for c in range(3):
        gap = jnp.abs(block_means(strip2, 16, 0, c) - sone[c, 0, chunk(8), :])
        total = gap if total is None else total + gap
    total = 10.0 * total
    for i in range(8):
        at = chunk(8 * i)
        value = jnp.where(lane == 127, roll(total, 117 - 16 * i), err[at, :])
        err[at, :] = jnp.where(lane == 0, roll(total, -(16 * i + 2)), value)

    for c in range(3):
        for k in range(-8, 17):
            col = 32 * c + 2 * k
            if k < 0:
                x = roll(corner, -(col + 32))
            else:
                x = roll(lower_right, -32 * c) if k == 16 else roll(right, -col)
            st[c, 2, chunk(BASE + 8 * k), :] = x

    for copy in copies[8:10]:
        copy.wait_recv()
    for c in range(3):
        for g in range(2):
            for k in range(8):
                here = st[c, g, chunk(BASE + 8 * k), :]
                above = st[c, g, chunk(64 + 8 * k - rc), :]
                rm[c, g, chunk(8 * k), :] = jnp.where(row8 + 8 * k < rc, above, here)
    given = (rl[:1], up_low[pl.ds(96, 1)], dn[pl.ds(12, 1)], url[:1], dl[pl.ds(12, 1)], dr[:1], lpack[:1])
    for i, x in enumerate(given):
        cnt[pl.ds(i, 1), :] = x
    keep = pltpu.make_async_copy(cnt, counts, local_sem.at[0])
    keep.start()
    copies[10].wait_recv()
    for copy in copies:
        copy.wait_send()
    keep.wait()


def patch_kernel(
    cnt, pos, ext, st, rm, l_low, l_high, ul, dl, err_in,
    err, moved_out, refined,
    tiles, win, wvel, ctr, dcol, plus, base, mid, low, moved, sem,
):
    lane = lanes()
    row8 = lax.broadcasted_iota(jnp.int32, (8, 128), 0)
    writes = [
        pltpu.make_async_copy(err_in, err, sem.at[0]),
        pltpu.make_async_copy(moved, moved_out, sem.at[1]),
    ]
    writes[0].start()
    rc_of = lambda i: cnt[i, 96].astype(jnp.int32)
    cc_of = lambda i: cnt[i, 97].astype(jnp.int32)
    rows_below = (rc_of(4), rc_of(2), rc_of(2), rc_of(5))
    cols_in = {"up": (cc_of(1), cc_of(3)), "own": (cc_of(6), cc_of(0)), "down": (cc_of(2), cc_of(5))}

    rc_right = rc_of(0)
    for c in range(3):
        for k in range(4):
            for start, x in ((0, l_high[c, chunk(8 * k), :]), (64, l_low[chunk(32 * c + 8 * k), :])):
                tiles[0, c, chunk(8 + start + 8 * k), :] = x
                tiles[0, c, chunk(40 + start + 8 * k), :] = roll(x, 64)
        tiles[0, c, chunk(0), :] = ul[chunk(4 + 4 * c), :]

    for c in range(3):
        for k in range(-1, 17):
            at = chunk(BASE + 8 * k)
            if k < 0:
                values = [ul[chunk(4 + 4 * c), :], st[c, 0, at, :], st[c, 1, at, :], st[c, 2, at, :]]
            elif k < 16:
                own = [rm[c, g, chunk(8 * k), :] if k < 8 else st[c, g, at, :] for g in range(2)]
                beside = st[c, 2, at, :]
                if k < 8:
                    above = st[c, 2, chunk(BASE + 8 * k - rc_right), :]
                    beside = jnp.where(row8 + 8 * k < rc_right, above, beside)
                values = [tiles[0, c, chunk(8 * k + 8), :], *own, beside]
            else:
                above = [
                    tiles[0, c, chunk(136 - rows_below[0]), :],
                    st[c, 0, chunk(BASE + 128 - rows_below[1]), :],
                    st[c, 1, chunk(BASE + 128 - rows_below[2]), :],
                    st[c, 2, chunk(BASE + 128 - rows_below[3]), :],
                ]
                below = [dl[chunk(2 + 4 * c), :], st[c, 0, at, :], st[c, 1, at, :], st[c, 2, at, :]]
                values = [jnp.where(row8 < rows_below[g], above[g], below[g]) for g in range(4)]
                tiles[0, c, chunk(136), :] = values[0]
            c0, c_right = cols_in["up" if k < 0 else "down" if k == 16 else "own"]
            m0 = jnp.where(lane < c0, roll(values[0], c0), values[1])
            m_right = jnp.where(lane < c_right, roll(values[2], c_right), values[3])
            put = chunk(8 * k + 8)
            for g, value in enumerate((m0, values[2], m_right)):
                tiles[g + 1, c, put, :] = value
            if 0 <= k < 16:
                moved[c, chunk(8 * k), pl.ds(0, 128)] = m0
                moved[c, chunk(8 * k), pl.ds(128, 128)] = values[2]

    writes[1].start()

    p0, p1 = pos[0, 0, 0], pos[0, 0, 1]
    group = lax.shift_right_logical(p1 + 126, 7)
    offset = lax.bitwise_and(p1 + 126, 127)
    back = lax.bitwise_and(128 - offset, 127)
    for k in range(10):
        u = []
        for c in range(3):
            at = chunk(p0 + 8 * k)
            a, b = tiles[group, c, at, :], tiles[group + 1, c, at, :]
            u.append(jnp.where(lane < 128 - offset, roll(a, back), roll(b, back)))
            win[c, chunk(8 * k + 8), :] = u[c]
        for c, value in enumerate(speeds(*u)):
            wvel[c, chunk(8 * k + 8), :] = value

    for k in range(10):
        row = 8 * k + 8

        def load(shift, normal):
            at = chunk(row + shift)
            return side([win[c, at, :] for c in range(3)], [wvel[c, at, :] for c in range(3)], normal)

        here = load(0, 1)
        down, up = face(load(-1, 1), here), face(here, load(1, 1))
        across = load(0, 2)
        lower = [roll(x, 1) for x in across[0]]
        left = face(side(lower, speeds(*lower), 2), across)
        right = [roll(x, 127) for x in left]
        for a in range(2):
            near = [[] for _ in range(4)]
            for c in range(3):
                twice = 2.0 * here[1][c]
                tall = up[c] - twice if a else twice - down[c]
                half_way = here[0][c] - HALF * tall
                twice = 2.0 * across[1][c]
                e = half_way - HALF * (twice - left[c])
                o = half_way - HALF * (right[c] - twice)
                ctr[2 * a, c, chunk(row), :] = e
                ctr[2 * a + 1, c, chunk(row), :] = o
                if 1 <= k < 9:
                    inner, outer = o - e, e - roll(o, 1)
                    s_e, s_o = 0.5 * minmod(outer, inner), 0.5 * minmod(inner, roll(outer, 127))
                    for i, x in enumerate((roll(o + s_o, 1), e - s_e, e + s_e, o - s_o)):
                        near[i].append(x)
            if 1 <= k < 9:
                sides = [side(u, speeds(*u), 2) for u in near]
                f_out, f_in = face(sides[0], sides[1]), face(sides[2], sides[3])
                for c in range(3):
                    dcol[2 * a, c, chunk(row), :] = f_in[c] - f_out[c]
                    dcol[2 * a + 1, c, chunk(row), :] = roll(f_out[c], 127) - f_in[c]

    for k in range(10):
        row = 8 * k + 8
        at = chunk(row)
        for b in range(2):
            l_side, r_side = [], []
            for c in range(3):
                c0, c1 = ctr[b, c, at, :], ctr[2 + b, c, at, :]
                inner = c1 - c0
                before = c0 - ctr[2 + b, c, chunk(row - 1), :]
                after = ctr[b, c, chunk(row + 1), :] - c1
                s0, s1 = 0.5 * minmod(before, inner), 0.5 * minmod(inner, after)
                base[b, c, at, :] = c0 - s0
                plus[b, c, at, :] = c1 + s1
                l_side.append(c0 + s0)
                r_side.append(c1 - s1)
            if 1 <= k < 9:
                f = face(side(l_side, speeds(*l_side), 1), side(r_side, speeds(*r_side), 1))
                for c in range(3):
                    mid[b, c, at, :] = f[c]
    for k in range(1, 10):
        row = 8 * k + 8
        for b in range(2):
            l_side = [plus[b, c, chunk(row - 1), :] for c in range(3)]
            r_side = [base[b, c, chunk(row), :] for c in range(3)]
            f = face(side(l_side, speeds(*l_side), 1), side(r_side, speeds(*r_side), 1))
            for c in range(3):
                low[b, c, chunk(row), :] = f[c]
    source = lax.shift_right_logical(lane, 1)
    odd = lax.bitwise_and(lane, 1) == 1
    inside_col = source < ext[0, 0, 1]
    for k in range(1, 9):
        row = 8 * k + 8
        at = chunk(row)
        inside = inside_col & (row8 + 8 * (k - 1) < ext[0, 0, 0])
        for c in range(3):
            done = [[], []]
            for b in range(2):
                f_mid, f_low, f_next = mid[b, c, at, :], low[b, c, at, :], low[b, c, chunk(row + 1), :]
                for a, tall in enumerate((f_mid - f_low, f_next - f_mid)):
                    x = ctr[2 * a + b, c, at, :] - HALF * (tall + dcol[2 * a + b, c, at, :])
                    done[a].append(
                        pick(x, source + 2)
                    )
            for a in range(2):
                x = jnp.where(odd, done[a][1], done[a][0])
                refined[c, pl.ds(16 * (k - 1) + a, 8, stride=2), :] = jnp.where(inside, x, 0.0)
    for write in writes:
        write.wait()


def solution(mesh):
    n_row, n_col = mesh.shape["row"], mesh.shape["col"]
    vmem = pl.BlockSpec(memory_space=pltpu.VMEM)
    smem = pl.BlockSpec(memory_space=pltpu.SMEM)
    hbm = pl.BlockSpec(memory_space=pltpu.HBM)
    buf = lambda *shape: pltpu.VMEM(shape, F32)

    def per_device(state, row_count, col_count, patch_pos, patch_ext):
        in_hbm = [
            x if x.ndim == 2 else pltpu.with_memory_space_constraint(x, pltpu.HBM)
            for x in (state, row_count, col_count, patch_pos, patch_ext)
        ]
        corner = buf(3, 8, 128)
        half = buf(3, 32, 128)
        *parts, cnt, pos, ext, err = pl.pallas_call(
            functools.partial(exchange_kernel, n_row, n_col),
            out_shape=(
                buf(3, 3, ROWS, 128), buf(3, 2, 64, 128), buf(112, 128), half, buf(32, 128), buf(24, 128),
                pltpu.SMEM((8, 128), F32),
                pltpu.SMEM((1, 1, 2), jnp.int32),
                pltpu.SMEM((1, 1, 2), jnp.int32),
                buf(64, 128),
            ),
            in_specs=[hbm, smem, smem, hbm, hbm],
            out_specs=(vmem,) * 6 + (smem,) * 3 + (vmem,),
            scratch_shapes=[
                buf(8, 128), buf(128, 128), half, buf(16, 128), *([buf(8, 128)] * 4), buf(16, 128),
                buf(128, 128), buf(3, 128, 128), corner,
                *([buf(3, 2, ROWS, 128)] * 4), *([buf(3, 1, 88, 128)] * 3),
                *([buf(3, 1, 48, 128)] * 8),
                pltpu.SemaphoreType.DMA((4,)),
                pltpu.SemaphoreType.DMA((N_MSG,)),
                pltpu.SemaphoreType.DMA((N_MSG,)),
            ],
            compiler_params=pltpu.CompilerParams(
                collective_id=0, has_side_effects=True, vmem_limit_bytes=24 << 20
            ),
        )(*in_hbm)
        return pl.pallas_call(
            patch_kernel,
            out_shape=(
                jax.ShapeDtypeStruct((64, 128), F32),
                jax.ShapeDtypeStruct((3, 128, 256), F32),
                jax.ShapeDtypeStruct((3, 128, 128), F32),
            ),
            in_specs=[smem] * 3 + [vmem] * 7,
            out_specs=(hbm, hbm, vmem),
            scratch_shapes=[
                buf(4, 3, 144, 128), buf(3, 96, 128), buf(3, 96, 128),
                buf(4, 3, 96, 128), buf(4, 3, 96, 128), *([buf(2, 3, 96, 128)] * 4),
                buf(3, 128, 256), pltpu.SemaphoreType.DMA((2,)),
            ],
            compiler_params=pltpu.CompilerParams(vmem_limit_bytes=24 << 20),
        )(cnt, pos, ext, *parts, err)

    return jax.shard_map(
        per_device,
        mesh=mesh,
        in_specs=(
            P(None, "row", "col"),
            P("row", "col"),
            P("row", "col"),
            P("row", "col", None),
            P("row", "col", None),
        ),
        out_specs=(P("row", "col"), P(None, "row", "col"), P(None, "row", "col")),
        check_vma=False,
    )
```
